32 devices in a mesh: section: 8 (over y, x, core), expert: 4 (over z).
Axes of the slice: x: 2, y: 2, z: 4, core: 2. Of those that a mesh axis runs over, the one named last changes fastest.
Arguments:
- acts: bfloat16 [8, 128, 2560], P('section', 'expert'), may hold values from -6 to 6
- incoming: bfloat16 [1, 128, 2560], P(None, 'expert'), may hold values from -6 to 6
- routes: int32 [2, 8, 128, 2], P(None, 'section', 'expert'), may hold values from 0 to 3, all different within a row; in each aligned block of 32 rows (0 to 31, 32 to 63, ..., all dimensions but the last counted through in order) at most 24 rows name the same one
- route_weight: float32 [2, 8, 128, 2], P(None, 'section', 'expert'), may hold values from 0.25 to 1
- norm_gain: float32 [8, 2560], P('section'), may hold values from 0.25 to 1.75
- w_gate: bfloat16 [8, 2560, 3072], P('section', None, 'expert'), may hold values from -0.125 to 0.125
- w_up: bfloat16 [8, 2560, 3072], P('section', None, 'expert'), may hold values from -0.125 to 0.125
- w_down: bfloat16 [8, 3072, 2560], P('section', 'expert'), may hold values from -0.21875 to 0.21875
Outputs:
- section_outputs: bfloat16 [2, 8, 128, 2560], P(None, 'section', 'expert')
The draws below stay inside these ranges and needn't reach their ends.
Inputs may be any that keep to these rules, and one draw needn't show every extreme that they name: `routes`: a token's 2 experts are distinct; in each aligned block of 32 tokens (the tokens of one device) no expert is chosen more than 24 times, and that count is reached.
All inputs are finite; a program needn't handle non-finite values.
Results may differ from the reference program's by a relative error of at most 0.009.
Values may be sent and summed in bfloat16 or wider, within the bound.
A program may use at most 64 MiB of HBM per device.

```python
import math
import jax
import jax.numpy as jnp
import numpy as np
from jax import lax

D = 2560
FF = 768
EXPERTS = 4
TOP = 2
TICKS = 2
TOK_DEV = 32
CAP = 24
GROUP = 128
N_SECTION = 8
N_EXPERT = 4


def block_scale(rng, extent, pieces, low, largest):
    factor_of, own = 1.0, jax.random.fold_in(rng, 6)
    for position, shards_of in pieces:
        draws = jnp.exp(jax.random.uniform(jax.random.fold_in(own, position), (shards_of,), jnp.float32, low / len(pieces), largest / len(pieces)))
        factor_of = factor_of * jnp.repeat(draws, extent[position] // shards_of).reshape([-1 if axis == position else 1 for axis in range(len(extent))])
    return factor_of


def routed_block(own_key, own, number, rows, amount, top, most, skew):
    order = jax.random.permutation(own_key, amount)
    packed, common = portions_of(amount, rows * top, most, skew, True), portions_of(amount, rows * top, most, skew, False)
    places = jnp.arange(amount)

    def named(lengths, offset_by):
        used = int((lengths > 0).sum())
        fixed = max(1, used // 4)
        shifted = fixed + (places - fixed + offset_by * (used - fixed)) % max(1, amount - fixed)
        return jnp.zeros((amount,), jnp.int32).at[order[jnp.where(places < fixed, places, shifted)]].set(jnp.asarray(lengths, jnp.int32))

    lengths = jnp.where(number % 4 == 0, named(packed, number // 4), named(common, number - number // 4 - 1))
    mixed = jax.random.permutation(jax.random.fold_in(own, 3), amount)
    giver, receiver = mixed[0:amount // 2 * 2:2], mixed[1:amount // 2 * 2:2]
    margin = jnp.minimum(lengths[giver] - 1, most - lengths[receiver]) // 2
    margin = jnp.where((giver == order[0]) | (receiver == order[0]) | (lengths[receiver] == 0), 0, jnp.maximum(margin, 0))
    shifted = jax.random.randint(jax.random.fold_in(own, 4), (amount // 2,), 0, 1 << 20) % (margin + 1)
    lengths = lengths.at[giver].add(-shifted).at[receiver].add(shifted)
    items = jnp.searchsorted(jnp.cumsum(lengths), jnp.arange(rows * top), side="right").astype(jnp.int32)
    grid = items.reshape(top, rows).T
    grid = grid[jax.random.permutation(jax.random.fold_in(own, 1), rows)]
    offset_by = jax.random.randint(jax.random.fold_in(own, 2), (rows, 1), 0, top)
    return jnp.take_along_axis(grid, (jnp.arange(top)[None, :] + offset_by) % top, axis=1)


def portions_of(number_of, total, most, slope, full):
    portions = [(1 << 20) // math.isqrt(rank ** slope) + 1 for rank in range(1, number_of + 1)]
    largest = most if full else min(most, max(-(-total // number_of), total * portions[0] // sum(portions)))
    least = 1 if total - largest >= number_of - 1 else 0
    given, spare = [largest] + [least] * (number_of - 1), total - largest - least * (number_of - 1)
    while spare > 0:
        candidates = [i for i in range(1, number_of) if given[i] < largest] or [i for i in range(1, number_of) if given[i] < most]
        pool, budget = sum([portions[i] for i in candidates]), spare
        for i in candidates:
            addition = min(most - given[i], max(1, budget * portions[i] // pool), spare)
            given[i] = given[i] + addition
            spare = spare - addition
    return np.array(given)


def noise(own_key, shape, spread, limit, pieces=(), kind=jnp.bfloat16):
    drawn = spread * jax.random.normal(own_key, shape, jnp.float32)
    if pieces:
        drawn = drawn * block_scale(own_key, shape, pieces, -0.22, 0.18)
    return jnp.clip(drawn, -limit, limit).astype(kind)


def setup_inputs(seed: int = 0) -> dict:
    keys = jax.random.split(jax.random.key(seed), 9)
    acts = noise(keys[0], (N_SECTION, GROUP, D), 1.0, 6.0, ((0, 8), (1, 4)))
    incoming = noise(keys[1], (TICKS - 1, GROUP, D), 1.0, 6.0, ((1, 4),))
    routes_keys = jax.random.split(jax.random.fold_in(keys[2], 1), TICKS * N_SECTION * GROUP // TOK_DEV)
    routes_turns = jax.random.permutation(jax.random.fold_in(keys[2], 3), TICKS * N_SECTION * GROUP // TOK_DEV)
    routes = jax.vmap(lambda own, number: routed_block(jax.random.fold_in(keys[2], 2), own, number, TOK_DEV, EXPERTS, TOP, CAP, 2))(routes_keys, routes_turns).reshape((TICKS, N_SECTION, GROUP, TOP))
    route_weight = jnp.clip(0.25 + 0.75 * jax.random.uniform(keys[3], (TICKS, N_SECTION, GROUP, TOP), jnp.float32) ** block_scale(keys[3], (TICKS, N_SECTION, GROUP, TOP), ((1, 8), (2, 4)), -0.2, 0.2), 0.25, 1.0)
    norm_gain = jnp.clip(1.0 + 0.15 * jax.random.normal(keys[4], (N_SECTION, D), jnp.float32), 0.25, 1.75)
    w_gate = noise(keys[5], (N_SECTION, D, EXPERTS * FF), D ** -0.5, 0.125, ((0, 8), (2, 4)))
    w_up = noise(keys[6], (N_SECTION, D, EXPERTS * FF), D ** -0.5, 0.125, ((0, 8), (2, 4)))
    w_down = noise(keys[7], (N_SECTION, EXPERTS * FF, D), FF ** -0.5, 0.21875, ((0, 8), (1, 4)))
    return {"acts": acts, "incoming": incoming, "routes": routes, "route_weight": route_weight, "norm_gain": norm_gain, "w_gate": w_gate, "w_up": w_up, "w_down": w_down}


def section_layer(tokens_in, chosen, chosen_weight, gain, w_gate, w_up, w_down):
    blocks = N_EXPERT
    group = N_EXPERT // EXPERTS
    width = EXPERTS * FF // N_EXPERT
    tok_f = tokens_in.astype(jnp.float32)
    normed = (tok_f * lax.rsqrt(lax.optimization_barrier(jnp.mean(tok_f * tok_f, axis=-1, keepdims=True)) + 1e-06) * gain).astype(jnp.bfloat16)
    gate_val = jnp.dot(normed, w_gate, preferred_element_type=jnp.float32)
    up_val = jnp.dot(normed, w_up, preferred_element_type=jnp.float32)
    hidden = (jax.nn.silu(gate_val) * up_val).astype(jnp.bfloat16)
    hidden_b = hidden.reshape(hidden.shape[0], blocks, width).astype(jnp.float32)
    down_b = w_down.reshape(blocks, width, w_down.shape[1]).astype(jnp.float32)
    partial_value = jnp.einsum('tbh,bhd->btd', hidden_b, down_b, precision=lax.Precision.HIGHEST).astype(jnp.bfloat16)
    summed = partial_value.astype(jnp.float32).reshape(EXPERTS, group, hidden.shape[0], w_down.shape[1]).sum(axis=1)
    expert_hot = (chosen[:, :, None] == jnp.arange(EXPERTS, dtype=jnp.int32)[None, None, :]).astype(jnp.float32)
    mixing = lax.optimization_barrier(jnp.sum(chosen_weight[:, :, None] * expert_hot, axis=1))
    routed = jnp.einsum('te,etd->td', mixing, summed, precision=lax.Precision.HIGHEST)
    return (tok_f + routed).astype(jnp.bfloat16)

def reference(acts, incoming, routes, route_weight, norm_gain, w_gate, w_up, w_down):
    state = acts
    results = []
    for tick in range(TICKS):
        layer_out = lax.map(lambda items: section_layer(*items), (state, routes[tick], route_weight[tick], norm_gain, w_gate, w_up, w_down))
        results.append(layer_out)
        if tick + 1 < TICKS:
            state = jnp.concatenate([incoming[tick][None], layer_out[:-1]], axis=0)
    return jnp.stack(results)
```

```python
import functools

import jax
import jax.numpy as jnp
from jax import lax
from jax.experimental import pallas as pl
from jax.experimental.pallas import tpu as pltpu
from jax.sharding import PartitionSpec as P

MESH = pl.DeviceIdType.MESH
EXPERTS = 4
CAP = 24


def kernel(
    n,
    sections,
    acts,
    incoming,
    routes,
    route_weight,
    gain,
    w_gate_hbm,
    w_up_hbm,
    w_down_hbm,
    out,
    w_gate,
    w_up,
    w_down,
    xown,
    moved,
    xsend,
    xrecv,
    psend,
    precv,
    sel_out,
    sel_in,
    pick,
    w_sem,
    own_sem,
    sel_send,
    sel_recv,
    raw_send,
    raw_recv,
    x_send,
    x_recv,
    p_send,
    p_recv,
):
    s = lax.axis_index("section")
    e = lax.axis_index("expert")
    ticks, chunks, tokens, cols = xown.shape
    top = routes.shape[2]
    cap = xsend.shape[3]
    group = n // EXPERTS
    width = chunks * cols
    rows = n * cap
    has_next = s < sections - 1
    has_prev = s > 0
    following = jnp.minimum(s + 1, sections - 1)
    previous = jnp.maximum(s - 1, 0)
    half = jnp.bfloat16
    single = jnp.float32

    def others(body):
        def step(i, _):
            k = n - 1 - i
            for d, there in ((e + k, e + k < n), (e - k, e - k >= 0)):

                @pl.when(there)
                def _():
                    body(jnp.clip(d, 0, n - 1))

            return 0

        lax.fori_loop(0, n - 1, step, 0)

    def own_copy(t, c):
        source = acts if t == 0 else incoming.at[t - 1]
        return pltpu.make_async_copy(
            source.at[:, pl.ds(c * cols, cols)], xown.at[t, c], own_sem.at[t, c]
        )

    def gate_copy(c):
        span = pl.ds(c * cols, cols)
        return (
            pltpu.make_async_copy(w_gate_hbm.at[span], w_gate.at[span], w_sem.at[0, c]),
            pltpu.make_async_copy(w_up_hbm.at[span], w_up.at[span], w_sem.at[1, c]),
        )

    down_copy = pltpu.make_async_copy(w_down_hbm, w_down, w_sem.at[2, 0])

    def sel_copy(t):
        return pltpu.make_async_remote_copy(
            sel_out.at[t],
            sel_in.at[t],
            sel_send.at[t],
            sel_recv.at[t],
            device_id=(previous, e),
            device_id_type=MESH,
        )

    def raw_copy(t, c):
        return pltpu.make_async_remote_copy(
            moved.at[t, c],
            xown.at[t + 1, c],
            raw_send.at[t, c],
            raw_recv.at[t, c],
            device_id=(following, e),
            device_id_type=MESH,
        )

    def x_copy(slot, t, c, section, d):
        return pltpu.make_async_remote_copy(
            xsend.at[slot, c, d // group],
            xrecv.at[t, c, e],
            x_send.at[slot, c, d],
            x_recv.at[t, c, e],
            device_id=(section, d),
            device_id_type=MESH,
        )

    def x_arrival(t, c, d):
        return pltpu.make_async_remote_copy(
            xrecv.at[t, c, d],
            xrecv.at[t, c, d],
            x_send.at[0, c, d],
            x_recv.at[t, c, d],
            device_id=(s, d),
            device_id_type=MESH,
        )

    def p_copy(t, c, d):
        return pltpu.make_async_remote_copy(
            psend.at[t, c, d],
            precv.at[t, c, e],
            p_send.at[t, c, d],
            p_recv.at[t, c, e],
            device_id=(s, d),
            device_id_type=MESH,
        )

    def p_arrival(t, c, d):
        return pltpu.make_async_remote_copy(
            precv.at[t, c, d],
            precv.at[t, c, d],
            p_send.at[t, c, d],
            p_recv.at[t, c, d],
            device_id=(s, d),
            device_id_type=MESH,
        )

    for c in range(chunks):
        own_copy(0, c).start()

    barrier = pltpu.get_barrier_semaphore()

    def greet(d, _):
        @pl.when(d != e)
        def _():
            pl.semaphore_signal(barrier, inc=1, device_id=(s, d), device_id_type=MESH)

        @pl.when(has_next)
        def _():
            pl.semaphore_signal(barrier, inc=1, device_id=(following, d), device_id_type=MESH)

        @pl.when(has_prev)
        def _():
            pl.semaphore_signal(barrier, inc=1, device_id=(previous, d), device_id_type=MESH)

        return 0

    lax.fori_loop(0, n, greet, 0)

    for c in range(chunks):
        for copy in gate_copy(c):
            copy.start()
    down_copy.start()

    @pl.when(jnp.logical_not(has_prev))
    def _():
        for t in range(1, ticks):
            for c in range(chunks):
                own_copy(t, c).start()

    def iota(shape, axis):
        return lax.broadcasted_iota(jnp.int32, shape, axis)

    before = (iota((tokens, tokens), 0) < iota((tokens, tokens), 1)).astype(half)
    diagonal = iota((tokens, tokens), 0) == iota((tokens, tokens), 1)
    sel_first = None
    for t in range(ticks):
        chosen = routes[t, 0]
        hot = sum(
            (iota((EXPERTS, tokens), 0) == chosen[k : k + 1]).astype(single) for k in range(top)
        )
        rank = jnp.dot(hot.astype(half), before, preferred_element_type=single)
        place = iota((cap, tokens), 0).astype(single)
        whole = None
        for k in range(top):
            blocks = []
            for x in range(EXPERTS):
                slot = jnp.where(chosen[k : k + 1] == x, rank[x : x + 1], -1.0)
                blocks.append((place == slot).astype(single))
            spread = jnp.concatenate([b for b in blocks for _ in range(group)], axis=0)
            pick[t, k * tokens : (k + 1) * tokens, :] = lax.dot_general(
                diagonal.astype(half),
                spread.astype(half),
                (((1,), (1,)), ((), ())),
                preferred_element_type=single,
            ).astype(half)
            mine = jnp.concatenate(blocks, axis=0)
            whole = mine if whole is None else whole + mine
        if t == 0:
            sel_first = whole.astype(half)
        else:
            sel_out[t - 1] = whole.astype(half)

    pl.semaphore_wait(
        barrier, n - 1 + jnp.where(has_next, n, 0) + jnp.where(has_prev, n, 0)
    )

    def pack(slot, c, sel, value):
        packed = jnp.dot(sel, value, preferred_element_type=single)
        for x in range(EXPERTS):
            xsend[slot, c, x] = packed[x * cap : (x + 1) * cap].astype(half)

    def keep(slot, t, c):
        xrecv[t, c, e] = xsend[slot, c, e // group]

    for c in range(chunks):
        own_copy(0, c).wait()
        pack(0, c, sel_first, xown[0, c])
        others(lambda d: x_copy(0, 0, c, s, d).start())
        keep(0, 0, c)

    @pl.when(has_prev)
    def _():
        for t in range(ticks - 1):
            sel_copy(t).start()

    def stack(ref, t, c):
        return jnp.concatenate([ref[t, c, d].astype(single) for d in range(n)], axis=0)

    for t in range(ticks):
        gate_val = up_val = None
        squares = jnp.zeros((rows, 1), single)
        for c in range(chunks):
            if t == 0:
                others(lambda d: x_arrival(t, c, d).wait_recv())
                for copy in gate_copy(c):
                    copy.wait()
            else:

                def arrive(d, _):
                    @pl.when(jnp.logical_or(has_prev, d != e))
                    def _():
                        x_arrival(t, c, d).wait_recv()

                    return 0

                lax.fori_loop(0, n, arrive, 0)
            span = pl.ds(c * cols, cols)
            value = stack(xrecv, t, c)
            squares = squares + jnp.sum(value * value, axis=1, keepdims=True)
            normed = (value * gain[:, span]).astype(half)
            gate_part = jnp.dot(normed, w_gate[span, :], preferred_element_type=single)
            up_part = jnp.dot(normed, w_up[span, :], preferred_element_type=single)
            gate_val = gate_part if gate_val is None else gate_val + gate_part
            up_val = up_part if up_val is None else up_val + up_part
        scale = lax.rsqrt(squares * (1.0 / width) + 1e-06)
        hidden = (jax.nn.silu(gate_val * scale) * (up_val * scale)).astype(half)
        if t == 0:
            down_copy.wait()
        for c in range(chunks):
            span = pl.ds(c * cols, cols)
            value = jnp.dot(hidden, w_down[:, span], preferred_element_type=single)
            for d in range(n):
                psend[t, c, d] = value[d * cap : (d + 1) * cap].astype(half)
            others(lambda d: p_copy(t, c, d).start())
            precv[t, c, e] = psend[t, c, e]

        if t < ticks - 1:

            @pl.when(jnp.logical_not(has_prev))
            def _():
                for c in range(chunks):
                    own_copy(t + 1, c).wait()
                    pack(t + 1, c, sel_out[t], xown[t + 1, c])
                    others(lambda d: x_copy(t + 1, t + 1, c, s, d).start())
                    keep(t + 1, t + 1, c)

            @pl.when(has_next)
            def _():
                sel_copy(t).wait_recv()

        weights = [
            jnp.sum(
                jnp.where(diagonal, route_weight[t, 0][k : k + 1], 0.0), axis=1, keepdims=True
            )
            for k in range(top)
        ]
        for c in range(chunks):
            if t > 0:

                @pl.when(has_prev)
                def _():
                    raw_copy(t - 1, c).wait_recv()

            others(lambda d: p_arrival(t, c, d).wait_recv())
            back = jnp.dot(
                pick[t], stack(precv, t, c).astype(half), preferred_element_type=single
            )
            layer = xown[t, c].astype(single)
            for k in range(top):
                layer = layer + back[k * tokens : (k + 1) * tokens] * weights[k]
            layer = layer.astype(half)
            out[t, :, pl.ds(c * cols, cols)] = layer
            if t < ticks - 1:

                @pl.when(has_next)
                def _():
                    pack(ticks + t, c, sel_in[t], layer)

                    def forward(i, _):
                        x_copy(ticks + t, t + 1, c, following, i).start()
                        return 0

                    lax.fori_loop(0, n, forward, 0)
                    moved[t, c] = layer
                    raw_copy(t, c).start()

    def drain(d, _):
        for c in range(chunks):

            @pl.when(d != e)
            def _():
                x_copy(0, 0, c, s, d).wait_send()
                for t in range(ticks):
                    p_copy(t, c, d).wait_send()

            @pl.when(jnp.logical_and(d != e, jnp.logical_not(has_prev)))
            def _():
                for t in range(1, ticks):
                    x_copy(t, t, c, s, d).wait_send()

            @pl.when(has_next)
            def _():
                for t in range(ticks - 1):
                    x_copy(ticks + t, t + 1, c, following, d).wait_send()

        return 0

    lax.fori_loop(0, n, drain, 0)

    for t in range(ticks - 1):

        @pl.when(has_next)
        def _():
            for c in range(chunks):
                raw_copy(t, c).wait_send()

        @pl.when(has_prev)
        def _():
            sel_copy(t).wait_send()


def solution(mesh):
    n = mesh.shape["expert"]
    sections = mesh.shape["section"]

    def shards(acts, incoming, routes, route_weight, norm_gain, w_gate, w_up, w_down):
        ticks, _, tokens, _ = routes.shape
        width, hidden = w_gate.shape[1:]
        chunks = 5 if width % (5 * 128) == 0 else 4
        cols = width // chunks
        cap = min(CAP, tokens)
        half = jnp.bfloat16
        anywhere = pl.BlockSpec(memory_space=pl.ANY)
        vmem = pl.BlockSpec(memory_space=pltpu.VMEM)
        dma = pltpu.SemaphoreType.DMA
        moves = max(ticks - 1, 1)
        result = pl.pallas_call(
            functools.partial(kernel, n, sections),
            out_shape=jax.ShapeDtypeStruct((ticks, tokens, width), half),
            in_specs=[anywhere, anywhere, vmem, vmem, vmem, anywhere, anywhere, anywhere],
            out_specs=vmem,
            scratch_shapes=[
                pltpu.VMEM((width, hidden), half),
                pltpu.VMEM((width, hidden), half),
                pltpu.VMEM((hidden, width), half),
                pltpu.VMEM((ticks, chunks, tokens, cols), half),
                pltpu.VMEM((moves, chunks, tokens, cols), half),
                pltpu.VMEM((2 * ticks - 1, chunks, EXPERTS, cap, cols), half),
                pltpu.VMEM((ticks, chunks, n, cap, cols), half),
                pltpu.VMEM((ticks, chunks, n, cap, cols), half),
                pltpu.VMEM((ticks, chunks, n, cap, cols), half),
                pltpu.VMEM((moves, EXPERTS * cap, tokens), half),
                pltpu.VMEM((moves, EXPERTS * cap, tokens), half),
                pltpu.VMEM((ticks, routes.shape[3] * tokens, n * cap), half),
                dma((3, chunks)),
                dma((ticks, chunks)),
                dma((moves,)),
                dma((moves,)),
                dma((moves, chunks)),
                dma((moves, chunks)),
                dma((2 * ticks - 1, chunks, n)),
                dma((ticks, chunks, n)),
                dma((ticks, chunks, n)),
                dma((ticks, chunks, n)),
            ],
            compiler_params=pltpu.CompilerParams(
                collective_id=0, has_side_effects=True, vmem_limit_bytes=56 << 20
            ),
        )(
            acts[0],
            incoming,
            jnp.swapaxes(routes, 2, 3),
            jnp.swapaxes(route_weight, 2, 3),
            norm_gain,
            w_gate[0],
            w_up[0],
            w_down[0],
        )
        return result[:, None]

    return jax.shard_map(
        shards,
        mesh=mesh,
        in_specs=(
            P("section", "expert", None),
            P(None, "expert", None),
            P(None, "section", "expert", None),
            P(None, "section", "expert", None),
            P("section", None),
            P("section", None, "expert"),
            P("section", None, "expert"),
            P("section", "expert", None),
        ),
        out_specs=P(None, "section", "expert", None),
        check_vma=False,
    )
```

```python
import functools

import jax
import jax.numpy as jnp
from jax import lax
from jax.experimental import pallas as pl
from jax.experimental.pallas import tpu as pltpu
from jax.sharding import PartitionSpec as P

MESH = pl.DeviceIdType.MESH
EXPERTS = 4
CAP = 24


def kernel(
    n,
    sections,
    acts,
    incoming,
    routes,
    route_weight,
    gain,
    w_gate_hbm,
    w_up_hbm,
    w_down_hbm,
    out,
    w_gate,
    w_up,
    w_down,
    xown,
    moved,
    xsend,
    xrecv,
    psend,
    precv,
    sel_out,
    sel_in,
    pick,
    w_sem,
    own_sem,
    sel_send,
    sel_recv,
    raw_send,
    raw_recv,
    x_send,
    x_recv,
    p_send,
    p_recv,
    turn,
):
    s = lax.axis_index("section")
    e = lax.axis_index("expert")
    ticks, chunks, tokens, cols = xown.shape
    top = routes.shape[2]
    cap = xsend.shape[3]
    group = n // EXPERTS
    width = chunks * cols
    rows = n * cap
    has_next = s < sections - 1
    has_prev = s > 0
    following = jnp.minimum(s + 1, sections - 1)
    previous = jnp.maximum(s - 1, 0)
    half = jnp.bfloat16
    single = jnp.float32

    def others(body):
        def step(i, _):
            k = n - 1 - i
            for d, there in ((e + k, e + k < n), (e - k, e - k >= 0)):

                @pl.when(there)
                def _():
                    body(jnp.clip(d, 0, n - 1))

            return 0

        lax.fori_loop(0, n - 1, step, 0)

    def own_copy(t, c):
        source = acts if t == 0 else incoming.at[t - 1]
        return pltpu.make_async_copy(
            source.at[:, pl.ds(c * cols, cols)], xown.at[t, c], own_sem.at[t, c]
        )

    def gate_copy(c):
        span = pl.ds(c * cols, cols)
        return (
            pltpu.make_async_copy(w_gate_hbm.at[span], w_gate.at[span], w_sem.at[0, c]),
            pltpu.make_async_copy(w_up_hbm.at[span], w_up.at[span], w_sem.at[1, c]),
        )

    down_copy = pltpu.make_async_copy(w_down_hbm, w_down, w_sem.at[2, 0])

    def sel_copy(t):
        return pltpu.make_async_remote_copy(
            sel_out.at[t],
            sel_in.at[t],
            sel_send.at[t],
            sel_recv.at[t],
            device_id=(previous, e),
            device_id_type=MESH,
        )

    def raw_copy(t, c):
        return pltpu.make_async_remote_copy(
            moved.at[t, c],
            xown.at[t + 1, c],
            raw_send.at[t, c],
            raw_recv.at[t, c],
            device_id=(following, e),
            device_id_type=MESH,
        )

    def x_copy(slot, t, c, section, d):
        return pltpu.make_async_remote_copy(
            xsend.at[slot, c, d // group],
            xrecv.at[t, c, e],
            x_send.at[slot, c, d],
            x_recv.at[t, c, e],
            device_id=(section, d),
            device_id_type=MESH,
        )

    def x_arrival(t, c, d):
        return pltpu.make_async_remote_copy(
            xrecv.at[t, c, d],
            xrecv.at[t, c, d],
            x_send.at[0, c, d],
            x_recv.at[t, c, d],
            device_id=(s, d),
            device_id_type=MESH,
        )

    def p_copy(t, c, d):
        return pltpu.make_async_remote_copy(
            psend.at[t, c, d],
            precv.at[t, c, e],
            p_send.at[t, c, d],
            p_recv.at[t, c, e],
            device_id=(s, d),
            device_id_type=MESH,
        )

    def p_arrival(t, c, d):
        return pltpu.make_async_remote_copy(
            precv.at[t, c, d],
            precv.at[t, c, d],
            p_send.at[t, c, d],
            p_recv.at[t, c, d],
            device_id=(s, d),
            device_id_type=MESH,
        )

    for c in range(chunks):
        own_copy(0, c).start()

    barrier = pltpu.get_barrier_semaphore()

    def greet(d, _):
        @pl.when(d != e)
        def _():
            pl.semaphore_signal(barrier, inc=1, device_id=(s, d), device_id_type=MESH)

        @pl.when(has_next)
        def _():
            pl.semaphore_signal(barrier, inc=1, device_id=(following, d), device_id_type=MESH)

        @pl.when(has_prev)
        def _():
            pl.semaphore_signal(barrier, inc=1, device_id=(previous, d), device_id_type=MESH)

        return 0

    lax.fori_loop(0, n, greet, 0)

    for c in range(chunks):
        for copy in gate_copy(c):
            copy.start()
    down_copy.start()

    @pl.when(jnp.logical_not(has_prev))
    def _():
        for t in range(1, ticks):
            for c in range(chunks):
                own_copy(t, c).start()

    def iota(shape, axis):
        return lax.broadcasted_iota(jnp.int32, shape, axis)

    before = (iota((tokens, tokens), 0) < iota((tokens, tokens), 1)).astype(half)
    diagonal = iota((tokens, tokens), 0) == iota((tokens, tokens), 1)
    sel_first = None
    for t in range(ticks):
        chosen = routes[t, 0]
        hot = sum(
            (iota((EXPERTS, tokens), 0) == chosen[k : k + 1]).astype(single) for k in range(top)
        )
        rank = jnp.dot(hot.astype(half), before, preferred_element_type=single)
        place = iota((cap, tokens), 0).astype(single)
        whole = None
        for k in range(top):
            blocks = []
            for x in range(EXPERTS):
                slot = jnp.where(chosen[k : k + 1] == x, rank[x : x + 1], -1.0)
                blocks.append((place == slot).astype(single))
            spread = jnp.concatenate([b for b in blocks for _ in range(group)], axis=0)
            pick[t, k * tokens : (k + 1) * tokens, :] = lax.dot_general(
                diagonal.astype(half),
                spread.astype(half),
                (((1,), (1,)), ((), ())),
                preferred_element_type=single,
            ).astype(half)
            mine = jnp.concatenate(blocks, axis=0)
            whole = mine if whole is None else whole + mine
        if t == 0:
            sel_first = whole.astype(half)
        else:
            sel_out[t - 1] = whole.astype(half)

    pl.semaphore_wait(
        barrier, n - 1 + jnp.where(has_next, n, 0) + jnp.where(has_prev, n, 0)
    )

    def pack(slot, c, sel, value):
        packed = jnp.dot(sel, value, preferred_element_type=single)
        for x in range(EXPERTS):
            xsend[slot, c, x] = packed[x * cap : (x + 1) * cap].astype(half)

    def keep(slot, t, c):
        xrecv[t, c, e] = xsend[slot, c, e // group]

    paired = sections % 2 == 0
    leads = lax.rem(s, 2) == 0
    if paired:

        @pl.when(jnp.logical_not(leads))
        def _():
            pl.semaphore_wait(turn, 1)

    for c in range(chunks):
        own_copy(0, c).wait()
        pack(0, c, sel_first, xown[0, c])
        others(lambda d: x_copy(0, 0, c, s, d).start())
        keep(0, 0, c)

    @pl.when(has_prev)
    def _():
        for t in range(ticks - 1):
            sel_copy(t).start()

    for c in range(chunks):
        others(lambda d: x_copy(0, 0, c, s, d).wait_send())
    if paired:

        @pl.when(leads)
        def _():
            pl.semaphore_signal(turn, inc=1, device_id=(following, e), device_id_type=MESH)

    def stack(ref, t, c):
        return jnp.concatenate([ref[t, c, d].astype(single) for d in range(n)], axis=0)

    for t in range(ticks):
        gate_val = up_val = None
        squares = jnp.zeros((rows, 1), single)
        for c in range(chunks):
            if t == 0:
                others(lambda d: x_arrival(t, c, d).wait_recv())
                for copy in gate_copy(c):
                    copy.wait()
            else:

                def arrive(d, _):
                    @pl.when(jnp.logical_or(has_prev, d != e))
                    def _():
                        x_arrival(t, c, d).wait_recv()

                    return 0

                lax.fori_loop(0, n, arrive, 0)
            span = pl.ds(c * cols, cols)
            value = stack(xrecv, t, c)
            squares = squares + jnp.sum(value * value, axis=1, keepdims=True)
            normed = (value * gain[:, span]).astype(half)
            gate_part = jnp.dot(normed, w_gate[span, :], preferred_element_type=single)
            up_part = jnp.dot(normed, w_up[span, :], preferred_element_type=single)
            gate_val = gate_part if gate_val is None else gate_val + gate_part
            up_val = up_part if up_val is None else up_val + up_part
        scale = lax.rsqrt(squares * (1.0 / width) + 1e-06)
        hidden = (jax.nn.silu(gate_val * scale) * (up_val * scale)).astype(half)
        if t == 0:
            down_copy.wait()
        for c in range(chunks):
            span = pl.ds(c * cols, cols)
            value = jnp.dot(hidden, w_down[:, span], preferred_element_type=single)
            for d in range(n):
                psend[t, c, d] = value[d * cap : (d + 1) * cap].astype(half)
            others(lambda d: p_copy(t, c, d).start())
            precv[t, c, e] = psend[t, c, e]

        if t < ticks - 1:

            @pl.when(jnp.logical_not(has_prev))
            def _():
                for c in range(chunks):
                    own_copy(t + 1, c).wait()
                    pack(t + 1, c, sel_out[t], xown[t + 1, c])
                    others(lambda d: x_copy(t + 1, t + 1, c, s, d).start())
                    keep(t + 1, t + 1, c)

            @pl.when(has_next)
            def _():
                sel_copy(t).wait_recv()

        weights = [
            jnp.sum(
                jnp.where(diagonal, route_weight[t, 0][k : k + 1], 0.0), axis=1, keepdims=True
            )
            for k in range(top)
        ]
        for c in range(chunks):
            if t > 0:

                @pl.when(has_prev)
                def _():
                    raw_copy(t - 1, c).wait_recv()

            others(lambda d: p_arrival(t, c, d).wait_recv())
            back = jnp.dot(
                pick[t], stack(precv, t, c).astype(half), preferred_element_type=single
            )
            layer = xown[t, c].astype(single)
            for k in range(top):
                layer = layer + back[k * tokens : (k + 1) * tokens] * weights[k]
            layer = layer.astype(half)
            out[t, :, pl.ds(c * cols, cols)] = layer
            if t < ticks - 1:

                @pl.when(has_next)
                def _():
                    pack(ticks + t, c, sel_in[t], layer)

                    def forward(i, _):
                        x_copy(ticks + t, t + 1, c, following, i).start()
                        return 0

                    lax.fori_loop(0, n, forward, 0)
                    moved[t, c] = layer
                    raw_copy(t, c).start()

    def drain(d, _):
        for c in range(chunks):

            @pl.when(d != e)
            def _():
                for t in range(ticks):
                    p_copy(t, c, d).wait_send()

            @pl.when(jnp.logical_and(d != e, jnp.logical_not(has_prev)))
            def _():
                for t in range(1, ticks):
                    x_copy(t, t, c, s, d).wait_send()

            @pl.when(has_next)
            def _():
                for t in range(ticks - 1):
                    x_copy(ticks + t, t + 1, c, following, d).wait_send()

        return 0

    lax.fori_loop(0, n, drain, 0)

    for t in range(ticks - 1):

        @pl.when(has_next)
        def _():
            for c in range(chunks):
                raw_copy(t, c).wait_send()

        @pl.when(has_prev)
        def _():
            sel_copy(t).wait_send()


def solution(mesh):
    n = mesh.shape["expert"]
    sections = mesh.shape["section"]

    def shards(acts, incoming, routes, route_weight, norm_gain, w_gate, w_up, w_down):
        ticks, _, tokens, _ = routes.shape
        width, hidden = w_gate.shape[1:]
        chunks = 5 if width % (5 * 128) == 0 else 4
        cols = width // chunks
        cap = min(CAP, tokens)
        half = jnp.bfloat16
        anywhere = pl.BlockSpec(memory_space=pl.ANY)
        vmem = pl.BlockSpec(memory_space=pltpu.VMEM)
        dma = pltpu.SemaphoreType.DMA
        moves = max(ticks - 1, 1)
        result = pl.pallas_call(
            functools.partial(kernel, n, sections),
            out_shape=jax.ShapeDtypeStruct((ticks, tokens, width), half),
            in_specs=[anywhere, anywhere, vmem, vmem, vmem, anywhere, anywhere, anywhere],
            out_specs=vmem,
            scratch_shapes=[
                pltpu.VMEM((width, hidden), half),
                pltpu.VMEM((width, hidden), half),
                pltpu.VMEM((hidden, width), half),
                pltpu.VMEM((ticks, chunks, tokens, cols), half),
                pltpu.VMEM((moves, chunks, tokens, cols), half),
                pltpu.VMEM((2 * ticks - 1, chunks, EXPERTS, cap, cols), half),
                pltpu.VMEM((ticks, chunks, n, cap, cols), half),
                pltpu.VMEM((ticks, chunks, n, cap, cols), half),
                pltpu.VMEM((ticks, chunks, n, cap, cols), half),
                pltpu.VMEM((moves, EXPERTS * cap, tokens), half),
                pltpu.VMEM((moves, EXPERTS * cap, tokens), half),
                pltpu.VMEM((ticks, routes.shape[3] * tokens, n * cap), half),
                dma((3, chunks)),
                dma((ticks, chunks)),
                dma((moves,)),
                dma((moves,)),
                dma((moves, chunks)),
                dma((moves, chunks)),
                dma((2 * ticks - 1, chunks, n)),
                dma((ticks, chunks, n)),
                dma((ticks, chunks, n)),
                dma((ticks, chunks, n)),
                pltpu.SemaphoreType.REGULAR,
            ],
            compiler_params=pltpu.CompilerParams(
                collective_id=0, has_side_effects=True, vmem_limit_bytes=56 << 20
            ),
        )(
            acts[0],
            incoming,
            jnp.swapaxes(routes, 2, 3),
            jnp.swapaxes(route_weight, 2, 3),
            norm_gain,
            w_gate[0],
            w_up[0],
            w_down[0],
        )
        return result[:, None]

    return jax.shard_map(
        shards,
        mesh=mesh,
        in_specs=(
            P("section", "expert", None),
            P(None, "expert", None),
            P(None, "section", "expert", None),
            P(None, "section", "expert", None),
            P("section", None),
            P("section", None, "expert"),
            P("section", None, "expert"),
            P("section", "expert", None),
        ),
        out_specs=P(None, "section", "expert", None),
        check_vma=False,
    )
```

```python
import functools

import jax
import jax.numpy as jnp
from jax import lax
from jax.experimental import pallas as pl
from jax.experimental.pallas import tpu as pltpu
from jax.sharding import PartitionSpec as P

MESH = pl.DeviceIdType.MESH
EXPERTS = 4
CAP = 24


def kernel(
    n,
    sections,
    acts,
    incoming,
    routes,
    route_weight,
    gain,
    w_gate_hbm,
    w_up_hbm,
    w_down_hbm,
    out,
    w_gate,
    w_up,
    w_down,
    xown,
    moved,
    xsend,
    xrecv,
    psend,
    precv,
    sel_out,
    sel_in,
    pick,
    w_sem,
    own_sem,
    sel_send,
    sel_recv,
    raw_send,
    raw_recv,
    x_send,
    x_recv,
    p_send,
    p_recv,
    turn,
):
    s = lax.axis_index("section")
    e = lax.axis_index("expert")
    ticks, chunks, tokens, cols = xown.shape
    top = routes.shape[2]
    cap = xsend.shape[3]
    group = n // EXPERTS
    width = chunks * cols
    rows = n * cap
    has_next = s < sections - 1
    has_prev = s > 0
    following = jnp.minimum(s + 1, sections - 1)
    previous = jnp.maximum(s - 1, 0)
    half = jnp.bfloat16
    single = jnp.float32

    def others(body):
        def step(i, _):
            k = n - 1 - i
            for d, there in ((e + k, e + k < n), (e - k, e - k >= 0)):

                @pl.when(there)
                def _():
                    body(jnp.clip(d, 0, n - 1))

            return 0

        lax.fori_loop(0, n - 1, step, 0)

    def own_copy(t, c):
        source = acts if t == 0 else incoming.at[t - 1]
        return pltpu.make_async_copy(
            source.at[:, pl.ds(c * cols, cols)], xown.at[t, c], own_sem.at[t, c]
        )

    def gate_copy(c):
        span = pl.ds(c * cols, cols)
        return (
            pltpu.make_async_copy(w_gate_hbm.at[span], w_gate.at[span], w_sem.at[0, c]),
            pltpu.make_async_copy(w_up_hbm.at[span], w_up.at[span], w_sem.at[1, c]),
        )

    down_copy = pltpu.make_async_copy(w_down_hbm, w_down, w_sem.at[2, 0])

    def sel_copy(t):
        return pltpu.make_async_remote_copy(
            sel_out.at[t],
            sel_in.at[t],
            sel_send.at[t],
            sel_recv.at[t],
            device_id=(previous, e),
            device_id_type=MESH,
        )

    def raw_copy(t, c):
        return pltpu.make_async_remote_copy(
            moved.at[t, c],
            xown.at[t + 1, c],
            raw_send.at[t, c],
            raw_recv.at[t, c],
            device_id=(following, e),
            device_id_type=MESH,
        )

    def x_copy(slot, t, c, section, d):
        return pltpu.make_async_remote_copy(
            xsend.at[slot, c, d // group],
            xrecv.at[t, c, e],
            x_send.at[slot, c, d],
            x_recv.at[t, c, e],
            device_id=(section, d),
            device_id_type=MESH,
        )

    def x_arrival(t, c, d):
        return pltpu.make_async_remote_copy(
            xrecv.at[t, c, d],
            xrecv.at[t, c, d],
            x_send.at[0, c, d],
            x_recv.at[t, c, d],
            device_id=(s, d),
            device_id_type=MESH,
        )

    def p_copy(t, c, d):
        return pltpu.make_async_remote_copy(
            psend.at[t, c, d],
            precv.at[t, c, e],
            p_send.at[t, c, d],
            p_recv.at[t, c, e],
            device_id=(s, d),
            device_id_type=MESH,
        )

    def p_arrival(t, c, d):
        return pltpu.make_async_remote_copy(
            precv.at[t, c, d],
            precv.at[t, c, d],
            p_send.at[t, c, d],
            p_recv.at[t, c, d],
            device_id=(s, d),
            device_id_type=MESH,
        )

    for c in range(chunks):
        own_copy(0, c).start()

    barrier = pltpu.get_barrier_semaphore()

    def greet(d, _):
        @pl.when(d != e)
        def _():
            pl.semaphore_signal(barrier, inc=1, device_id=(s, d), device_id_type=MESH)

        return 0

    lax.fori_loop(0, n, greet, 0)
    for there, section in ((has_next, following), (has_prev, previous)):

        @pl.when(there)
        def _():
            pl.semaphore_signal(barrier, inc=1, device_id=(section, e), device_id_type=MESH)

    for c in range(chunks):
        for copy in gate_copy(c):
            copy.start()
    down_copy.start()

    @pl.when(jnp.logical_not(has_prev))
    def _():
        for t in range(1, ticks):
            for c in range(chunks):
                own_copy(t, c).start()

    def iota(shape, axis):
        return lax.broadcasted_iota(jnp.int32, shape, axis)

    before = (iota((tokens, tokens), 0) < iota((tokens, tokens), 1)).astype(half)
    diagonal = iota((tokens, tokens), 0) == iota((tokens, tokens), 1)
    sel_first = None
    for t in range(ticks):
        chosen = routes[t, 0]
        hot = sum(
            (iota((EXPERTS, tokens), 0) == chosen[k : k + 1]).astype(single) for k in range(top)
        )
        rank = jnp.dot(hot.astype(half), before, preferred_element_type=single)
        place = iota((cap, tokens), 0).astype(single)
        whole = None
        for k in range(top):
            blocks = []
            for x in range(EXPERTS):
                slot = jnp.where(chosen[k : k + 1] == x, rank[x : x + 1], -1.0)
                blocks.append((place == slot).astype(single))
            spread = jnp.concatenate([b for b in blocks for _ in range(group)], axis=0)
            pick[t, k * tokens : (k + 1) * tokens, :] = lax.dot_general(
                diagonal.astype(half),
                spread.astype(half),
                (((1,), (1,)), ((), ())),
                preferred_element_type=single,
            ).astype(half)
            mine = jnp.concatenate(blocks, axis=0)
            whole = mine if whole is None else whole + mine
        if t == 0:
            sel_first = whole.astype(half)
        else:
            sel_out[t - 1] = whole.astype(half)

    pl.semaphore_wait(
        barrier, n - 1 + jnp.where(has_next, 1, 0) + jnp.where(has_prev, 1, 0)
    )

    def pack(slot, c, sel, value):
        packed = jnp.dot(sel, value, preferred_element_type=single)
        for x in range(EXPERTS):
            xsend[slot, c, x] = packed[x * cap : (x + 1) * cap].astype(half)

    def keep(slot, t, c):
        xrecv[t, c, e] = xsend[slot, c, e // group]

    paired = sections % 2 == 0
    leads = lax.rem(s, 2) == 0
    if paired:

        @pl.when(jnp.logical_not(leads))
        def _():
            pl.semaphore_wait(turn, 1)

    for c in range(chunks):
        own_copy(0, c).wait()
        pack(0, c, sel_first, xown[0, c])
        others(lambda d: x_copy(0, 0, c, s, d).start())
        keep(0, 0, c)

    @pl.when(has_prev)
    def _():
        for t in range(ticks - 1):
            sel_copy(t).start()

    for c in range(chunks):
        others(lambda d: x_copy(0, 0, c, s, d).wait_send())
    if paired:

        @pl.when(leads)
        def _():
            pl.semaphore_signal(turn, inc=1, device_id=(following, e), device_id_type=MESH)

    def stack(ref, t, c):
        return jnp.concatenate([ref[t, c, d].astype(single) for d in range(n)], axis=0)

    for t in range(ticks):
        gate_val = up_val = None
        squares = jnp.zeros((rows, 1), single)
        for c in range(chunks):
            if t == 0:
                others(lambda d: x_arrival(t, c, d).wait_recv())
                for copy in gate_copy(c):
                    copy.wait()
            else:

                def arrive(d, _):
                    @pl.when(jnp.logical_or(has_prev, d != e))
                    def _():
                        x_arrival(t, c, d).wait_recv()

                    return 0

                lax.fori_loop(0, n, arrive, 0)
            span = pl.ds(c * cols, cols)
            value = stack(xrecv, t, c)
            squares = squares + jnp.sum(value * value, axis=1, keepdims=True)
            normed = (value * gain[:, span]).astype(half)
            gate_part = jnp.dot(normed, w_gate[span, :], preferred_element_type=single)
            up_part = jnp.dot(normed, w_up[span, :], preferred_element_type=single)
            gate_val = gate_part if gate_val is None else gate_val + gate_part
            up_val = up_part if up_val is None else up_val + up_part
        scale = lax.rsqrt(squares * (1.0 / width) + 1e-06)
        hidden = (jax.nn.silu(gate_val * scale) * (up_val * scale)).astype(half)
        if t == 0:
            down_copy.wait()
        for c in range(chunks):
            span = pl.ds(c * cols, cols)
            value = jnp.dot(hidden, w_down[:, span], preferred_element_type=single)
            for d in range(n):
                psend[t, c, d] = value[d * cap : (d + 1) * cap].astype(half)
            others(lambda d: p_copy(t, c, d).start())
            precv[t, c, e] = psend[t, c, e]

        if t < ticks - 1:

            @pl.when(has_next)
            def _():
                sel_copy(t).wait_recv()

        weights = [
            jnp.sum(
                jnp.where(diagonal, route_weight[t, 0][k : k + 1], 0.0), axis=1, keepdims=True
            )
            for k in range(top)
        ]
        for c in range(chunks):
            if t > 0:

                @pl.when(has_prev)
                def _():
                    raw_copy(t - 1, c).wait_recv()

            others(lambda d: p_arrival(t, c, d).wait_recv())
            back = jnp.dot(
                pick[t], stack(precv, t, c).astype(half), preferred_element_type=single
            )
            layer = xown[t, c].astype(single)
            for k in range(top):
                layer = layer + back[k * tokens : (k + 1) * tokens] * weights[k]
            layer = layer.astype(half)
            out[t, :, pl.ds(c * cols, cols)] = layer
            if t < ticks - 1:

                @pl.when(has_next)
                def _():
                    pack(ticks + t, c, sel_in[t], layer)

                    def forward(i, _):
                        x_copy(ticks + t, t + 1, c, following, i).start()
                        return 0

                    lax.fori_loop(0, n, forward, 0)
                    moved[t, c] = layer
                    raw_copy(t, c).start()

        if t < ticks - 1:

            @pl.when(jnp.logical_not(has_prev))
            def _():
                for c in range(chunks):
                    own_copy(t + 1, c).wait()
                    pack(t + 1, c, sel_out[t], xown[t + 1, c])
                    others(lambda d: x_copy(t + 1, t + 1, c, s, d).start())
                    keep(t + 1, t + 1, c)

    def drain(d, _):
        for c in range(chunks):

            @pl.when(d != e)
            def _():
                for t in range(ticks):
                    p_copy(t, c, d).wait_send()

            @pl.when(jnp.logical_and(d != e, jnp.logical_not(has_prev)))
            def _():
                for t in range(1, ticks):
                    x_copy(t, t, c, s, d).wait_send()

            @pl.when(has_next)
            def _():
                for t in range(ticks - 1):
                    x_copy(ticks + t, t + 1, c, following, d).wait_send()

        return 0

    lax.fori_loop(0, n, drain, 0)

    for t in range(ticks - 1):

        @pl.when(has_next)
        def _():
            for c in range(chunks):
                raw_copy(t, c).wait_send()

        @pl.when(has_prev)
        def _():
            sel_copy(t).wait_send()


def solution(mesh):
    n = mesh.shape["expert"]
    sections = mesh.shape["section"]

    def shards(acts, incoming, routes, route_weight, norm_gain, w_gate, w_up, w_down):
        ticks, _, tokens, _ = routes.shape
        width, hidden = w_gate.shape[1:]
        chunks = 5 if width % (5 * 128) == 0 else 4
        cols = width // chunks
        cap = min(CAP, tokens)
        half = jnp.bfloat16
        anywhere = pl.BlockSpec(memory_space=pl.ANY)
        vmem = pl.BlockSpec(memory_space=pltpu.VMEM)
        dma = pltpu.SemaphoreType.DMA
        moves = max(ticks - 1, 1)
        result = pl.pallas_call(
            functools.partial(kernel, n, sections),
            out_shape=jax.ShapeDtypeStruct((ticks, tokens, width), half),
            in_specs=[anywhere, anywhere, vmem, vmem, vmem, anywhere, anywhere, anywhere],
            out_specs=vmem,
            scratch_shapes=[
                pltpu.VMEM((width, hidden), half),
                pltpu.VMEM((width, hidden), half),
                pltpu.VMEM((hidden, width), half),
                pltpu.VMEM((ticks, chunks, tokens, cols), half),
                pltpu.VMEM((moves, chunks, tokens, cols), half),
                pltpu.VMEM((2 * ticks - 1, chunks, EXPERTS, cap, cols), half),
                pltpu.VMEM((ticks, chunks, n, cap, cols), half),
                pltpu.VMEM((ticks, chunks, n, cap, cols), half),
                pltpu.VMEM((ticks, chunks, n, cap, cols), half),
                pltpu.VMEM((moves, EXPERTS * cap, tokens), half),
                pltpu.VMEM((moves, EXPERTS * cap, tokens), half),
                pltpu.VMEM((ticks, routes.shape[3] * tokens, n * cap), half),
                dma((3, chunks)),
                dma((ticks, chunks)),
                dma((moves,)),
                dma((moves,)),
                dma((moves, chunks)),
                dma((moves, chunks)),
                dma((2 * ticks - 1, chunks, n)),
                dma((ticks, chunks, n)),
                dma((ticks, chunks, n)),
                dma((ticks, chunks, n)),
                pltpu.SemaphoreType.REGULAR,
            ],
            compiler_params=pltpu.CompilerParams(
                collective_id=0, has_side_effects=True, vmem_limit_bytes=56 << 20
            ),
        )(
            acts[0],
            incoming,
            jnp.swapaxes(routes, 2, 3),
            jnp.swapaxes(route_weight, 2, 3),
            norm_gain,
            w_gate[0],
            w_up[0],
            w_down[0],
        )
        return result[:, None]

    return jax.shard_map(
        shards,
        mesh=mesh,
        in_specs=(
            P("section", "expert", None),
            P(None, "expert", None),
            P(None, "section", "expert", None),
            P(None, "section", "expert", None),
            P("section", None),
            P("section", None, "expert"),
            P("section", None, "expert"),
            P("section", "expert", None),
        ),
        out_specs=P(None, "section", "expert", None),
        check_vma=False,
    )
```

```python
import functools

import jax
import jax.numpy as jnp
from jax import lax
from jax.experimental import pallas as pl
from jax.experimental.pallas import tpu as pltpu
from jax.sharding import PartitionSpec as P

MESH = pl.DeviceIdType.MESH
EXPERTS = 4
CAP = 24


def kernel(
    n,
    sections,
    acts,
    incoming,
    routes,
    route_weight,
    gain,
    w_gate_hbm,
    w_up_hbm,
    w_down_hbm,
    out,
    w_gate,
    w_up,
    w_down,
    xown,
    moved,
    xsend,
    xraw,
    xrelay,
    xrecv,
    psend,
    precv,
    pgate,
    fsend,
    frecv,
    sel,
    sel_in,
    sel_far,
    pick,
    pick_far,
    rate,
    rate_far,
    w_sem,
    own_sem,
    table_send,
    table_recv,
    sel_send,
    sel_recv,
    raw_send,
    raw_recv,
    far_send,
    far_recv,
    x_send,
    x_recv,
    relay_send,
    p_send,
    p_recv,
    gate_send,
    gate_recv,
    f_send,
    f_recv,
    turn,
):
    s = lax.axis_index("section")
    e = lax.axis_index("expert")
    ticks, chunks, tokens, cols = xown.shape
    top = routes.shape[2]
    cap = xrecv.shape[3]
    group = n // EXPERTS
    mid = n // 2
    sided = EXPERTS // 2
    width = chunks * cols
    rows = n * cap
    side = e // mid
    base, far_base = side * mid, (1 - side) * mid
    own = e - base
    near_gate = jnp.where(side == 0, mid - 1, mid)
    far_gate = jnp.where(side == 0, mid, mid - 1)
    is_gate = e == near_gate
    not_gate = e != near_gate
    has_next = s < sections - 1
    has_prev = s > 0
    following = jnp.minimum(s + 1, sections - 1)
    previous = jnp.maximum(s - 1, 0)
    half = jnp.bfloat16
    single = jnp.float32

    def remote(source, target, send, recv, section, device):
        return pltpu.make_async_remote_copy(
            source, target, send, recv, device_id=(section, device), device_id_type=MESH
        )

    def near(body, own_too=False):
        def step(i, _):
            body(base + lax.rem(own + i, mid))
            return 0

        lax.fori_loop(0 if own_too else 1, mid, step, 0)

    def own_copy(t, c):
        source = acts if t == 0 else incoming.at[t - 1]
        return pltpu.make_async_copy(
            source.at[:, pl.ds(c * cols, cols)], xown.at[t, c], own_sem.at[t, c]
        )

    def gate_copy(c):
        span = pl.ds(c * cols, cols)
        return (
            pltpu.make_async_copy(w_gate_hbm.at[span], w_gate.at[span], w_sem.at[0, c]),
            pltpu.make_async_copy(w_up_hbm.at[span], w_up.at[span], w_sem.at[1, c]),
        )

    down_copy = pltpu.make_async_copy(w_down_hbm, w_down, w_sem.at[2, 0])

    def table_copies(t):
        pairs = (
            (sel.at[t, 1 - side], sel_far),
            (pick.at[t, 1 - side], pick_far),
            (rate.at[t], rate_far),
        )
        return [
            remote(
                source,
                target.at[t, own],
                table_send.at[i, t],
                table_recv.at[i, t, own],
                s,
                far_gate,
            )
            for i, (source, target) in enumerate(pairs)
        ]

    def table_arrival(i, t, j):
        target = (sel_far, pick_far, rate_far)[i].at[t, j]
        return remote(target, target, table_send.at[i, t], table_recv.at[i, t, j], s, far_base + j)

    def sel_copy(t):
        return remote(
            sel.at[t + 1, side], sel_in.at[t], sel_send.at[t], sel_recv.at[t], previous, e
        )

    def raw_copy(t, c):
        return remote(
            moved.at[t, c], xown.at[t + 1, c], raw_send.at[t, c], raw_recv.at[t, c], following, e
        )

    def far_copy(slot, t, c, section, source):
        return remote(
            source, xraw.at[t, c, own], far_send.at[slot, c], far_recv.at[t, c, own], section, far_gate
        )

    def far_arrival(t, c, j):
        target = xraw.at[t, c, j]
        return remote(target, target, far_send.at[0, c], far_recv.at[t, c, j], s, far_base + j)

    def x_copy(slot, t, c, section, d):
        return remote(
            xsend.at[slot, c, d // group - side * sided],
            xrecv.at[t, c, e],
            x_send.at[slot, c, d - base],
            x_recv.at[t, c, e],
            section,
            d,
        )

    def relay_copy(t, c, j, d):
        return remote(
            xrelay.at[t, c, j, d // group - side * sided],
            xrecv.at[t, c, far_base + j],
            relay_send.at[t, c, j, d - base],
            x_recv.at[t, c, far_base + j],
            s,
            d,
        )

    def x_arrival(t, c, d):
        target = xrecv.at[t, c, d]
        return remote(target, target, x_send.at[0, c, 0], x_recv.at[t, c, d], s, d)

    def p_copy(t, c, d):
        return remote(
            psend.at[t, c, side, d - base],
            precv.at[t, c, own],
            p_send.at[t, c, d - base],
            p_recv.at[t, c, own],
            s,
            d,
        )

    def p_arrival(t, c, d):
        target = precv.at[t, c, d - base]
        return remote(target, target, p_send.at[t, c, 0], p_recv.at[t, c, d - base], s, d)

    def gate_send_copy(t, c):
        return remote(
            psend.at[t, c, 1 - side],
            pgate.at[t, c, own],
            gate_send.at[t, c],
            gate_recv.at[t, c, own],
            s,
            near_gate,
        )

    def gate_arrival(t, c, d):
        target = pgate.at[t, c, d - base]
        return remote(target, target, gate_send.at[t, c], gate_recv.at[t, c, d - base], s, d)

    def f_copy(t, c, j):
        return remote(
            fsend.at[t, c, j], frecv.at[t, c], f_send.at[t, c, j], f_recv.at[t, c], s, far_base + j
        )

    for c in range(chunks):
        own_copy(0, c).start()

    barrier = pltpu.get_barrier_semaphore()

    def greet(d, _):
        @pl.when(d != e)
        def _():
            pl.semaphore_signal(barrier, inc=1, device_id=(s, d), device_id_type=MESH)

        return 0

    lax.fori_loop(0, n, greet, 0)
    for there, section in ((has_next, following), (has_prev, previous)):

        @pl.when(there)
        def _():
            pl.semaphore_signal(barrier, inc=1, device_id=(section, e), device_id_type=MESH)

    for c in range(chunks):
        for copy in gate_copy(c):
            copy.start()
    down_copy.start()

    @pl.when(jnp.logical_not(has_prev))
    def _():
        for t in range(1, ticks):
            for c in range(chunks):
                own_copy(t, c).start()

    def iota(shape, axis):
        return lax.broadcasted_iota(jnp.int32, shape, axis)

    before = (iota((tokens, tokens), 0) < iota((tokens, tokens), 1)).astype(half)
    diagonal = iota((tokens, tokens), 0) == iota((tokens, tokens), 1)
    place = iota((cap, tokens), 0).astype(single)
    for t in range(ticks):
        chosen = routes[t, 0]
        hot = sum(
            (iota((EXPERTS, tokens), 0) == chosen[k : k + 1]).astype(single) for k in range(top)
        )
        rank = jnp.dot(hot.astype(half), before, preferred_element_type=single)
        blocks = [
            [
                (place == jnp.where(chosen[k : k + 1] == x, rank[x : x + 1], -1.0)).astype(single)
                for x in range(EXPERTS)
            ]
            for k in range(top)
        ]
        for h in range(2):
            experts = range(h * sided, (h + 1) * sided)
            sel[t, h] = sum(
                jnp.concatenate([blocks[k][x] for x in experts], axis=0) for k in range(top)
            ).astype(half)
            for k in range(top):
                spread = jnp.concatenate(
                    [blocks[k][x] for x in experts for _ in range(group)], axis=0
                )
                pick[t, h, k * tokens : (k + 1) * tokens, :] = lax.dot_general(
                    diagonal.astype(half),
                    spread.astype(half),
                    (((1,), (1,)), ((), ())),
                    preferred_element_type=single,
                ).astype(half)
        rate[t] = jnp.zeros_like(rate[t])
        rate[t, 0:top, 0:tokens] = route_weight[t, 0]

    pl.semaphore_wait(
        barrier, n - 1 + jnp.where(has_next, 1, 0) + jnp.where(has_prev, 1, 0)
    )

    def pack(target, table, value):
        packed = jnp.dot(table, value, preferred_element_type=single)
        for x in range(sided):
            target[x] = packed[x * cap : (x + 1) * cap].astype(half)

    def dispatch(t, c):
        own_copy(t, c).wait()
        far_copy(t, t, c, s, xown.at[t, c]).start()
        pack(xsend.at[t, c], sel[t, side], xown[t, c])
        near(lambda d: x_copy(t, t, c, s, d).start())
        xrecv[t, c, e] = xsend[t, c, e // group - side * sided]

    paired = sections % 2 == 0
    leads = lax.rem(s, 2) == 0
    table_copies(0)[0].start()
    if paired:

        @pl.when(jnp.logical_not(leads))
        def _():
            pl.semaphore_wait(turn, 1)

    for c in range(chunks):
        dispatch(0, c)
    for t in range(ticks):
        for copy in table_copies(t)[1 if t == 0 else 0 :]:
            copy.start()

    @pl.when(has_prev)
    def _():
        for t in range(ticks - 1):
            sel_copy(t).start()

    def pass_turn():
        for c in range(chunks):
            far_copy(0, 0, c, s, xown.at[0, c]).wait_send()
            near(lambda d: x_copy(0, 0, c, s, d).wait_send())
        if paired:

            @pl.when(leads)
            def _():
                pl.semaphore_signal(turn, inc=1, device_id=(following, e), device_id_type=MESH)

    def relay(t, c):
        for j in range(mid):
            if c == 0:
                table_arrival(0, t, j).wait_recv()
            far_arrival(t, c, j).wait_recv()
            pack(xrelay.at[t, c, j], sel_far[t, j], xraw[t, c, j])
            near(lambda d: relay_copy(t, c, j, d).start())
            xrecv[t, c, far_base + j] = xrelay[t, c, j, e // group - side * sided]

    def combine(t, c):
        near(lambda d: gate_arrival(t, c, d).wait_recv())
        for j in range(mid):
            if c == 0:
                table_arrival(1, t, j).wait_recv()
                table_arrival(2, t, j).wait_recv()
            value = jnp.concatenate(
                [pgate[t, c, d, j].astype(single) for d in range(mid)], axis=0
            ).astype(half)
            back = jnp.dot(pick_far[t, j], value, preferred_element_type=single)
            total = None
            for k in range(top):
                part = back[k * tokens : (k + 1) * tokens] * column(rate_far[t, j], k)
                total = part if total is None else total + part
            fsend[t, c, j] = total.astype(half)
            f_copy(t, c, j).start()

    def column(table, k):
        return jnp.sum(
            jnp.where(diagonal, table[k : k + 1, 0:tokens], 0.0), axis=1, keepdims=True
        )

    for t in range(ticks):
        gate_val = up_val = None
        squares = jnp.zeros((rows, 1), single)
        if t == 0:

            @pl.when(not_gate)
            def _():
                pass_turn()

        for c in range(chunks):

            @pl.when(is_gate)
            def _():
                relay(t, c)

            @pl.when(not_gate)
            def _():
                for j in range(mid):
                    x_arrival(t, c, far_base + j).wait_recv()

            near(lambda d: x_arrival(t, c, d).wait_recv())
            if t == 0:
                for copy in gate_copy(c):
                    copy.wait()
            else:

                @pl.when(has_prev)
                def _():
                    x_arrival(t, c, e).wait_recv()

            span = pl.ds(c * cols, cols)
            value = jnp.concatenate([xrecv[t, c, d].astype(single) for d in range(n)], axis=0)
            squares = squares + jnp.sum(value * value, axis=1, keepdims=True)
            normed = (value * gain[:, span]).astype(half)
            gate_part = jnp.dot(normed, w_gate[span, :], preferred_element_type=single)
            up_part = jnp.dot(normed, w_up[span, :], preferred_element_type=single)
            gate_val = gate_part if gate_val is None else gate_val + gate_part
            up_val = up_part if up_val is None else up_val + up_part
        scale = lax.rsqrt(squares * (1.0 / width) + 1e-06)
        hidden = (jax.nn.silu(gate_val * scale) * (up_val * scale)).astype(half)
        if t == 0:

            @pl.when(is_gate)
            def _():
                pass_turn()

            down_copy.wait()
        for c in range(chunks):
            span = pl.ds(c * cols, cols)
            value = jnp.dot(hidden, w_down[:, span], preferred_element_type=single)
            for d in range(n):
                psend[t, c, d // mid, d % mid] = value[d * cap : (d + 1) * cap].astype(half)

            @pl.when(not_gate)
            def _():
                gate_send_copy(t, c).start()

            @pl.when(is_gate)
            def _():
                pgate[t, c, own] = psend[t, c, 1 - side]

            near(lambda d: p_copy(t, c, d).start())
            precv[t, c, own] = psend[t, c, side, own]

        @pl.when(is_gate)
        def _():
            for c in range(chunks):
                combine(t, c)

        if t < ticks - 1:

            @pl.when(has_next)
            def _():
                sel_copy(t).wait_recv()

        weights = [column(rate[t], k) for k in range(top)]
        for c in range(chunks):
            if t > 0:

                @pl.when(has_prev)
                def _():
                    raw_copy(t - 1, c).wait_recv()

            near(lambda d: p_arrival(t, c, d).wait_recv())
            f_copy(t, c, 0).wait_recv()
            value = jnp.concatenate(
                [precv[t, c, d].astype(single) for d in range(mid)], axis=0
            ).astype(half)
            back = jnp.dot(pick[t, side], value, preferred_element_type=single)
            layer = xown[t, c].astype(single) + frecv[t, c].astype(single)
            for k in range(top):
                layer = layer + back[k * tokens : (k + 1) * tokens] * weights[k]
            layer = layer.astype(half)
            out[t, :, pl.ds(c * cols, cols)] = layer
            if t < ticks - 1:

                @pl.when(has_next)
                def _():
                    moved[t, c] = layer
                    far_copy(ticks + t, t + 1, c, following, moved.at[t, c]).start()
                    pack(xsend.at[ticks + t, c], sel_in[t], layer)
                    near(lambda d: x_copy(ticks + t, t + 1, c, following, d).start(), True)
                    raw_copy(t, c).start()

        if t < ticks - 1:
            if paired:

                @pl.when(s == 1)
                def _():
                    pl.semaphore_signal(turn, inc=1, device_id=(previous, e), device_id_type=MESH)

            @pl.when(jnp.logical_not(has_prev))
            def _():
                if paired:
                    pl.semaphore_wait(turn, 1)
                for c in range(chunks):
                    dispatch(t + 1, c)

    for t in range(ticks):
        for copy in table_copies(t):
            copy.wait_send()
        for c in range(chunks):
            near(lambda d: p_copy(t, c, d).wait_send())

            @pl.when(not_gate)
            def _():
                gate_send_copy(t, c).wait_send()

            @pl.when(is_gate)
            def _():
                for j in range(mid):
                    f_copy(t, c, j).wait_send()
                    near(lambda d: relay_copy(t, c, j, d).wait_send())

            if t > 0:

                @pl.when(jnp.logical_not(has_prev))
                def _():
                    far_copy(t, t, c, s, xown.at[t, c]).wait_send()
                    near(lambda d: x_copy(t, t, c, s, d).wait_send())

            if t < ticks - 1:

                @pl.when(has_next)
                def _():
                    far_copy(ticks + t, t + 1, c, following, moved.at[t, c]).wait_send()
                    near(lambda d: x_copy(ticks + t, t + 1, c, following, d).wait_send(), True)
                    raw_copy(t, c).wait_send()

    @pl.when(has_prev)
    def _():
        for t in range(ticks - 1):
            sel_copy(t).wait_send()


def solution(mesh):
    n = mesh.shape["expert"]
    sections = mesh.shape["section"]

    def shards(acts, incoming, routes, route_weight, norm_gain, w_gate, w_up, w_down):
        ticks, _, tokens, top = routes.shape
        width, hidden = w_gate.shape[1:]
        chunks = 5 if width % (5 * 128) == 0 else 4
        cols = width // chunks
        cap = min(CAP, tokens)
        mid, sided, moves = n // 2, EXPERTS // 2, max(ticks - 1, 1)
        half, single = jnp.bfloat16, jnp.float32
        anywhere = pl.BlockSpec(memory_space=pl.ANY)
        vmem = pl.BlockSpec(memory_space=pltpu.VMEM)
        dma = pltpu.SemaphoreType.DMA
        result = pl.pallas_call(
            functools.partial(kernel, n, sections),
            out_shape=jax.ShapeDtypeStruct((ticks, tokens, width), half),
            in_specs=[anywhere, anywhere, vmem, vmem, vmem, anywhere, anywhere, anywhere],
            out_specs=vmem,
            scratch_shapes=[
                pltpu.VMEM((width, hidden), half),
                pltpu.VMEM((width, hidden), half),
                pltpu.VMEM((hidden, width), half),
                pltpu.VMEM((ticks, chunks, tokens, cols), half),
                pltpu.VMEM((moves, chunks, tokens, cols), half),
                pltpu.VMEM((2 * ticks - 1, chunks, sided, cap, cols), half),
                pltpu.VMEM((ticks, chunks, mid, tokens, cols), half),
                pltpu.VMEM((ticks, chunks, mid, sided, cap, cols), half),
                pltpu.VMEM((ticks, chunks, n, cap, cols), half),
                pltpu.VMEM((ticks, chunks, 2, mid, cap, cols), half),
                pltpu.VMEM((ticks, chunks, mid, cap, cols), half),
                pltpu.VMEM((ticks, chunks, mid, mid, cap, cols), half),
                pltpu.VMEM((ticks, chunks, mid, tokens, cols), half),
                pltpu.VMEM((ticks, chunks, tokens, cols), half),
                pltpu.VMEM((ticks, 2, sided * cap, tokens), half),
                pltpu.VMEM((moves, sided * cap, tokens), half),
                pltpu.VMEM((ticks, mid, sided * cap, tokens), half),
                pltpu.VMEM((ticks, 2, top * tokens, mid * cap), half),
                pltpu.VMEM((ticks, mid, top * tokens, mid * cap), half),
                pltpu.VMEM((ticks, 8, 128), single),
                pltpu.VMEM((ticks, mid, 8, 128), single),
                dma((3, chunks)),
                dma((ticks, chunks)),
                dma((3, ticks)),
                dma((3, ticks, mid)),
                dma((moves,)),
                dma((moves,)),
                dma((moves, chunks)),
                dma((moves, chunks)),
                dma((2 * ticks - 1, chunks)),
                dma((ticks, chunks, mid)),
                dma((2 * ticks - 1, chunks, mid)),
                dma((ticks, chunks, n)),
                dma((ticks, chunks, mid, mid)),
                dma((ticks, chunks, mid)),
                dma((ticks, chunks, mid)),
                dma((ticks, chunks)),
                dma((ticks, chunks, mid)),
                dma((ticks, chunks, mid)),
                dma((ticks, chunks)),
                pltpu.SemaphoreType.REGULAR,
            ],
            compiler_params=pltpu.CompilerParams(
                collective_id=0, has_side_effects=True, vmem_limit_bytes=60 << 20
            ),
        )(
            acts[0],
            incoming,
            jnp.swapaxes(routes, 2, 3),
            jnp.swapaxes(route_weight, 2, 3),
            norm_gain,
            w_gate[0],
            w_up[0],
            w_down[0],
        )
        return result[:, None]

    return jax.shard_map(
        shards,
        mesh=mesh,
        in_specs=(
            P("section", "expert", None),
            P(None, "expert", None),
            P(None, "section", "expert", None),
            P(None, "section", "expert", None),
            P("section", None),
            P("section", None, "expert"),
            P("section", None, "expert"),
            P("section", "expert", None),
        ),
        out_specs=P(None, "section", "expert", None),
        check_vma=False,
    )
```

```python
import functools

import jax
import jax.numpy as jnp
from jax import lax
from jax.experimental import pallas as pl
from jax.experimental.pallas import tpu as pltpu
from jax.sharding import PartitionSpec as P

MESH = pl.DeviceIdType.MESH
EXPERTS = 4
CAP = 24


def kernel(
    n,
    sections,
    acts,
    incoming,
    routes,
    route_weight,
    gain,
    w_gate_hbm,
    w_up_hbm,
    w_down_hbm,
    out,
    w_gate,
    w_up,
    w_down,
    xown,
    made,
    xsend,
    xrecv,
    psend,
    precv,
    pgate,
    fsend,
    frecv,
    sel,
    sel_in,
    pick,
    pick_far,
    rate,
    rate_far,
    w_sem,
    out_sem,
    own_sem,
    table_send,
    table_recv,
    sel_send,
    sel_recv,
    raw_send,
    raw_recv,
    x_send,
    x_recv,
    p_send,
    p_recv,
    gate_send,
    gate_recv,
    f_send,
    f_recv,
    turn,
):
    s = lax.axis_index("section")
    e = lax.axis_index("expert")
    ticks, chunks, tokens, cols = xown.shape
    top = routes.shape[2]
    cap = xrecv.shape[3]
    group = n // EXPERTS
    mid = n // 2
    sided = EXPERTS // 2
    gated = [t < ticks - 1 for t in range(ticks)]
    width = chunks * cols
    rows = n * cap
    side = e // mid
    base, far_base = side * mid, (1 - side) * mid
    own = e - base
    near_gate = jnp.where(side == 0, mid - 1, mid)
    far_gate = jnp.where(side == 0, mid, mid - 1)
    is_gate = e == near_gate
    not_gate = e != near_gate
    has_next = s < sections - 1
    has_prev = s > 0
    following = jnp.minimum(s + 1, sections - 1)
    previous = jnp.maximum(s - 1, 0)
    half = jnp.bfloat16
    single = jnp.float32

    def remote(source, target, send, recv, section, device):
        return pltpu.make_async_remote_copy(
            source, target, send, recv, device_id=(section, device), device_id_type=MESH
        )

    def near(body, own_too=False):
        def step(i, _):
            body(base + lax.rem(own + i, mid))
            return 0

        lax.fori_loop(0 if own_too else 1, mid, step, 0)

    def far(body):
        def step(i, _):
            body(far_base + i)
            return 0

        lax.fori_loop(0, mid, step, 0)

    def own_copy(t, c):
        source = acts if t == 0 else incoming.at[t - 1]
        return pltpu.make_async_copy(
            source.at[:, pl.ds(c * cols, cols)], xown.at[t, c], own_sem.at[t, c]
        )

    def gate_copy(c):
        span = pl.ds(c * cols, cols)
        return (
            pltpu.make_async_copy(w_gate_hbm.at[span], w_gate.at[span], w_sem.at[0, c]),
            pltpu.make_async_copy(w_up_hbm.at[span], w_up.at[span], w_sem.at[1, c]),
        )

    down_copy = pltpu.make_async_copy(w_down_hbm, w_down, w_sem.at[2, 0])

    def table_copies(t):
        pairs = ((pick.at[t, 1 - side], pick_far), (rate.at[t], rate_far))
        return [
            remote(
                source,
                target.at[t, own],
                table_send.at[i, t],
                table_recv.at[i, t, own],
                s,
                far_gate,
            )
            for i, (source, target) in enumerate(pairs)
        ]

    def table_arrival(i, t, j):
        target = (pick_far, rate_far)[i].at[t, j]
        return remote(target, target, table_send.at[i, t], table_recv.at[i, t, j], s, far_base + j)

    def out_copy(t, c):
        return pltpu.make_async_copy(
            made.at[t, c], out.at[t, :, pl.ds(c * cols, cols)], out_sem.at[t, c]
        )

    def sel_copy(t):
        return remote(
            sel.at[t + 1], sel_in.at[t], sel_send.at[t], sel_recv.at[t], previous, e
        )

    def raw_copy(t, c):
        return remote(
            made.at[t, c], xown.at[t + 1, c], raw_send.at[t, c], raw_recv.at[t, c], following, e
        )

    def x_copy(slot, t, c, section, d):
        return remote(
            xsend.at[slot, c, d // group],
            xrecv.at[t, c, e],
            x_send.at[slot, c, d],
            x_recv.at[t, c, e],
            section,
            d,
        )

    def x_arrival(t, c, d):
        target = xrecv.at[t, c, d]
        return remote(target, target, x_send.at[0, c, 0], x_recv.at[t, c, d], s, d)

    def p_copy(t, c, d):
        return remote(
            psend.at[t, c, d], precv.at[t, c, e], p_send.at[t, c, d], p_recv.at[t, c, e], s, d
        )

    def p_arrival(t, c, d):
        target = precv.at[t, c, d]
        return remote(target, target, p_send.at[t, c, 0], p_recv.at[t, c, d], s, d)

    def gate_send_copy(t, c):
        return remote(
            psend.at[t, c, pl.ds(far_base, mid)],
            pgate.at[t, c, own],
            gate_send.at[t, c],
            gate_recv.at[t, c, own],
            s,
            near_gate,
        )

    def gate_arrival(t, c, d):
        target = pgate.at[t, c, d - base]
        return remote(target, target, gate_send.at[t, c], gate_recv.at[t, c, d - base], s, d)

    def f_copy(t, c, j):
        return remote(
            fsend.at[t, c, j], frecv.at[t, c], f_send.at[t, c, j], f_recv.at[t, c], s, far_base + j
        )

    for c in range(chunks):
        own_copy(0, c).start()

    barrier = pltpu.get_barrier_semaphore()

    def greet(d, _):
        @pl.when(d != e)
        def _():
            pl.semaphore_signal(barrier, inc=1, device_id=(s, d), device_id_type=MESH)

        return 0

    lax.fori_loop(0, n, greet, 0)
    for there, section in ((has_next, following), (has_prev, previous)):

        @pl.when(there)
        def _():
            pl.semaphore_signal(barrier, inc=1, device_id=(section, e), device_id_type=MESH)

    for c in range(chunks):
        for copy in gate_copy(c):
            copy.start()
    down_copy.start()

    @pl.when(jnp.logical_not(has_prev))
    def _():
        for t in range(1, ticks):
            for c in range(chunks):
                own_copy(t, c).start()

    def iota(shape, axis):
        return lax.broadcasted_iota(jnp.int32, shape, axis)

    before = (iota((tokens, tokens), 0) < iota((tokens, tokens), 1)).astype(half)
    diagonal = iota((tokens, tokens), 0) == iota((tokens, tokens), 1)
    place = iota((cap, tokens), 0).astype(single)
    for t in range(ticks):
        chosen = routes[t, 0]
        hot = sum(
            (iota((EXPERTS, tokens), 0) == chosen[k : k + 1]).astype(single) for k in range(top)
        )
        rank = jnp.dot(hot.astype(half), before, preferred_element_type=single)
        blocks = [
            [
                (place == jnp.where(chosen[k : k + 1] == x, rank[x : x + 1], -1.0)).astype(single)
                for x in range(EXPERTS)
            ]
            for k in range(top)
        ]
        sel[t] = sum(jnp.concatenate(blocks[k], axis=0) for k in range(top)).astype(half)
        for h in range(2):
            experts = range(h * sided, (h + 1) * sided)
            for k in range(top):
                spread = jnp.concatenate(
                    [blocks[k][x] for x in experts for _ in range(group)], axis=0
                )
                pick[t, h, k * tokens : (k + 1) * tokens, :] = lax.dot_general(
                    diagonal.astype(half),
                    spread.astype(half),
                    (((1,), (1,)), ((), ())),
                    preferred_element_type=single,
                ).astype(half)
        rate[t] = jnp.zeros_like(rate[t])
        rate[t, 0:top, 0:tokens] = route_weight[t, 0]

    pl.semaphore_wait(
        barrier, n - 1 + jnp.where(has_next, 1, 0) + jnp.where(has_prev, 1, 0)
    )

    def pack(target, table, value):
        packed = jnp.dot(table, value, preferred_element_type=single)
        for x in range(EXPERTS):
            target[x] = packed[x * cap : (x + 1) * cap].astype(half)

    def dispatch(t, c):
        own_copy(t, c).wait()
        pack(xsend.at[t, c], sel[t], xown[t, c])
        far(lambda d: x_copy(t, t, c, s, d).start())
        near(lambda d: x_copy(t, t, c, s, d).start())
        xrecv[t, c, e] = xsend[t, c, e // group]

    paired = sections % 2 == 0
    leads = lax.rem(s, 2) == 0
    if paired:

        @pl.when(jnp.logical_not(leads))
        def _():
            pl.semaphore_wait(turn, 1)

    for c in range(chunks):
        dispatch(0, c)
    for t in range(ticks):
        if gated[t]:
            for copy in table_copies(t):
                copy.start()

    @pl.when(has_prev)
    def _():
        for t in range(ticks - 1):
            sel_copy(t).start()

    for c in range(chunks):
        far(lambda d: x_copy(0, 0, c, s, d).wait_send())
        near(lambda d: x_copy(0, 0, c, s, d).wait_send())
        if paired and c == max(chunks - 2, 0):

            @pl.when(leads)
            def _():
                pl.semaphore_signal(turn, inc=1, device_id=(following, e), device_id_type=MESH)

    def combine(t, c):
        near(lambda d: gate_arrival(t, c, d).wait_recv())
        for j in range(mid):
            if c == 0:
                table_arrival(0, t, j).wait_recv()
                table_arrival(1, t, j).wait_recv()
            value = jnp.concatenate(
                [pgate[t, c, d, j].astype(single) for d in range(mid)], axis=0
            ).astype(half)
            back = jnp.dot(pick_far[t, j], value, preferred_element_type=single)
            total = None
            for k in range(top):
                part = back[k * tokens : (k + 1) * tokens] * column(rate_far[t, j], k)
                total = part if total is None else total + part
            fsend[t, c, j] = total.astype(half)
            f_copy(t, c, j).start()

    def column(table, k):
        return jnp.sum(
            jnp.where(diagonal, table[k : k + 1, 0:tokens], 0.0), axis=1, keepdims=True
        )

    for t in range(ticks):
        gate_val = up_val = None
        squares = jnp.zeros((rows, 1), single)
        for c in range(chunks):
            far(lambda d: x_arrival(t, c, d).wait_recv())
            near(lambda d: x_arrival(t, c, d).wait_recv())
            if t == 0:
                for copy in gate_copy(c):
                    copy.wait()
            else:

                @pl.when(has_prev)
                def _():
                    x_arrival(t, c, e).wait_recv()

            span = pl.ds(c * cols, cols)
            value = jnp.concatenate([xrecv[t, c, d].astype(single) for d in range(n)], axis=0)
            squares = squares + jnp.sum(value * value, axis=1, keepdims=True)
            normed = (value * gain[:, span]).astype(half)
            gate_part = jnp.dot(normed, w_gate[span, :], preferred_element_type=single)
            up_part = jnp.dot(normed, w_up[span, :], preferred_element_type=single)
            gate_val = gate_part if gate_val is None else gate_val + gate_part
            up_val = up_part if up_val is None else up_val + up_part
        scale = lax.rsqrt(squares * (1.0 / width) + 1e-06)
        hidden = (jax.nn.silu(gate_val * scale) * (up_val * scale)).astype(half)
        if t == 0:
            down_copy.wait()
        for c in range(chunks):
            span = pl.ds(c * cols, cols)
            value = jnp.dot(hidden, w_down[:, span], preferred_element_type=single)
            for d in range(n):
                psend[t, c, d] = value[d * cap : (d + 1) * cap].astype(half)
            if gated[t]:

                @pl.when(not_gate)
                def _():
                    gate_send_copy(t, c).start()

                @pl.when(is_gate)
                def _():
                    pgate[t, c, own] = psend[t, c, pl.ds(far_base, mid)]

            else:
                far(lambda d: p_copy(t, c, d).start())
            near(lambda d: p_copy(t, c, d).start())
            precv[t, c, e] = psend[t, c, e]

        if gated[t]:

            @pl.when(is_gate)
            def _():
                for c in range(chunks):
                    combine(t, c)

        for c in range(chunks):
            near(lambda d: p_copy(t, c, d).wait_send())
            if gated[t]:

                @pl.when(not_gate)
                def _():
                    gate_send_copy(t, c).wait_send()

            else:
                far(lambda d: p_copy(t, c, d).wait_send())

        if t < ticks - 1:
            if paired:

                @pl.when(s == 1)
                def _():
                    pl.semaphore_signal(turn, inc=1, device_id=(previous, e), device_id_type=MESH)

            @pl.when(has_next)
            def _():
                sel_copy(t).wait_recv()

        weights = [column(rate[t], k) for k in range(top)]
        for c in range(chunks):
            if t > 0:

                @pl.when(has_prev)
                def _():
                    raw_copy(t - 1, c).wait_recv()

            near(lambda d: p_arrival(t, c, d).wait_recv())
            layer = xown[t, c].astype(single)
            if gated[t]:
                f_copy(t, c, 0).wait_recv()
                layer = layer + frecv[t, c].astype(single)
                sources, table = [base + j for j in range(mid)], pick[t, side]
            else:
                far(lambda d: p_arrival(t, c, d).wait_recv())
                sources = list(range(n))
                table = jnp.concatenate([pick[t, 0], pick[t, 1]], axis=1)
            value = jnp.concatenate(
                [precv[t, c, d].astype(single) for d in sources], axis=0
            ).astype(half)
            back = jnp.dot(table, value, preferred_element_type=single)
            for k in range(top):
                layer = layer + back[k * tokens : (k + 1) * tokens] * weights[k]
            layer = layer.astype(half)
            made[t, c] = layer
            out_copy(t, c).start()
            if t < ticks - 1:

                @pl.when(has_next)
                def _():
                    pack(xsend.at[ticks + t, c], sel_in[t], layer)
                    far(lambda d: x_copy(ticks + t, t + 1, c, following, d).start())
                    near(lambda d: x_copy(ticks + t, t + 1, c, following, d).start(), True)
                    raw_copy(t, c).start()

        if t < ticks - 1:

            @pl.when(jnp.logical_not(has_prev))
            def _():
                if paired:
                    pl.semaphore_wait(turn, 1)
                for c in range(chunks):
                    dispatch(t + 1, c)

    for t in range(ticks):
        if gated[t]:
            for copy in table_copies(t):
                copy.wait_send()
        for c in range(chunks):
            if gated[t]:

                @pl.when(is_gate)
                def _():
                    for j in range(mid):
                        f_copy(t, c, j).wait_send()

            if t > 0:

                @pl.when(jnp.logical_not(has_prev))
                def _():
                    far(lambda d: x_copy(t, t, c, s, d).wait_send())
                    near(lambda d: x_copy(t, t, c, s, d).wait_send())

            if t < ticks - 1:

                @pl.when(has_next)
                def _():
                    far(lambda d: x_copy(ticks + t, t + 1, c, following, d).wait_send())
                    near(lambda d: x_copy(ticks + t, t + 1, c, following, d).wait_send(), True)
                    raw_copy(t, c).wait_send()

            out_copy(t, c).wait()

    @pl.when(has_prev)
    def _():
        for t in range(ticks - 1):
            sel_copy(t).wait_send()


def solution(mesh):
    n = mesh.shape["expert"]
    sections = mesh.shape["section"]

    def shards(acts, incoming, routes, route_weight, norm_gain, w_gate, w_up, w_down):
        ticks, _, tokens, top = routes.shape
        width, hidden = w_gate.shape[1:]
        chunks = 5 if width % (5 * 128) == 0 else 4
        cols = width // chunks
        cap = min(CAP, tokens)
        mid, moves = n // 2, max(ticks - 1, 1)
        half, single = jnp.bfloat16, jnp.float32
        anywhere = pl.BlockSpec(memory_space=pl.ANY)
        vmem = pl.BlockSpec(memory_space=pltpu.VMEM)
        dma = pltpu.SemaphoreType.DMA
        result = pl.pallas_call(
            functools.partial(kernel, n, sections),
            out_shape=jax.ShapeDtypeStruct((ticks, tokens, width), half),
            in_specs=[anywhere, anywhere, vmem, vmem, vmem, anywhere, anywhere, anywhere],
            out_specs=anywhere,
            scratch_shapes=[
                pltpu.VMEM((width, hidden), half),
                pltpu.VMEM((width, hidden), half),
                pltpu.VMEM((hidden, width), half),
                pltpu.VMEM((ticks, chunks, tokens, cols), half),
                pltpu.VMEM((ticks, chunks, tokens, cols), half),
                pltpu.VMEM((2 * ticks - 1, chunks, EXPERTS, cap, cols), half),
                pltpu.VMEM((ticks, chunks, n, cap, cols), half),
                pltpu.VMEM((ticks, chunks, n, cap, cols), half),
                pltpu.VMEM((ticks, chunks, n, cap, cols), half),
                pltpu.VMEM((ticks, chunks, mid, mid, cap, cols), half),
                pltpu.VMEM((ticks, chunks, mid, tokens, cols), half),
                pltpu.VMEM((ticks, chunks, tokens, cols), half),
                pltpu.VMEM((ticks, EXPERTS * cap, tokens), half),
                pltpu.VMEM((moves, EXPERTS * cap, tokens), half),
                pltpu.VMEM((ticks, 2, top * tokens, mid * cap), half),
                pltpu.VMEM((ticks, mid, top * tokens, mid * cap), half),
                pltpu.VMEM((ticks, 8, 128), single),
                pltpu.VMEM((ticks, mid, 8, 128), single),
                dma((3, chunks)),
                dma((ticks, chunks)),
                dma((ticks, chunks)),
                dma((2, ticks)),
                dma((2, ticks, mid)),
                dma((moves,)),
                dma((moves,)),
                dma((moves, chunks)),
                dma((moves, chunks)),
                dma((2 * ticks - 1, chunks, n)),
                dma((ticks, chunks, n)),
                dma((ticks, chunks, n)),
                dma((ticks, chunks, n)),
                dma((ticks, chunks)),
                dma((ticks, chunks, mid)),
                dma((ticks, chunks, mid)),
                dma((ticks, chunks)),
                pltpu.SemaphoreType.REGULAR,
            ],
            compiler_params=pltpu.CompilerParams(
                collective_id=0, has_side_effects=True, vmem_limit_bytes=60 << 20
            ),
        )(
            acts[0],
            incoming,
            jnp.swapaxes(routes, 2, 3),
            jnp.swapaxes(route_weight, 2, 3),
            norm_gain,
            w_gate[0],
            w_up[0],
            w_down[0],
        )
        return result[:, None]

    return jax.shard_map(
        shards,
        mesh=mesh,
        in_specs=(
            P("section", "expert", None),
            P(None, "expert", None),
            P(None, "section", "expert", None),
            P(None, "section", "expert", None),
            P("section", None),
            P("section", None, "expert"),
            P("section", None, "expert"),
            P("section", "expert", None),
        ),
        out_specs=P(None, "section", "expert", None),
        check_vma=False,
    )
```

```python
import functools

import jax
import jax.numpy as jnp
from jax import lax
from jax.experimental import pallas as pl
from jax.experimental.pallas import tpu as pltpu
from jax.sharding import PartitionSpec as P

MESH = pl.DeviceIdType.MESH
EXPERTS = 4
CAP = 24


def kernel(
    n,
    sections,
    acts,
    incoming,
    routes,
    route_weight,
    gain,
    w_gate_hbm,
    w_up_hbm,
    w_down_hbm,
    out,
    w_gate,
    w_up,
    w_down,
    xown,
    made,
    xsend,
    xraw,
    xrelay,
    xrecv,
    psend,
    precv,
    pgate,
    fsend,
    frecv,
    sel,
    sel_in,
    sel_far,
    pick,
    pick_far,
    rate,
    rate_far,
    w_sem,
    out_sem,
    own_sem,
    table_send,
    table_recv,
    sel_send,
    sel_recv,
    raw_send,
    raw_recv,
    far_send,
    far_recv,
    x_send,
    x_recv,
    relay_send,
    p_send,
    p_recv,
    gate_send,
    gate_recv,
    f_send,
    f_recv,
    turn,
):
    s = lax.axis_index("section")
    e = lax.axis_index("expert")
    ticks, chunks, tokens, cols = xown.shape
    top = routes.shape[2]
    cap = xrecv.shape[3]
    group = n // EXPERTS
    mid = n // 2
    sided = EXPERTS // 2
    gated = [t < ticks - 1 for t in range(ticks)]
    early = max(chunks - 2, 1)
    width = chunks * cols
    rows = n * cap
    side = e // mid
    base, far_base = side * mid, (1 - side) * mid
    own = e - base
    near_gate = jnp.where(side == 0, mid - 1, mid)
    far_gate = jnp.where(side == 0, mid, mid - 1)
    is_gate = e == near_gate
    not_gate = e != near_gate
    has_next = s < sections - 1
    has_prev = s > 0
    following = jnp.minimum(s + 1, sections - 1)
    previous = jnp.maximum(s - 1, 0)
    half = jnp.bfloat16
    single = jnp.float32

    def remote(source, target, send, recv, section, device):
        return pltpu.make_async_remote_copy(
            source, target, send, recv, device_id=(section, device), device_id_type=MESH
        )

    def near(body, own_too=False):
        def step(i, _):
            body(base + lax.rem(own + i, mid))
            return 0

        lax.fori_loop(0 if own_too else 1, mid, step, 0)

    def far(body):
        def step(i, _):
            body(far_base + i)
            return 0

        lax.fori_loop(0, mid, step, 0)

    def sent(source, send):
        remote(source, source, send, send, s, far_gate).wait_send()

    def landed(target, recv):
        remote(target, target, recv, recv, s, far_gate).wait_recv()

    def own_copy(t, c):
        source = acts if t == 0 else incoming.at[t - 1]
        return pltpu.make_async_copy(
            source.at[:, pl.ds(c * cols, cols)],
            xown.at[t, c],
            own_sem.at[c if t == 0 else chunks + t - 1],
        )

    def gate_copy(c):
        span = pl.ds(c * cols, cols)
        return (
            pltpu.make_async_copy(w_gate_hbm.at[span], w_gate.at[span], w_sem.at[0, c]),
            pltpu.make_async_copy(w_up_hbm.at[span], w_up.at[span], w_sem.at[1, c]),
        )

    down_copy = pltpu.make_async_copy(w_down_hbm, w_down, w_sem.at[2, 0])

    def table_copies(t):
        pairs = ((sel.at[t, 1 - side], sel_far), (pick.at[t, 1 - side], pick_far), (rate.at[t], rate_far))
        return [
            remote(
                source, target.at[t, own], table_send.at[i, t], table_recv.at[i, t], s, far_gate
            )
            for i, (source, target) in enumerate(pairs)
        ][: 3 if gated[t] else 1]

    def table_arrival(i, t):
        landed((sel_far, pick_far, rate_far)[i].at[t], table_recv.at[i, t])

    def sel_copy(t):
        return remote(
            sel.at[t + 1, side], sel_in.at[t], sel_send.at[t], sel_recv.at[t], previous, e
        )

    def raw_copy(t, c):
        return remote(
            made.at[t, c], xown.at[t + 1, c], raw_send.at[t], raw_recv.at[t], following, e
        )

    def bank(slot, c):
        return slot if slot > 0 or c < early else 2 * ticks - 1

    def far_copy(slot, t, c, section, source):
        return remote(
            source, xraw.at[t, c, own], far_send.at[bank(slot, c)], far_recv.at[t, c], section, far_gate
        )

    def x_copy(slot, t, c, section, d):
        return remote(
            xsend.at[slot, c, d // group - side * sided],
            xrecv.at[t, c, e],
            x_send.at[bank(slot, c)],
            x_recv.at[t, c],
            section,
            d,
        )

    def dispatched(slot, first, last, peers):
        span = pl.ds(first, last - first)
        sent(xown.at[0, span], far_send.at[bank(slot, first)])
        if peers:
            sent(xrecv.at[0, span, pl.ds(0, peers)], x_send.at[bank(slot, first)])

    def relay_copy(t, c, j, d):
        return remote(
            xrelay.at[t, c, j, d // group - side * sided],
            xrecv.at[t, c, far_base + j],
            relay_send.at[t, j],
            x_recv.at[t, c],
            s,
            d,
        )

    def p_copy(t, c, d):
        return remote(
            psend.at[t, c, d], precv.at[t, c, e], p_send.at[t], p_recv.at[t, c], s, d
        )

    def gate_send_copy(t, c):
        return remote(
            psend.at[t, c, pl.ds(far_base, mid)],
            pgate.at[t, c, own],
            gate_send.at[t],
            gate_recv.at[t, c],
            s,
            near_gate,
        )

    def f_copy(t, c, j):
        return remote(
            fsend.at[t, c, j], frecv.at[t, c], f_send.at[t], f_recv.at[t, c], s, far_base + j
        )

    def out_copy(t, c):
        return pltpu.make_async_copy(
            made.at[t, c], out.at[t, :, pl.ds(c * cols, cols)], out_sem.at[0]
        )

    for c in range(chunks):
        own_copy(0, c).start()

    barrier = pltpu.get_barrier_semaphore()

    def greet(d, _):
        @pl.when(d != e)
        def _():
            pl.semaphore_signal(barrier, inc=1, device_id=(s, d), device_id_type=MESH)

        return 0

    lax.fori_loop(0, n, greet, 0)
    for there, section in ((has_next, following), (has_prev, previous)):

        @pl.when(there)
        def _():
            pl.semaphore_signal(barrier, inc=1, device_id=(section, e), device_id_type=MESH)

    for c in range(chunks):
        for copy in gate_copy(c):
            copy.start()
    down_copy.start()

    @pl.when(jnp.logical_not(has_prev))
    def _():
        for t in range(1, ticks):
            for c in range(chunks):
                own_copy(t, c).start()

    def iota(shape, axis):
        return lax.broadcasted_iota(jnp.int32, shape, axis)

    before = (iota((tokens, tokens), 0) < iota((tokens, tokens), 1)).astype(half)
    diagonal = iota((tokens, tokens), 0) == iota((tokens, tokens), 1)
    place = iota((cap, tokens), 0).astype(single)
    for t in range(ticks):
        chosen = routes[t, 0]
        hot = sum(
            (iota((EXPERTS, tokens), 0) == chosen[k : k + 1]).astype(single) for k in range(top)
        )
        rank = jnp.dot(hot.astype(half), before, preferred_element_type=single)
        blocks = [
            [
                (place == jnp.where(chosen[k : k + 1] == x, rank[x : x + 1], -1.0)).astype(single)
                for x in range(EXPERTS)
            ]
            for k in range(top)
        ]
        for h in range(2):
            experts = range(h * sided, (h + 1) * sided)
            sel[t, h] = sum(
                jnp.concatenate([blocks[k][x] for x in experts], axis=0) for k in range(top)
            ).astype(half)
            for k in range(top):
                spread = jnp.concatenate(
                    [blocks[k][x] for x in experts for _ in range(group)], axis=0
                )
                pick[t, h, k * tokens : (k + 1) * tokens, :] = lax.dot_general(
                    diagonal.astype(half),
                    spread.astype(half),
                    (((1,), (1,)), ((), ())),
                    preferred_element_type=single,
                ).astype(half)
        rate[t] = jnp.zeros_like(rate[t])
        rate[t, 0:top, 0:tokens] = route_weight[t, 0]

    pl.semaphore_wait(
        barrier, n - 1 + jnp.where(has_next, 1, 0) + jnp.where(has_prev, 1, 0)
    )

    def pack(target, table, value):
        packed = jnp.dot(table, value, preferred_element_type=single)
        for x in range(sided):
            target[x] = packed[x * cap : (x + 1) * cap].astype(half)

    def landed_own(t):
        pltpu.make_async_copy(xown.at[t], xown.at[t], own_sem.at[chunks + t - 1]).wait()

    def dispatch(t, c):
        if t == 0:
            own_copy(t, c).wait()
        far_copy(t, t, c, s, xown.at[t, c]).start()
        pack(xsend.at[t, c], sel[t, side], xown[t, c])
        near(lambda d: x_copy(t, t, c, s, d).start())
        xrecv[t, c, e] = xsend[t, c, e // group - side * sided]

    paired = sections % 2 == 0
    leads = lax.rem(s, 2) == 0
    table_copies(0)[0].start()
    if paired:

        @pl.when(jnp.logical_not(leads))
        def _():
            pl.semaphore_wait(turn, 1)

    for c in range(chunks):
        dispatch(0, c)
    for t in range(ticks):
        for copy in table_copies(t)[1 if t == 0 else 0 :]:
            copy.start()

    @pl.when(has_prev)
    def _():
        for t in range(ticks - 1):
            sel_copy(t).start()

    dispatched(0, 0, early, mid - 1)
    if paired:

        @pl.when(leads)
        def _():
            pl.semaphore_signal(turn, inc=1, device_id=(following, e), device_id_type=MESH)

    def relay(t, c):
        if c == 0:
            table_arrival(0, t)
        landed(xraw.at[t, c], far_recv.at[t, c])
        for j in range(mid):
            pack(xrelay.at[t, c, j], sel_far[t, j], xraw[t, c, j])
            near(lambda d: relay_copy(t, c, j, d).start())
            xrecv[t, c, far_base + j] = xrelay[t, c, j, e // group - side * sided]

    def combine(t, c):
        if c == 0:
            table_arrival(1, t)
            table_arrival(2, t)
        if mid > 1:
            landed(pgate.at[t, c, pl.ds(0, mid - 1)], gate_recv.at[t, c])
        for j in range(mid):
            value = jnp.concatenate(
                [pgate[t, c, d, j].astype(single) for d in range(mid)], axis=0
            ).astype(half)
            back = jnp.dot(pick_far[t, j], value, preferred_element_type=single)
            total = None
            for k in range(top):
                part = back[k * tokens : (k + 1) * tokens] * column(rate_far[t, j], k)
                total = part if total is None else total + part
            fsend[t, c, j] = total.astype(half)
            f_copy(t, c, j).start()

    def column(table, k):
        return jnp.sum(
            jnp.where(diagonal, table[k : k + 1, 0:tokens], 0.0), axis=1, keepdims=True
        )

    for t in range(ticks):
        gate_val = up_val = None
        squares = jnp.zeros((rows, 1), single)
        for c in range(chunks):

            @pl.when(jnp.logical_and(is_gate, leads) if paired and t > 0 else is_gate)
            def _():
                relay(t, c)

            for packed, there in ((0, is_gate), (mid, not_gate)):
                if t == 0:
                    cases = ((mid - 1, there),)
                else:
                    cases = (
                        (mid, jnp.logical_and(there, has_prev)),
                        (mid - 1, jnp.logical_and(there, jnp.logical_not(has_prev))),
                    )
                for number, case in cases:
                    if packed + number:

                        @pl.when(case)
                        def _():
                            landed(xrecv.at[t, c, pl.ds(0, packed + number)], x_recv.at[t, c])

            if t == 0:
                for copy in gate_copy(c):
                    copy.wait()
            span = pl.ds(c * cols, cols)
            value = jnp.concatenate([xrecv[t, c, d].astype(single) for d in range(n)], axis=0)
            squares = squares + jnp.sum(value * value, axis=1, keepdims=True)
            normed = (value * gain[:, span]).astype(half)
            gate_part = jnp.dot(normed, w_gate[span, :], preferred_element_type=single)
            up_part = jnp.dot(normed, w_up[span, :], preferred_element_type=single)
            gate_val = gate_part if gate_val is None else gate_val + gate_part
            up_val = up_part if up_val is None else up_val + up_part
        scale = lax.rsqrt(squares * (1.0 / width) + 1e-06)
        hidden = (jax.nn.silu(gate_val * scale) * (up_val * scale)).astype(half)
        if t == 0:
            down_copy.wait()
        for c in range(chunks):
            span = pl.ds(c * cols, cols)
            value = jnp.dot(hidden, w_down[:, span], preferred_element_type=single)
            for d in range(n):
                psend[t, c, d] = value[d * cap : (d + 1) * cap].astype(half)
            if gated[t]:

                @pl.when(not_gate)
                def _():
                    gate_send_copy(t, c).start()

                @pl.when(is_gate)
                def _():
                    pgate[t, c, own] = psend[t, c, pl.ds(far_base, mid)]

            else:
                far(lambda d: p_copy(t, c, d).start())
            near(lambda d: p_copy(t, c, d).start())
            precv[t, c, e] = psend[t, c, e]

        if gated[t]:

            @pl.when(is_gate)
            def _():
                for c in range(chunks):
                    combine(t, c)

        if gated[t]:

            @pl.when(not_gate)
            def _():
                sent(psend.at[t, :, pl.ds(0, mid)], gate_send.at[t])

            peers = mid - 1
        else:
            peers = n - 1
        if peers:
            sent(psend.at[t, :, pl.ds(0, peers)], p_send.at[t])

        if t < ticks - 1:
            if paired:

                @pl.when(s == 1)
                def _():
                    pl.semaphore_signal(turn, inc=1, device_id=(previous, e), device_id_type=MESH)

                @pl.when(jnp.logical_and(is_gate, jnp.logical_not(leads)))
                def _():
                    for c in range(chunks):
                        relay(t + 1, c)

            @pl.when(has_next)
            def _():
                landed(sel_in.at[t], sel_recv.at[t])

        if t > 0:

            @pl.when(has_prev)
            def _():
                landed(xown.at[t], raw_recv.at[t - 1])

        weights = [column(rate[t], k) for k in range(top)]
        for c in range(chunks):
            layer = xown[t, c].astype(single)
            if gated[t]:
                landed(frecv.at[t, c], f_recv.at[t, c])
                layer = layer + frecv[t, c].astype(single)
                sources, table = [base + j for j in range(mid)], pick[t, side]
            else:
                sources = list(range(n))
                table = jnp.concatenate([pick[t, 0], pick[t, 1]], axis=1)
            if peers:
                landed(precv.at[t, c, pl.ds(0, peers)], p_recv.at[t, c])
            value = jnp.concatenate(
                [precv[t, c, d].astype(single) for d in sources], axis=0
            ).astype(half)
            back = jnp.dot(table, value, preferred_element_type=single)
            for k in range(top):
                layer = layer + back[k * tokens : (k + 1) * tokens] * weights[k]
            layer = layer.astype(half)
            made[t, c] = layer
            out_copy(t, c).start()
            if t < ticks - 1:

                @pl.when(has_next)
                def _():
                    far_copy(ticks + t, t + 1, c, following, made.at[t, c]).start()
                    pack(xsend.at[ticks + t, c], sel_in[t], layer)
                    near(lambda d: x_copy(ticks + t, t + 1, c, following, d).start(), True)
                    raw_copy(t, c).start()

        if t < ticks - 1:

            @pl.when(jnp.logical_not(has_prev))
            def _():
                if paired:
                    pl.semaphore_wait(turn, 1)
                landed_own(t + 1)
                for c in range(chunks):
                    dispatch(t + 1, c)

    dispatched(0, early, chunks, mid - 1)
    for t in range(ticks):
        for copy in table_copies(t):
            copy.wait_send()

        @pl.when(is_gate)
        def _():
            if mid > 1:
                for j in range(mid):
                    sent(xrecv.at[t, :, pl.ds(0, mid - 1)], relay_send.at[t, j])
            if gated[t]:
                sent(fsend.at[t], f_send.at[t])

        if t > 0:

            @pl.when(jnp.logical_not(has_prev))
            def _():
                dispatched(t, 0, chunks, mid - 1)

        if t < ticks - 1:

            @pl.when(has_next)
            def _():
                dispatched(ticks + t, 0, chunks, mid)
                sent(made.at[t], raw_send.at[t])

    pltpu.make_async_copy(made, made, out_sem.at[0]).wait()

    @pl.when(has_prev)
    def _():
        for t in range(ticks - 1):
            sel_copy(t).wait_send()


def solution(mesh):
    n = mesh.shape["expert"]
    sections = mesh.shape["section"]

    def shards(acts, incoming, routes, route_weight, norm_gain, w_gate, w_up, w_down):
        ticks, _, tokens, top = routes.shape
        width, hidden = w_gate.shape[1:]
        chunks = 5 if width % (5 * 128) == 0 else 4
        cols = width // chunks
        cap = min(CAP, tokens)
        mid, sided, moves = n // 2, EXPERTS // 2, max(ticks - 1, 1)
        half, single = jnp.bfloat16, jnp.float32
        anywhere = pl.BlockSpec(memory_space=pl.ANY)
        vmem = pl.BlockSpec(memory_space=pltpu.VMEM)
        dma = pltpu.SemaphoreType.DMA
        result = pl.pallas_call(
            functools.partial(kernel, n, sections),
            out_shape=jax.ShapeDtypeStruct((ticks, tokens, width), half),
            in_specs=[anywhere, anywhere, vmem, vmem, vmem, anywhere, anywhere, anywhere],
            out_specs=anywhere,
            scratch_shapes=[
                pltpu.VMEM((width, hidden), half),
                pltpu.VMEM((width, hidden), half),
                pltpu.VMEM((hidden, width), half),
                pltpu.VMEM((ticks, chunks, tokens, cols), half),
                pltpu.VMEM((ticks, chunks, tokens, cols), half),
                pltpu.VMEM((2 * ticks - 1, chunks, sided, cap, cols), half),
                pltpu.VMEM((ticks, chunks, mid, tokens, cols), half),
                pltpu.VMEM((ticks, chunks, mid, sided, cap, cols), half),
                pltpu.VMEM((ticks, chunks, n, cap, cols), half),
                pltpu.VMEM((ticks, chunks, n, cap, cols), half),
                pltpu.VMEM((ticks, chunks, n, cap, cols), half),
                pltpu.VMEM((moves, chunks, mid, mid, cap, cols), half),
                pltpu.VMEM((moves, chunks, mid, tokens, cols), half),
                pltpu.VMEM((moves, chunks, tokens, cols), half),
                pltpu.VMEM((ticks, 2, sided * cap, tokens), half),
                pltpu.VMEM((moves, sided * cap, tokens), half),
                pltpu.VMEM((ticks, mid, sided * cap, tokens), half),
                pltpu.VMEM((ticks, 2, top * tokens, mid * cap), half),
                pltpu.VMEM((ticks, mid, top * tokens, mid * cap), half),
                pltpu.VMEM((ticks, 8, 128), single),
                pltpu.VMEM((ticks, mid, 8, 128), single),
                dma((3, chunks)),
                dma((1,)),
                dma((chunks + moves,)),
                dma((3, ticks)),
                dma((3, ticks)),
                dma((moves,)),
                dma((moves,)),
                dma((moves,)),
                dma((moves,)),
                dma((2 * ticks,)),
                dma((ticks, chunks)),
                dma((2 * ticks,)),
                dma((ticks, chunks)),
                dma((ticks, mid)),
                dma((ticks,)),
                dma((ticks, chunks)),
                dma((moves,)),
                dma((moves, chunks)),
                dma((moves,)),
                dma((moves, chunks)),
                pltpu.SemaphoreType.REGULAR,
            ],
            compiler_params=pltpu.CompilerParams(
                collective_id=0, has_side_effects=True, vmem_limit_bytes=60 << 20
            ),
        )(
            acts[0],
            incoming,
            jnp.swapaxes(routes, 2, 3),
            jnp.swapaxes(route_weight, 2, 3),
            norm_gain,
            w_gate[0],
            w_up[0],
            w_down[0],
        )
        return result[:, None]

    return jax.shard_map(
        shards,
        mesh=mesh,
        in_specs=(
            P("section", "expert", None),
            P(None, "expert", None),
            P(None, "section", "expert", None),
            P(None, "section", "expert", None),
            P("section", None),
            P("section", None, "expert"),
            P("section", None, "expert"),
            P("section", "expert", None),
        ),
        out_specs=P(None, "section", "expert", None),
        check_vma=False,
    )
```

```python
import functools

import jax
import jax.numpy as jnp
from jax import lax
from jax.experimental import pallas as pl
from jax.experimental.pallas import tpu as pltpu
from jax.sharding import PartitionSpec as P

MESH = pl.DeviceIdType.MESH
EXPERTS = 4
CAP = 24


def kernel(
    n,
    sections,
    acts,
    incoming,
    routes_hbm,
    route_weight_hbm,
    gain_hbm,
    w_gate_hbm,
    w_up_hbm,
    w_down_hbm,
    out,
    routes,
    route_weight,
    gain,
    w_gate,
    w_up,
    w_down,
    xown,
    made,
    xsend,
    xraw,
    xrelay,
    xrecv,
    psend,
    precv,
    pgate,
    fsend,
    frecv,
    sel,
    sel_in,
    sel_far,
    pick,
    pick_far,
    rate,
    rate_far,
    small_sem,
    w_sem,
    out_sem,
    own_sem,
    table_send,
    table_recv,
    sel_send,
    sel_recv,
    raw_send,
    raw_recv,
    far_send,
    far_recv,
    x_send,
    x_recv,
    relay_send,
    p_send,
    p_recv,
    gate_send,
    gate_recv,
    f_send,
    f_recv,
    turn,
):
    s = lax.axis_index("section")
    e = lax.axis_index("expert")
    ticks, chunks, tokens, cols = xown.shape
    top = routes.shape[2]
    cap = xrecv.shape[3]
    group = n // EXPERTS
    mid = n // 2
    sided = EXPERTS // 2
    gated = [t < ticks - 1 for t in range(ticks)]
    early = max(chunks - 2, 1)
    width = chunks * cols
    rows = n * cap
    side = e // mid
    base, far_base = side * mid, (1 - side) * mid
    own = e - base
    near_gate = jnp.where(side == 0, mid - 1, mid)
    far_gate = jnp.where(side == 0, mid, mid - 1)
    is_gate = e == near_gate
    not_gate = e != near_gate
    has_next = s < sections - 1
    has_prev = s > 0
    following = jnp.minimum(s + 1, sections - 1)
    previous = jnp.maximum(s - 1, 0)
    half = jnp.bfloat16
    single = jnp.float32

    def remote(source, target, send, recv, section, device):
        return pltpu.make_async_remote_copy(
            source, target, send, recv, device_id=(section, device), device_id_type=MESH
        )

    def near(body, own_too=False):
        def step(i, _):
            body(base + lax.rem(own + i, mid))
            return 0

        lax.fori_loop(0 if own_too else 1, mid, step, 0)

    def far(body):
        def step(i, _):
            body(far_base + i)
            return 0

        lax.fori_loop(0, mid, step, 0)

    def sent(source, send):
        remote(source, source, send, send, s, far_gate).wait_send()

    def landed(target, recv):
        remote(target, target, recv, recv, s, far_gate).wait_recv()

    def own_copy(t, c):
        source = acts if t == 0 else incoming.at[t - 1]
        return pltpu.make_async_copy(
            source.at[:, pl.ds(c * cols, cols)],
            xown.at[t, c],
            own_sem.at[c if t == 0 else chunks + t - 1],
        )

    def gate_copy(c):
        span = pl.ds(c * cols, cols)
        return (
            pltpu.make_async_copy(w_gate_hbm.at[span], w_gate.at[span], w_sem.at[0, c]),
            pltpu.make_async_copy(w_up_hbm.at[span], w_up.at[span], w_sem.at[1, c]),
        )

    down_copy = pltpu.make_async_copy(w_down_hbm, w_down, w_sem.at[2, 0])

    def table_copies(t):
        pairs = ((sel.at[t, 1 - side], sel_far), (pick.at[t, 1 - side], pick_far), (rate.at[t], rate_far))
        return [
            remote(
                source, target.at[t, own], table_send.at[i, t], table_recv.at[i, t], s, far_gate
            )
            for i, (source, target) in enumerate(pairs)
        ][: 3 if gated[t] else 1]

    def table_arrival(i, t):
        landed((sel_far, pick_far, rate_far)[i].at[t], table_recv.at[i, t])

    def sel_copy(t):
        return remote(
            sel.at[t + 1, side], sel_in.at[t], sel_send.at[t], sel_recv.at[t], previous, e
        )

    def raw_copy(t, c):
        return remote(
            made.at[t, c], xown.at[t + 1, c], raw_send.at[t], raw_recv.at[t], following, e
        )

    def bank(slot, c):
        return slot if slot > 0 or c < early else 2 * ticks - 1

    def far_copy(slot, t, c, section, source):
        return remote(
            source, xraw.at[t, c, own], far_send.at[bank(slot, c)], far_recv.at[t, c], section, far_gate
        )

    def x_copy(slot, t, c, section, d):
        return remote(
            xsend.at[slot, c, d // group - side * sided],
            xrecv.at[t, c, e],
            x_send.at[bank(slot, c)],
            x_recv.at[t, c],
            section,
            d,
        )

    def dispatched(slot, first, last, peers):
        span = pl.ds(first, last - first)
        sent(xown.at[0, span], far_send.at[bank(slot, first)])
        if peers:
            sent(xrecv.at[0, span, pl.ds(0, peers)], x_send.at[bank(slot, first)])

    def relay_copy(t, c, j, d):
        return remote(
            xrelay.at[t, c, j, d // group - side * sided],
            xrecv.at[t, c, far_base + j],
            relay_send.at[t, j],
            x_recv.at[t, c],
            s,
            d,
        )

    def p_copy(t, c, d):
        return remote(
            psend.at[t, c, d], precv.at[t, c, e], p_send.at[t], p_recv.at[t, c], s, d
        )

    def gate_send_copy(t, c):
        return remote(
            psend.at[t, c, pl.ds(far_base, mid)],
            pgate.at[t, c, own],
            gate_send.at[t],
            gate_recv.at[t, c],
            s,
            near_gate,
        )

    def f_copy(t, c, j):
        return remote(
            fsend.at[t, c, j], frecv.at[t, c], f_send.at[t], f_recv.at[t, c], s, far_base + j
        )

    def out_copy(t, c):
        return pltpu.make_async_copy(
            made.at[t, c], out.at[t, :, pl.ds(c * cols, cols)], out_sem.at[0]
        )

    small = [
        pltpu.make_async_copy(source, target, small_sem.at[i])
        for i, (source, target) in enumerate(
            ((routes_hbm, routes), (route_weight_hbm, route_weight), (gain_hbm, gain))
        )
    ]
    for copy in small:
        copy.start()
    for c in range(chunks):
        own_copy(0, c).start()

    barrier = pltpu.get_barrier_semaphore()

    def greet(d, _):
        @pl.when(d != e)
        def _():
            pl.semaphore_signal(barrier, inc=1, device_id=(s, d), device_id_type=MESH)

        return 0

    lax.fori_loop(0, n, greet, 0)
    for there, section in ((has_next, following), (has_prev, previous)):

        @pl.when(there)
        def _():
            pl.semaphore_signal(barrier, inc=1, device_id=(section, e), device_id_type=MESH)

    for c in range(chunks):
        for copy in gate_copy(c):
            copy.start()
    down_copy.start()

    @pl.when(jnp.logical_not(has_prev))
    def _():
        for t in range(1, ticks):
            for c in range(chunks):
                own_copy(t, c).start()

    for copy in small:
        copy.wait()

    def iota(shape, axis):
        return lax.broadcasted_iota(jnp.int32, shape, axis)

    before = (iota((tokens, tokens), 0) < iota((tokens, tokens), 1)).astype(half)
    diagonal = iota((tokens, tokens), 0) == iota((tokens, tokens), 1)
    place = iota((cap, tokens), 0).astype(single)
    for t in range(ticks):
        chosen = routes[t, 0]
        hot = sum(
            (iota((EXPERTS, tokens), 0) == chosen[k : k + 1]).astype(single) for k in range(top)
        )
        rank = jnp.dot(hot.astype(half), before, preferred_element_type=single)
        blocks = [
            [
                (place == jnp.where(chosen[k : k + 1] == x, rank[x : x + 1], -1.0)).astype(single)
                for x in range(EXPERTS)
            ]
            for k in range(top)
        ]
        for h in range(2):
            experts = range(h * sided, (h + 1) * sided)
            sel[t, h] = sum(
                jnp.concatenate([blocks[k][x] for x in experts], axis=0) for k in range(top)
            ).astype(half)
            for k in range(top):
                spread = jnp.concatenate(
                    [blocks[k][x] for x in experts for _ in range(group)], axis=0
                )
                pick[t, h, k * tokens : (k + 1) * tokens, :] = lax.dot_general(
                    diagonal.astype(half),
                    spread.astype(half),
                    (((1,), (1,)), ((), ())),
                    preferred_element_type=single,
                ).astype(half)
        rate[t] = jnp.zeros_like(rate[t])
        rate[t, 0:top, 0:tokens] = route_weight[t, 0]

    pl.semaphore_wait(
        barrier, n - 1 + jnp.where(has_next, 1, 0) + jnp.where(has_prev, 1, 0)
    )

    def pack(target, table, value):
        packed = jnp.dot(table, value, preferred_element_type=single)
        for x in range(sided):
            target[x] = packed[x * cap : (x + 1) * cap].astype(half)

    def landed_own(t):
        pltpu.make_async_copy(xown.at[t], xown.at[t], own_sem.at[chunks + t - 1]).wait()

    def dispatch(t, c):
        if t == 0:
            own_copy(t, c).wait()
        far_copy(t, t, c, s, xown.at[t, c]).start()
        pack(xsend.at[t, c], sel[t, side], xown[t, c])
        near(lambda d: x_copy(t, t, c, s, d).start())
        xrecv[t, c, e] = xsend[t, c, e // group - side * sided]

    paired = sections % 2 == 0
    leads = lax.rem(s, 2) == 0
    held = leads if paired else s < 0
    table_copies(0)[0].start()
    if paired:

        @pl.when(jnp.logical_not(leads))
        def _():
            pl.semaphore_wait(turn, 1)

    for c in range(chunks):
        dispatch(0, c)
    for t in range(ticks):
        for copy in table_copies(t)[1 if t == 0 else 0 :]:
            copy.start()

    @pl.when(has_prev)
    def _():
        for t in range(ticks - 1):
            sel_copy(t).start()

    dispatched(0, 0, early, mid - 1)
    if paired:

        @pl.when(leads)
        def _():
            pl.semaphore_signal(turn, inc=1, device_id=(following, e), device_id_type=MESH)

    def relay(t, c):
        if c == 0:
            table_arrival(0, t)
        landed(xraw.at[t, c], far_recv.at[t, c])
        for j in range(mid):
            pack(xrelay.at[t, c, j], sel_far[t, j], xraw[t, c, j])
            near(lambda d: relay_copy(t, c, j, d).start())
            xrecv[t, c, far_base + j] = xrelay[t, c, j, e // group - side * sided]

    def combine(t, c):
        if c == 0:
            table_arrival(1, t)
            table_arrival(2, t)
        if mid > 1:
            landed(pgate.at[t, c, pl.ds(0, mid - 1)], gate_recv.at[t, c])
        for j in range(mid):
            value = jnp.concatenate(
                [pgate[t, c, d, j].astype(single) for d in range(mid)], axis=0
            ).astype(half)
            back = jnp.dot(pick_far[t, j], value, preferred_element_type=single)
            total = None
            for k in range(top):
                part = back[k * tokens : (k + 1) * tokens] * column(rate_far[t, j], k)
                total = part if total is None else total + part
            fsend[t, c, j] = total.astype(half)
            f_copy(t, c, j).start()

    def forward(t, c):
        far_copy(ticks + t, t + 1, c, following, made.at[t, c]).start()
        pack(xsend.at[ticks + t, c], sel_in[t], made[t, c])
        near(lambda d: x_copy(ticks + t, t + 1, c, following, d).start(), True)
        raw_copy(t, c).start()

    def column(table, k):
        return jnp.sum(
            jnp.where(diagonal, table[k : k + 1, 0:tokens], 0.0), axis=1, keepdims=True
        )

    for t in range(ticks):
        gate_val = up_val = None
        squares = jnp.zeros((rows, 1), single)
        for c in range(chunks):

            @pl.when(is_gate)
            def _():
                relay(t, c)

            for packed, there in ((0, is_gate), (mid, not_gate)):
                if t == 0:
                    cases = ((mid - 1, there),)
                else:
                    cases = (
                        (mid, jnp.logical_and(there, has_prev)),
                        (mid - 1, jnp.logical_and(there, jnp.logical_not(has_prev))),
                    )
                for number, case in cases:
                    if packed + number:

                        @pl.when(case)
                        def _():
                            landed(xrecv.at[t, c, pl.ds(0, packed + number)], x_recv.at[t, c])

            if t == 0:
                for copy in gate_copy(c):
                    copy.wait()
            span = pl.ds(c * cols, cols)
            value = jnp.concatenate([xrecv[t, c, d].astype(single) for d in range(n)], axis=0)
            squares = squares + jnp.sum(value * value, axis=1, keepdims=True)
            normed = (value * gain[:, span]).astype(half)
            gate_part = jnp.dot(normed, w_gate[span, :], preferred_element_type=single)
            up_part = jnp.dot(normed, w_up[span, :], preferred_element_type=single)
            gate_val = gate_part if gate_val is None else gate_val + gate_part
            up_val = up_part if up_val is None else up_val + up_part
        scale = lax.rsqrt(squares * (1.0 / width) + 1e-06)
        hidden = (jax.nn.silu(gate_val * scale) * (up_val * scale)).astype(half)
        if t == 0:
            down_copy.wait()
        for c in range(chunks):
            span = pl.ds(c * cols, cols)
            value = jnp.dot(hidden, w_down[:, span], preferred_element_type=single)
            for d in range(n):
                psend[t, c, d] = value[d * cap : (d + 1) * cap].astype(half)
            if gated[t]:

                @pl.when(not_gate)
                def _():
                    gate_send_copy(t, c).start()

                @pl.when(is_gate)
                def _():
                    pgate[t, c, own] = psend[t, c, pl.ds(far_base, mid)]

            else:
                far(lambda d: p_copy(t, c, d).start())
            near(lambda d: p_copy(t, c, d).start())
            precv[t, c, e] = psend[t, c, e]

        if gated[t]:

            @pl.when(is_gate)
            def _():
                for c in range(chunks):
                    combine(t, c)

        if gated[t]:

            @pl.when(not_gate)
            def _():
                sent(psend.at[t, :, pl.ds(0, mid)], gate_send.at[t])

            @pl.when(is_gate)
            def _():
                sent(fsend.at[t], f_send.at[t])

            peers = mid - 1
        else:
            peers = n - 1
        if peers:
            sent(psend.at[t, :, pl.ds(0, peers)], p_send.at[t])

        if t < ticks - 1:
            if paired:

                @pl.when(jnp.logical_not(leads))
                def _():
                    pl.semaphore_signal(turn, inc=1, device_id=(previous, e), device_id_type=MESH)

            @pl.when(has_next)
            def _():
                landed(sel_in.at[t], sel_recv.at[t])

        if t > 0:

            @pl.when(has_prev)
            def _():
                landed(xown.at[t], raw_recv.at[t - 1])

        weights = [column(rate[t], k) for k in range(top)]
        for c in range(chunks):
            layer = xown[t, c].astype(single)
            if gated[t]:
                landed(frecv.at[t, c], f_recv.at[t, c])
                layer = layer + frecv[t, c].astype(single)
                sources, table = [base + j for j in range(mid)], pick[t, side]
            else:
                sources = list(range(n))
                table = jnp.concatenate([pick[t, 0], pick[t, 1]], axis=1)
            if peers:
                landed(precv.at[t, c, pl.ds(0, peers)], p_recv.at[t, c])
            value = jnp.concatenate(
                [precv[t, c, d].astype(single) for d in sources], axis=0
            ).astype(half)
            back = jnp.dot(table, value, preferred_element_type=single)
            for k in range(top):
                layer = layer + back[k * tokens : (k + 1) * tokens] * weights[k]
            layer = layer.astype(half)
            made[t, c] = layer
            out_copy(t, c).start()
            if t < ticks - 1:

                @pl.when(jnp.logical_and(has_next, jnp.logical_not(held)))
                def _():
                    forward(t, c)

        if t < ticks - 1 and paired:

            @pl.when(held)
            def _():
                pl.semaphore_wait(turn, 1)
                for c in range(chunks):
                    forward(t, c)

        if t < ticks - 1:

            @pl.when(jnp.logical_not(has_prev))
            def _():
                landed_own(t + 1)
                for c in range(chunks):
                    dispatch(t + 1, c)

    dispatched(0, early, chunks, mid - 1)
    for t in range(ticks):
        for copy in table_copies(t):
            copy.wait_send()

        @pl.when(is_gate)
        def _():
            if mid > 1:
                for j in range(mid):
                    sent(xrecv.at[t, :, pl.ds(0, mid - 1)], relay_send.at[t, j])

        if t > 0:

            @pl.when(jnp.logical_not(has_prev))
            def _():
                dispatched(t, 0, chunks, mid - 1)

        if t < ticks - 1:

            @pl.when(has_next)
            def _():
                dispatched(ticks + t, 0, chunks, mid)
                sent(made.at[t], raw_send.at[t])

    pltpu.make_async_copy(made, made, out_sem.at[0]).wait()

    @pl.when(has_prev)
    def _():
        for t in range(ticks - 1):
            sel_copy(t).wait_send()


def solution(mesh):
    n = mesh.shape["expert"]
    sections = mesh.shape["section"]

    def shards(acts, incoming, routes, route_weight, norm_gain, w_gate, w_up, w_down):
        ticks, _, tokens, top = routes.shape
        width, hidden = w_gate.shape[1:]
        chunks = 5 if width % (5 * 128) == 0 else 4
        cols = width // chunks
        cap = min(CAP, tokens)
        mid, sided, moves = n // 2, EXPERTS // 2, max(ticks - 1, 1)
        half, single = jnp.bfloat16, jnp.float32
        anywhere = pl.BlockSpec(memory_space=pl.ANY)
        dma = pltpu.SemaphoreType.DMA
        result = pl.pallas_call(
            functools.partial(kernel, n, sections),
            out_shape=jax.ShapeDtypeStruct((ticks, tokens, width), half),
            in_specs=[anywhere] * 8,
            out_specs=anywhere,
            scratch_shapes=[
                pltpu.VMEM((ticks, 1, top, tokens), routes.dtype),
                pltpu.VMEM((ticks, 1, top, tokens), single),
                pltpu.VMEM(norm_gain.shape, single),
                pltpu.VMEM((width, hidden), half),
                pltpu.VMEM((width, hidden), half),
                pltpu.VMEM((hidden, width), half),
                pltpu.VMEM((ticks, chunks, tokens, cols), half),
                pltpu.VMEM((ticks, chunks, tokens, cols), half),
                pltpu.VMEM((2 * ticks - 1, chunks, sided, cap, cols), half),
                pltpu.VMEM((ticks, chunks, mid, tokens, cols), half),
                pltpu.VMEM((ticks, chunks, mid, sided, cap, cols), half),
                pltpu.VMEM((ticks, chunks, n, cap, cols), half),
                pltpu.VMEM((ticks, chunks, n, cap, cols), half),
                pltpu.VMEM((ticks, chunks, n, cap, cols), half),
                pltpu.VMEM((moves, chunks, mid, mid, cap, cols), half),
                pltpu.VMEM((moves, chunks, mid, tokens, cols), half),
                pltpu.VMEM((moves, chunks, tokens, cols), half),
                pltpu.VMEM((ticks, 2, sided * cap, tokens), half),
                pltpu.VMEM((moves, sided * cap, tokens), half),
                pltpu.VMEM((ticks, mid, sided * cap, tokens), half),
                pltpu.VMEM((ticks, 2, top * tokens, mid * cap), half),
                pltpu.VMEM((ticks, mid, top * tokens, mid * cap), half),
                pltpu.VMEM((ticks, 8, 128), single),
                pltpu.VMEM((ticks, mid, 8, 128), single),
                dma((3,)),
                dma((3, chunks)),
                dma((1,)),
                dma((chunks + moves,)),
                dma((3, ticks)),
                dma((3, ticks)),
                dma((moves,)),
                dma((moves,)),
                dma((moves,)),
                dma((moves,)),
                dma((2 * ticks,)),
                dma((ticks, chunks)),
                dma((2 * ticks,)),
                dma((ticks, chunks)),
                dma((ticks, mid)),
                dma((ticks,)),
                dma((ticks, chunks)),
                dma((moves,)),
                dma((moves, chunks)),
                dma((moves,)),
                dma((moves, chunks)),
                pltpu.SemaphoreType.REGULAR,
            ],
            compiler_params=pltpu.CompilerParams(
                collective_id=0, has_side_effects=True, vmem_limit_bytes=60 << 20
            ),
        )(
            acts[0],
            incoming,
            jnp.swapaxes(routes, 2, 3),
            jnp.swapaxes(route_weight, 2, 3),
            norm_gain,
            w_gate[0],
            w_up[0],
            w_down[0],
        )
        return result[:, None]

    return jax.shard_map(
        shards,
        mesh=mesh,
        in_specs=(
            P("section", "expert", None),
            P(None, "expert", None),
            P(None, "section", "expert", None),
            P(None, "section", "expert", None),
            P("section", None),
            P("section", None, "expert"),
            P("section", None, "expert"),
            P("section", "expert", None),
        ),
        out_specs=P(None, "section", "expert", None),
        check_vma=False,
    )
```

```python
import functools

import jax
import jax.numpy as jnp
from jax import lax
from jax.experimental import pallas as pl
from jax.experimental.pallas import tpu as pltpu
from jax.sharding import PartitionSpec as P

MESH = pl.DeviceIdType.MESH
EXPERTS = 4
CAP = 24


def kernel(
    n,
    sections,
    acts,
    incoming,
    routes_hbm,
    route_weight_hbm,
    gain_hbm,
    w_gate_hbm,
    w_up_hbm,
    w_down_hbm,
    out,
    routes,
    route_weight,
    gain,
    w_gate,
    w_up,
    w_down,
    xown,
    made,
    xsend,
    xraw,
    xrelay,
    xrecv,
    psend,
    precv,
    pgate,
    fsend,
    frecv,
    sel,
    sel_in,
    sel_far,
    pick,
    pick_far,
    rate,
    rate_far,
    small_sem,
    w_sem,
    out_sem,
    own_sem,
    table_send,
    table_recv,
    sel_send,
    sel_recv,
    raw_send,
    raw_recv,
    far_send,
    far_recv,
    x_send,
    x_recv,
    relay_send,
    p_send,
    p_recv,
    gate_send,
    gate_recv,
    f_send,
    f_recv,
    turn,
):
    s = lax.axis_index("section")
    e = lax.axis_index("expert")
    ticks, chunks, tokens, cols = xown.shape
    top = routes.shape[2]
    cap = xrecv.shape[3]
    group = n // EXPERTS
    mid = n // 2
    sided = EXPERTS // 2
    gated = [t < ticks - 1 for t in range(ticks)]
    early = max(chunks - 2, 1)
    width = chunks * cols
    rows = n * cap
    side = e // mid
    base, far_base = side * mid, (1 - side) * mid
    own = e - base
    near_gate = jnp.where(side == 0, mid - 1, mid)
    far_gate = jnp.where(side == 0, mid, mid - 1)
    is_gate = e == near_gate
    not_gate = e != near_gate
    has_next = s < sections - 1
    has_prev = s > 0
    following = jnp.minimum(s + 1, sections - 1)
    previous = jnp.maximum(s - 1, 0)
    half = jnp.bfloat16
    single = jnp.float32

    def remote(source, target, send, recv, section, device):
        return pltpu.make_async_remote_copy(
            source, target, send, recv, device_id=(section, device), device_id_type=MESH
        )

    def near(body, own_too=False):
        def step(i, _):
            body(base + lax.rem(own + i, mid))
            return 0

        lax.fori_loop(0 if own_too else 1, mid, step, 0)

    def far(body):
        def step(i, _):
            body(far_base + i)
            return 0

        lax.fori_loop(0, mid, step, 0)

    def sent(source, send):
        remote(source, source, send, send, s, far_gate).wait_send()

    def landed(target, recv):
        remote(target, target, recv, recv, s, far_gate).wait_recv()

    def own_copy(t, c):
        source = acts if t == 0 else incoming.at[t - 1]
        return pltpu.make_async_copy(
            source.at[:, pl.ds(c * cols, cols)],
            xown.at[t, c],
            own_sem.at[c if t == 0 else chunks + t - 1],
        )

    def gate_copy(c):
        span = pl.ds(c * cols, cols)
        return (
            pltpu.make_async_copy(w_gate_hbm.at[span], w_gate.at[span], w_sem.at[0, c]),
            pltpu.make_async_copy(w_up_hbm.at[span], w_up.at[span], w_sem.at[1, c]),
        )

    down_copy = pltpu.make_async_copy(w_down_hbm, w_down, w_sem.at[2, 0])

    def table_copies(t):
        pairs = ((sel.at[t, 1 - side], sel_far), (pick.at[t, 1 - side], pick_far), (rate.at[t], rate_far))
        return [
            remote(
                source, target.at[t, own], table_send.at[i, t], table_recv.at[i, t], s, far_gate
            )
            for i, (source, target) in enumerate(pairs)
        ][: 3 if gated[t] else 1]

    def table_arrival(i, t):
        landed((sel_far, pick_far, rate_far)[i].at[t], table_recv.at[i, t])

    def sel_copy(t):
        return remote(
            sel.at[t + 1, side], sel_in.at[t], sel_send.at[t], sel_recv.at[t], previous, e
        )

    def raw_copy(t, c):
        return remote(
            made.at[t, c], xown.at[t + 1, c], raw_send.at[t], raw_recv.at[t], following, e
        )

    def bank(slot, c):
        return slot if slot > 0 or c < early else 2 * ticks - 1

    def far_copy(slot, t, c, section, source):
        return remote(
            source, xraw.at[t, c, own], far_send.at[bank(slot, c)], far_recv.at[t, c], section, far_gate
        )

    def x_copy(slot, t, c, section, d):
        return remote(
            xsend.at[slot, c, d // group - side * sided],
            xrecv.at[t, c, e],
            x_send.at[bank(slot, c)],
            x_recv.at[t, c],
            section,
            d,
        )

    def dispatched(slot, first, last, peers):
        span = pl.ds(first, last - first)
        sent(xown.at[0, span], far_send.at[bank(slot, first)])
        if peers:
            sent(xrecv.at[0, span, pl.ds(0, peers)], x_send.at[bank(slot, first)])

    def relay_copy(t, c, j, d):
        return remote(
            xrelay.at[t, c, j, d // group - side * sided],
            xrecv.at[t, c, far_base + j],
            relay_send.at[t, j],
            x_recv.at[t, c],
            s,
            d,
        )

    def p_copy(t, c, d):
        return remote(
            psend.at[t, c, d], precv.at[t, c, e], p_send.at[t], p_recv.at[t, c], s, d
        )

    def gate_send_copy(t, c):
        return remote(
            psend.at[t, c, pl.ds(far_base, mid)],
            pgate.at[t, c, own],
            gate_send.at[t],
            gate_recv.at[t, c],
            s,
            near_gate,
        )

    def f_copy(t, c, j):
        return remote(
            fsend.at[t, c, j], frecv.at[t, c], f_send.at[t], f_recv.at[t, c], s, far_base + j
        )

    def out_copy(t, c):
        return pltpu.make_async_copy(
            made.at[t, c], out.at[t, :, pl.ds(c * cols, cols)], out_sem.at[0]
        )

    small = [
        pltpu.make_async_copy(source, target, small_sem.at[i])
        for i, (source, target) in enumerate(
            ((routes_hbm, routes), (route_weight_hbm, route_weight), (gain_hbm, gain))
        )
    ]
    for copy in small:
        copy.start()
    for c in range(chunks):
        own_copy(0, c).start()

    barrier = pltpu.get_barrier_semaphore()

    def greet(d, _):
        @pl.when(d != e)
        def _():
            pl.semaphore_signal(barrier, inc=1, device_id=(s, d), device_id_type=MESH)

        return 0

    lax.fori_loop(0, n, greet, 0)
    for there, section in ((has_next, following), (has_prev, previous)):

        @pl.when(there)
        def _():
            pl.semaphore_signal(barrier, inc=1, device_id=(section, e), device_id_type=MESH)

    for c in range(chunks):
        for copy in gate_copy(c):
            copy.start()
    down_copy.start()

    @pl.when(jnp.logical_not(has_prev))
    def _():
        for t in range(1, ticks):
            for c in range(chunks):
                own_copy(t, c).start()

    for copy in small:
        copy.wait()

    def iota(shape, axis):
        return lax.broadcasted_iota(jnp.int32, shape, axis)

    before = (iota((tokens, tokens), 0) < iota((tokens, tokens), 1)).astype(half)
    diagonal = iota((tokens, tokens), 0) == iota((tokens, tokens), 1)
    place = iota((cap, tokens), 0).astype(single)
    for t in range(ticks):
        chosen = routes[t, 0]
        hot = sum(
            (iota((EXPERTS, tokens), 0) == chosen[k : k + 1]).astype(single) for k in range(top)
        )
        rank = jnp.dot(hot.astype(half), before, preferred_element_type=single)
        blocks = [
            [
                (place == jnp.where(chosen[k : k + 1] == x, rank[x : x + 1], -1.0)).astype(single)
                for x in range(EXPERTS)
            ]
            for k in range(top)
        ]
        for h in range(2):
            experts = range(h * sided, (h + 1) * sided)
            sel[t, h] = sum(
                jnp.concatenate([blocks[k][x] for x in experts], axis=0) for k in range(top)
            ).astype(half)
            for k in range(top):
                spread = jnp.concatenate(
                    [blocks[k][x] for x in experts for _ in range(group)], axis=0
                )
                pick[t, h, k * tokens : (k + 1) * tokens, :] = lax.dot_general(
                    diagonal.astype(half),
                    spread.astype(half),
                    (((1,), (1,)), ((), ())),
                    preferred_element_type=single,
                ).astype(half)
        rate[t] = jnp.zeros_like(rate[t])
        rate[t, 0:top, 0:tokens] = route_weight[t, 0]

    pl.semaphore_wait(
        barrier, n - 1 + jnp.where(has_next, 1, 0) + jnp.where(has_prev, 1, 0)
    )

    def pack(target, table, value):
        packed = jnp.dot(table, value, preferred_element_type=single)
        for x in range(sided):
            target[x] = packed[x * cap : (x + 1) * cap].astype(half)

    def landed_own(t):
        pltpu.make_async_copy(xown.at[t], xown.at[t], own_sem.at[chunks + t - 1]).wait()

    def dispatch(t, c):
        if t == 0:
            own_copy(t, c).wait()
        far_copy(t, t, c, s, xown.at[t, c]).start()
        pack(xsend.at[t, c], sel[t, side], xown[t, c])
        near(lambda d: x_copy(t, t, c, s, d).start())
        xrecv[t, c, e] = xsend[t, c, e // group - side * sided]

    paired = sections % 2 == 0
    leads = lax.rem(s, 2) == 0
    held = leads if paired else s < 0
    table_copies(0)[0].start()
    if paired:

        @pl.when(jnp.logical_not(leads))
        def _():
            pl.semaphore_wait(turn, 1)

    for c in range(chunks):
        dispatch(0, c)
    for t in range(ticks):
        for copy in table_copies(t)[1 if t == 0 else 0 :]:
            copy.start()

    @pl.when(has_prev)
    def _():
        for t in range(ticks - 1):
            sel_copy(t).start()

    dispatched(0, 0, early, mid - 1)
    if paired:

        @pl.when(leads)
        def _():
            pl.semaphore_signal(turn, inc=1, device_id=(following, e), device_id_type=MESH)

    def relay(t, c):
        if c == 0:
            table_arrival(0, t)
        landed(xraw.at[t, c], far_recv.at[t, c])
        for j in range(mid):
            pack(xrelay.at[t, c, j], sel_far[t, j], xraw[t, c, j])
            near(lambda d: relay_copy(t, c, j, d).start())
            xrecv[t, c, far_base + j] = xrelay[t, c, j, e // group - side * sided]

    def combine(t, c):
        if c == 0:
            table_arrival(1, t)
            table_arrival(2, t)
        if mid > 1:
            landed(pgate.at[t, c, pl.ds(0, mid - 1)], gate_recv.at[t, c])
        for j in range(mid):
            value = jnp.concatenate(
                [pgate[t, c, d, j].astype(single) for d in range(mid)], axis=0
            ).astype(half)
            back = jnp.dot(pick_far[t, j], value, preferred_element_type=single)
            total = None
            for k in range(top):
                part = back[k * tokens : (k + 1) * tokens] * column(rate_far[t, j], k)
                total = part if total is None else total + part
            fsend[t, c, j] = total.astype(half)
            f_copy(t, c, j).start()

    def forward(t, c):
        far_copy(ticks + t, t + 1, c, following, made.at[t, c]).start()
        pack(xsend.at[ticks + t, c], sel_in[t], made[t, c])
        near(lambda d: x_copy(ticks + t, t + 1, c, following, d).start(), True)
        raw_copy(t, c).start()

    def column(table, k):
        return jnp.sum(
            jnp.where(diagonal, table[k : k + 1, 0:tokens], 0.0), axis=1, keepdims=True
        )

    for t in range(ticks):
        gate_val = up_val = None
        squares = jnp.zeros((rows, 1), single)
        for c in range(chunks):

            @pl.when(is_gate)
            def _():
                relay(t, c)

            for packed, there in ((0, is_gate), (mid, not_gate)):
                if t == 0:
                    cases = ((mid - 1, there),)
                else:
                    cases = (
                        (mid, jnp.logical_and(there, has_prev)),
                        (mid - 1, jnp.logical_and(there, jnp.logical_not(has_prev))),
                    )
                for number, case in cases:
                    if packed + number:

                        @pl.when(case)
                        def _():
                            landed(xrecv.at[t, c, pl.ds(0, packed + number)], x_recv.at[t, c])

            if t == 0:
                for copy in gate_copy(c):
                    copy.wait()
            span = pl.ds(c * cols, cols)
            value = jnp.concatenate([xrecv[t, c, d].astype(single) for d in range(n)], axis=0)
            squares = squares + jnp.sum(value * value, axis=1, keepdims=True)
            normed = (value * gain[:, span]).astype(half)
            gate_part = jnp.dot(normed, w_gate[span, :], preferred_element_type=single)
            up_part = jnp.dot(normed, w_up[span, :], preferred_element_type=single)
            gate_val = gate_part if gate_val is None else gate_val + gate_part
            up_val = up_part if up_val is None else up_val + up_part
        scale = lax.rsqrt(squares * (1.0 / width) + 1e-06)
        hidden = (jax.nn.silu(gate_val * scale) * (up_val * scale)).astype(half)
        if t == 0:
            down_copy.wait()

        if t < ticks - 1:

            @pl.when(jnp.logical_not(has_prev))
            def _():
                landed_own(t + 1)
                for c in range(chunks):
                    dispatch(t + 1, c)

        for c in range(chunks):
            span = pl.ds(c * cols, cols)
            value = jnp.dot(hidden, w_down[:, span], preferred_element_type=single)
            for d in range(n):
                psend[t, c, d] = value[d * cap : (d + 1) * cap].astype(half)
            if gated[t]:

                @pl.when(not_gate)
                def _():
                    gate_send_copy(t, c).start()

                @pl.when(is_gate)
                def _():
                    pgate[t, c, own] = psend[t, c, pl.ds(far_base, mid)]

            else:
                far(lambda d: p_copy(t, c, d).start())
            near(lambda d: p_copy(t, c, d).start())
            precv[t, c, e] = psend[t, c, e]

        if gated[t]:

            @pl.when(is_gate)
            def _():
                for c in range(chunks):
                    combine(t, c)

        if gated[t]:

            @pl.when(not_gate)
            def _():
                sent(psend.at[t, :, pl.ds(0, mid)], gate_send.at[t])

            @pl.when(is_gate)
            def _():
                sent(fsend.at[t], f_send.at[t])

            peers = mid - 1
        else:
            peers = n - 1
        if peers:
            sent(psend.at[t, :, pl.ds(0, peers)], p_send.at[t])

        if t < ticks - 1:
            if paired:

                @pl.when(jnp.logical_not(leads))
                def _():
                    pl.semaphore_signal(turn, inc=1, device_id=(previous, e), device_id_type=MESH)

            @pl.when(has_next)
            def _():
                landed(sel_in.at[t], sel_recv.at[t])

        if t > 0:

            @pl.when(has_prev)
            def _():
                landed(xown.at[t], raw_recv.at[t - 1])

        weights = [column(rate[t], k) for k in range(top)]
        for c in range(chunks):
            layer = xown[t, c].astype(single)
            if gated[t]:
                landed(frecv.at[t, c], f_recv.at[t, c])
                layer = layer + frecv[t, c].astype(single)
                sources, table = [base + j for j in range(mid)], pick[t, side]
            else:
                sources = list(range(n))
                table = jnp.concatenate([pick[t, 0], pick[t, 1]], axis=1)
            if peers:
                landed(precv.at[t, c, pl.ds(0, peers)], p_recv.at[t, c])
            value = jnp.concatenate(
                [precv[t, c, d].astype(single) for d in sources], axis=0
            ).astype(half)
            back = jnp.dot(table, value, preferred_element_type=single)
            for k in range(top):
                layer = layer + back[k * tokens : (k + 1) * tokens] * weights[k]
            layer = layer.astype(half)
            made[t, c] = layer
            out_copy(t, c).start()
            if t < ticks - 1:

                @pl.when(jnp.logical_and(has_next, jnp.logical_not(held)))
                def _():
                    forward(t, c)

        if t < ticks - 1:

            @pl.when(held)
            def _():
                pl.semaphore_wait(turn, 1)

            @pl.when(held)
            def _():
                for c in range(chunks):
                    forward(t, c)

    dispatched(0, early, chunks, mid - 1)
    for t in range(ticks):
        for copy in table_copies(t):
            copy.wait_send()

        @pl.when(is_gate)
        def _():
            if mid > 1:
                for j in range(mid):
                    sent(xrecv.at[t, :, pl.ds(0, mid - 1)], relay_send.at[t, j])

        if t > 0:

            @pl.when(jnp.logical_not(has_prev))
            def _():
                dispatched(t, 0, chunks, mid - 1)

        if t < ticks - 1:

            @pl.when(has_next)
            def _():
                dispatched(ticks + t, 0, chunks, mid)
                sent(made.at[t], raw_send.at[t])

    pltpu.make_async_copy(made, made, out_sem.at[0]).wait()

    @pl.when(has_prev)
    def _():
        for t in range(ticks - 1):
            sel_copy(t).wait_send()


def solution(mesh):
    n = mesh.shape["expert"]
    sections = mesh.shape["section"]

    def shards(acts, incoming, routes, route_weight, norm_gain, w_gate, w_up, w_down):
        ticks, _, tokens, top = routes.shape
        width, hidden = w_gate.shape[1:]
        chunks = 5 if width % (5 * 128) == 0 else 4
        cols = width // chunks
        cap = min(CAP, tokens)
        mid, sided, moves = n // 2, EXPERTS // 2, max(ticks - 1, 1)
        half, single = jnp.bfloat16, jnp.float32
        anywhere = pl.BlockSpec(memory_space=pl.ANY)
        dma = pltpu.SemaphoreType.DMA
        result = pl.pallas_call(
            functools.partial(kernel, n, sections),
            out_shape=jax.ShapeDtypeStruct((ticks, tokens, width), half),
            in_specs=[anywhere] * 8,
            out_specs=anywhere,
            scratch_shapes=[
                pltpu.VMEM((ticks, 1, top, tokens), routes.dtype),
                pltpu.VMEM((ticks, 1, top, tokens), single),
                pltpu.VMEM(norm_gain.shape, single),
                pltpu.VMEM((width, hidden), half),
                pltpu.VMEM((width, hidden), half),
                pltpu.VMEM((hidden, width), half),
                pltpu.VMEM((ticks, chunks, tokens, cols), half),
                pltpu.VMEM((ticks, chunks, tokens, cols), half),
                pltpu.VMEM((2 * ticks - 1, chunks, sided, cap, cols), half),
                pltpu.VMEM((ticks, chunks, mid, tokens, cols), half),
                pltpu.VMEM((ticks, chunks, mid, sided, cap, cols), half),
                pltpu.VMEM((ticks, chunks, n, cap, cols), half),
                pltpu.VMEM((ticks, chunks, n, cap, cols), half),
                pltpu.VMEM((ticks, chunks, n, cap, cols), half),
                pltpu.VMEM((moves, chunks, mid, mid, cap, cols), half),
                pltpu.VMEM((moves, chunks, mid, tokens, cols), half),
                pltpu.VMEM((moves, chunks, tokens, cols), half),
                pltpu.VMEM((ticks, 2, sided * cap, tokens), half),
                pltpu.VMEM((moves, sided * cap, tokens), half),
                pltpu.VMEM((ticks, mid, sided * cap, tokens), half),
                pltpu.VMEM((ticks, 2, top * tokens, mid * cap), half),
                pltpu.VMEM((ticks, mid, top * tokens, mid * cap), half),
                pltpu.VMEM((ticks, 8, 128), single),
                pltpu.VMEM((ticks, mid, 8, 128), single),
                dma((3,)),
                dma((3, chunks)),
                dma((1,)),
                dma((chunks + moves,)),
                dma((3, ticks)),
                dma((3, ticks)),
                dma((moves,)),
                dma((moves,)),
                dma((moves,)),
                dma((moves,)),
                dma((2 * ticks,)),
                dma((ticks, chunks)),
                dma((2 * ticks,)),
                dma((ticks, chunks)),
                dma((ticks, mid)),
                dma((ticks,)),
                dma((ticks, chunks)),
                dma((moves,)),
                dma((moves, chunks)),
                dma((moves,)),
                dma((moves, chunks)),
                pltpu.SemaphoreType.REGULAR,
            ],
            compiler_params=pltpu.CompilerParams(
                collective_id=0, has_side_effects=True, vmem_limit_bytes=60 << 20
            ),
        )(
            acts[0],
            incoming,
            jnp.swapaxes(routes, 2, 3),
            jnp.swapaxes(route_weight, 2, 3),
            norm_gain,
            w_gate[0],
            w_up[0],
            w_down[0],
        )
        return result[:, None]

    return jax.shard_map(
        shards,
        mesh=mesh,
        in_specs=(
            P("section", "expert", None),
            P(None, "expert", None),
            P(None, "section", "expert", None),
            P(None, "section", "expert", None),
            P("section", None),
            P("section", None, "expert"),
            P("section", None, "expert"),
            P("section", "expert", None),
        ),
        out_specs=P(None, "section", "expert", None),
        check_vma=False,
    )
```

```python
import functools

import jax
import jax.numpy as jnp
from jax import lax
from jax.experimental import pallas as pl
from jax.experimental.pallas import tpu as pltpu
from jax.sharding import PartitionSpec as P

MESH = pl.DeviceIdType.MESH
EXPERTS = 4
CAP = 24


def kernel(
    n,
    sections,
    acts,
    incoming,
    routes_hbm,
    route_weight_hbm,
    gain_hbm,
    w_gate_hbm,
    w_up_hbm,
    w_down_hbm,
    out,
    routes,
    route_weight,
    gain,
    w_gate,
    w_up,
    w_down,
    xown,
    made,
    xsend,
    xraw,
    xrelay,
    xrecv,
    psend,
    precv,
    pgate,
    fsend,
    frecv,
    sel,
    sel_in,
    sel_far,
    pick,
    pick_far,
    rate,
    rate_far,
    small_sem,
    w_sem,
    out_sem,
    own_sem,
    table_send,
    table_recv,
    sel_send,
    sel_recv,
    raw_send,
    raw_recv,
    far_send,
    far_recv,
    x_send,
    x_recv,
    relay_send,
    p_send,
    p_recv,
    gate_send,
    gate_recv,
    f_send,
    f_recv,
    turn,
):
    s = lax.axis_index("section")
    e = lax.axis_index("expert")
    ticks, chunks, tokens, cols = xown.shape
    top = routes.shape[2]
    cap = xrecv.shape[3]
    group = n // EXPERTS
    mid = n // 2
    sided = EXPERTS // 2
    gated = [t < ticks - 1 for t in range(ticks)]
    early = max(chunks - 2, 1)
    width = chunks * cols
    rows = n * cap
    side = e // mid
    base, far_base = side * mid, (1 - side) * mid
    own = e - base
    near_gate = jnp.where(side == 0, mid - 1, mid)
    far_gate = jnp.where(side == 0, mid, mid - 1)
    is_gate = e == near_gate
    not_gate = e != near_gate
    has_next = s < sections - 1
    has_prev = s > 0
    following = jnp.minimum(s + 1, sections - 1)
    previous = jnp.maximum(s - 1, 0)
    half = jnp.bfloat16
    single = jnp.float32

    def remote(source, target, send, recv, section, device):
        return pltpu.make_async_remote_copy(
            source, target, send, recv, device_id=(section, device), device_id_type=MESH
        )

    def near(body, own_too=False):
        def step(i, _):
            body(base + lax.rem(own + i, mid))
            return 0

        lax.fori_loop(0 if own_too else 1, mid, step, 0)

    def far(body):
        def step(i, _):
            body(far_base + i)
            return 0

        lax.fori_loop(0, mid, step, 0)

    def sent(source, send):
        remote(source, source, send, send, s, far_gate).wait_send()

    def landed(target, recv):
        remote(target, target, recv, recv, s, far_gate).wait_recv()

    def own_copy(t, c):
        source = acts if t == 0 else incoming.at[t - 1]
        return pltpu.make_async_copy(
            source.at[:, pl.ds(c * cols, cols)],
            xown.at[t, c],
            own_sem.at[c if t == 0 else chunks + t - 1],
        )

    def gate_copy(c):
        span = pl.ds(c * cols, cols)
        return (
            pltpu.make_async_copy(w_gate_hbm.at[span], w_gate.at[span], w_sem.at[0, c]),
            pltpu.make_async_copy(w_up_hbm.at[span], w_up.at[span], w_sem.at[1, c]),
        )

    down_copy = pltpu.make_async_copy(w_down_hbm, w_down, w_sem.at[2, 0])

    def table_copies(t):
        pairs = ((sel.at[t, 1 - side], sel_far), (pick.at[t, 1 - side], pick_far), (rate.at[t], rate_far))
        return [
            remote(
                source, target.at[t, own], table_send.at[i, t], table_recv.at[i, t], s, far_gate
            )
            for i, (source, target) in enumerate(pairs)
        ][: 3 if gated[t] else 1]

    def table_arrival(i, t):
        landed((sel_far, pick_far, rate_far)[i].at[t], table_recv.at[i, t])

    def sel_copy(t):
        return remote(
            sel.at[t + 1, side], sel_in.at[t], sel_send.at[t], sel_recv.at[t], previous, e
        )

    def raw_copy(t, c):
        return remote(
            made.at[t, c], xown.at[t + 1, c], raw_send.at[t], raw_recv.at[t], following, e
        )

    def bank(slot, c):
        return slot if slot > 0 or c < early else 2 * ticks - 1

    def far_copy(slot, t, c, section, source):
        return remote(
            source, xraw.at[t, c, own], far_send.at[bank(slot, c)], far_recv.at[t, c], section, far_gate
        )

    def x_copy(slot, t, c, section, d):
        return remote(
            xsend.at[slot, c, d // group - side * sided],
            xrecv.at[t, c, e],
            x_send.at[bank(slot, c)],
            x_recv.at[t, c],
            section,
            d,
        )

    def dispatched(slot, first, last, peers):
        span = pl.ds(first, last - first)
        sent(xown.at[0, span], far_send.at[bank(slot, first)])
        if peers:
            sent(xrecv.at[0, span, pl.ds(0, peers)], x_send.at[bank(slot, first)])

    def relay_copy(t, c, j, d):
        return remote(
            xrelay.at[t, c, j, d // group - side * sided],
            xrecv.at[t, c, far_base + j],
            relay_send.at[t, j],
            x_recv.at[t, c],
            s,
            d,
        )

    def p_copy(t, c, d):
        return remote(
            psend.at[t, c, d], precv.at[t, c, e], p_send.at[t], p_recv.at[t, c], s, d
        )

    def gate_send_copy(t, c):
        return remote(
            psend.at[t, c, pl.ds(far_base, mid)],
            pgate.at[t, c, own],
            gate_send.at[t],
            gate_recv.at[t, c],
            s,
            near_gate,
        )

    def f_copy(t, c, j):
        return remote(
            fsend.at[t, c, j], frecv.at[t, c], f_send.at[t], f_recv.at[t, c], s, far_base + j
        )

    def out_copy(t, c):
        return pltpu.make_async_copy(
            made.at[t, c], out.at[t, :, pl.ds(c * cols, cols)], out_sem.at[0]
        )

    small = [
        pltpu.make_async_copy(source, target, small_sem.at[i])
        for i, (source, target) in enumerate(
            ((routes_hbm, routes), (route_weight_hbm, route_weight), (gain_hbm, gain))
        )
    ]
    for copy in small:
        copy.start()
    for c in range(chunks):
        own_copy(0, c).start()

    barrier = pltpu.get_barrier_semaphore()

    def greet(d, _):
        @pl.when(d != e)
        def _():
            pl.semaphore_signal(barrier, inc=1, device_id=(s, d), device_id_type=MESH)

        return 0

    lax.fori_loop(0, n, greet, 0)
    for there, section in ((has_next, following), (has_prev, previous)):

        @pl.when(there)
        def _():
            pl.semaphore_signal(barrier, inc=1, device_id=(section, e), device_id_type=MESH)

    for c in range(chunks):
        for copy in gate_copy(c):
            copy.start()
    down_copy.start()

    @pl.when(jnp.logical_not(has_prev))
    def _():
        for t in range(1, ticks):
            for c in range(chunks):
                own_copy(t, c).start()

    for copy in small:
        copy.wait()

    def iota(shape, axis):
        return lax.broadcasted_iota(jnp.int32, shape, axis)

    before = (iota((tokens, tokens), 0) < iota((tokens, tokens), 1)).astype(half)
    diagonal = iota((tokens, tokens), 0) == iota((tokens, tokens), 1)
    place = iota((cap, tokens), 0).astype(single)
    for t in range(ticks):
        chosen = routes[t, 0]
        hot = sum(
            (iota((EXPERTS, tokens), 0) == chosen[k : k + 1]).astype(single) for k in range(top)
        )
        rank = jnp.dot(hot.astype(half), before, preferred_element_type=single)
        blocks = [
            [
                (place == jnp.where(chosen[k : k + 1] == x, rank[x : x + 1], -1.0)).astype(single)
                for x in range(EXPERTS)
            ]
            for k in range(top)
        ]
        for h in range(2):
            experts = range(h * sided, (h + 1) * sided)
            sel[t, h] = sum(
                jnp.concatenate([blocks[k][x] for x in experts], axis=0) for k in range(top)
            ).astype(half)
            for k in range(top):
                spread = jnp.concatenate(
                    [blocks[k][x] for x in experts for _ in range(group)], axis=0
                )
                pick[t, h, k * tokens : (k + 1) * tokens, :] = lax.dot_general(
                    diagonal.astype(half),
                    spread.astype(half),
                    (((1,), (1,)), ((), ())),
                    preferred_element_type=single,
                ).astype(half)
        rate[t] = jnp.zeros_like(rate[t])
        rate[t, 0:top, 0:tokens] = route_weight[t, 0]

    pl.semaphore_wait(
        barrier, n - 1 + jnp.where(has_next, 1, 0) + jnp.where(has_prev, 1, 0)
    )

    def pack(target, table, value):
        packed = jnp.dot(table, value, preferred_element_type=single)
        for x in range(sided):
            target[x] = packed[x * cap : (x + 1) * cap].astype(half)

    def landed_own(t):
        pltpu.make_async_copy(xown.at[t], xown.at[t], own_sem.at[chunks + t - 1]).wait()

    def dispatch(t, c):
        if t == 0:
            own_copy(t, c).wait()
        far_copy(t, t, c, s, xown.at[t, c]).start()
        pack(xsend.at[t, c], sel[t, side], xown[t, c])
        near(lambda d: x_copy(t, t, c, s, d).start())
        xrecv[t, c, e] = xsend[t, c, e // group - side * sided]

    paired = sections % 2 == 0
    leads = lax.rem(s, 2) == 0
    held = leads if paired else s < 0
    table_copies(0)[0].start()
    if paired:

        @pl.when(jnp.logical_not(leads))
        def _():
            pl.semaphore_wait(turn, 1)

    for c in range(chunks):
        dispatch(0, c)
    for t in range(ticks):
        for copy in table_copies(t)[1 if t == 0 else 0 :]:
            copy.start()

    @pl.when(has_prev)
    def _():
        for t in range(ticks - 1):
            sel_copy(t).start()

    dispatched(0, 0, early, mid - 1)
    if paired:

        @pl.when(leads)
        def _():
            pl.semaphore_signal(turn, inc=1, device_id=(following, e), device_id_type=MESH)

    def relay(t, c):
        if c == 0:
            table_arrival(0, t)
        landed(xraw.at[t, c], far_recv.at[t, c])
        for j in range(mid):
            pack(xrelay.at[t, c, j], sel_far[t, j], xraw[t, c, j])
            near(lambda d: relay_copy(t, c, j, d).start())
            xrecv[t, c, far_base + j] = xrelay[t, c, j, e // group - side * sided]

    def combine(t, c):
        if c == 0:
            table_arrival(1, t)
            table_arrival(2, t)
        if mid > 1:
            landed(pgate.at[t, c, pl.ds(0, mid - 1)], gate_recv.at[t, c])
        for j in range(mid):
            value = jnp.concatenate(
                [pgate[t, c, d, j].astype(single) for d in range(mid)], axis=0
            ).astype(half)
            back = jnp.dot(pick_far[t, j], value, preferred_element_type=single)
            total = None
            for k in range(top):
                part = back[k * tokens : (k + 1) * tokens] * column(rate_far[t, j], k)
                total = part if total is None else total + part
            fsend[t, c, j] = total.astype(half)
            f_copy(t, c, j).start()

    def forward(t, c):
        far_copy(ticks + t, t + 1, c, following, made.at[t, c]).start()
        pack(xsend.at[ticks + t, c], sel_in[t], made[t, c])
        near(lambda d: x_copy(ticks + t, t + 1, c, following, d).start(), True)
        raw_copy(t, c).start()

    def column(table, k):
        return jnp.sum(
            jnp.where(diagonal, table[k : k + 1, 0:tokens], 0.0), axis=1, keepdims=True
        )

    for t in range(ticks):
        gate_val = up_val = None
        squares = jnp.zeros((rows, 1), single)
        for c in range(chunks):

            @pl.when(is_gate)
            def _():
                relay(t, c)

            for packed, there in ((0, is_gate), (mid, not_gate)):
                if t == 0:
                    cases = ((mid - 1, there),)
                else:
                    cases = (
                        (mid, jnp.logical_and(there, has_prev)),
                        (mid - 1, jnp.logical_and(there, jnp.logical_not(has_prev))),
                    )
                for number, case in cases:
                    if packed + number:

                        @pl.when(case)
                        def _():
                            landed(xrecv.at[t, c, pl.ds(0, packed + number)], x_recv.at[t, c])

            if t == 0:
                for copy in gate_copy(c):
                    copy.wait()
            span = pl.ds(c * cols, cols)
            value = jnp.concatenate([xrecv[t, c, d].astype(single) for d in range(n)], axis=0)
            squares = squares + jnp.sum(value * value, axis=1, keepdims=True)
            normed = (value * gain[:, span]).astype(half)
            gate_part = jnp.dot(normed, w_gate[span, :], preferred_element_type=single)
            up_part = jnp.dot(normed, w_up[span, :], preferred_element_type=single)
            gate_val = gate_part if gate_val is None else gate_val + gate_part
            up_val = up_part if up_val is None else up_val + up_part
        scale = lax.rsqrt(squares * (1.0 / width) + 1e-06)
        hidden = (jax.nn.silu(gate_val * scale) * (up_val * scale)).astype(half)
        if t == 0:
            down_copy.wait()

        for c in range(chunks):
            span = pl.ds(c * cols, cols)
            value = jnp.dot(hidden, w_down[:, span], preferred_element_type=single)
            for d in range(n):
                psend[t, c, d] = value[d * cap : (d + 1) * cap].astype(half)
            if gated[t]:

                @pl.when(not_gate)
                def _():
                    gate_send_copy(t, c).start()

                @pl.when(is_gate)
                def _():
                    pgate[t, c, own] = psend[t, c, pl.ds(far_base, mid)]

            else:
                far(lambda d: p_copy(t, c, d).start())
            near(lambda d: p_copy(t, c, d).start())
            precv[t, c, e] = psend[t, c, e]

        if t < ticks - 1:

            @pl.when(jnp.logical_not(has_prev))
            def _():
                landed_own(t + 1)
                for c in range(chunks):
                    dispatch(t + 1, c)

        if gated[t]:

            @pl.when(is_gate)
            def _():
                for c in range(chunks):
                    combine(t, c)

        if gated[t]:

            @pl.when(not_gate)
            def _():
                sent(psend.at[t, :, pl.ds(0, mid)], gate_send.at[t])

            @pl.when(is_gate)
            def _():
                sent(fsend.at[t], f_send.at[t])

            peers = mid - 1
        else:
            peers = n - 1
        if peers:
            sent(psend.at[t, :, pl.ds(0, peers)], p_send.at[t])

        if t < ticks - 1:
            if paired:

                @pl.when(jnp.logical_not(leads))
                def _():
                    pl.semaphore_signal(turn, inc=1, device_id=(previous, e), device_id_type=MESH)

            @pl.when(has_next)
            def _():
                landed(sel_in.at[t], sel_recv.at[t])

        if t > 0:

            @pl.when(has_prev)
            def _():
                landed(xown.at[t], raw_recv.at[t - 1])

        weights = [column(rate[t], k) for k in range(top)]
        for c in range(chunks):
            layer = xown[t, c].astype(single)
            if gated[t]:
                landed(frecv.at[t, c], f_recv.at[t, c])
                layer = layer + frecv[t, c].astype(single)
                sources, table = [base + j for j in range(mid)], pick[t, side]
            else:
                sources = list(range(n))
                table = jnp.concatenate([pick[t, 0], pick[t, 1]], axis=1)
            if peers:
                landed(precv.at[t, c, pl.ds(0, peers)], p_recv.at[t, c])
            value = jnp.concatenate(
                [precv[t, c, d].astype(single) for d in sources], axis=0
            ).astype(half)
            back = jnp.dot(table, value, preferred_element_type=single)
            for k in range(top):
                layer = layer + back[k * tokens : (k + 1) * tokens] * weights[k]
            layer = layer.astype(half)
            made[t, c] = layer
            out_copy(t, c).start()
            if t < ticks - 1:

                @pl.when(jnp.logical_and(has_next, jnp.logical_not(held)))
                def _():
                    forward(t, c)

        if t < ticks - 1:

            @pl.when(held)
            def _():
                pl.semaphore_wait(turn, 1)

            @pl.when(held)
            def _():
                for c in range(chunks):
                    forward(t, c)

    dispatched(0, early, chunks, mid - 1)
    for t in range(ticks):
        for copy in table_copies(t):
            copy.wait_send()

        @pl.when(is_gate)
        def _():
            if mid > 1:
                for j in range(mid):
                    sent(xrecv.at[t, :, pl.ds(0, mid - 1)], relay_send.at[t, j])

        if t > 0:

            @pl.when(jnp.logical_not(has_prev))
            def _():
                dispatched(t, 0, chunks, mid - 1)

        if t < ticks - 1:

            @pl.when(has_next)
            def _():
                dispatched(ticks + t, 0, chunks, mid)
                sent(made.at[t], raw_send.at[t])

    pltpu.make_async_copy(made, made, out_sem.at[0]).wait()

    @pl.when(has_prev)
    def _():
        for t in range(ticks - 1):
            sel_copy(t).wait_send()


def solution(mesh):
    n = mesh.shape["expert"]
    sections = mesh.shape["section"]

    def shards(acts, incoming, routes, route_weight, norm_gain, w_gate, w_up, w_down):
        ticks, _, tokens, top = routes.shape
        width, hidden = w_gate.shape[1:]
        chunks = 5 if width % (5 * 128) == 0 else 4
        cols = width // chunks
        cap = min(CAP, tokens)
        mid, sided, moves = n // 2, EXPERTS // 2, max(ticks - 1, 1)
        half, single = jnp.bfloat16, jnp.float32
        anywhere = pl.BlockSpec(memory_space=pl.ANY)
        dma = pltpu.SemaphoreType.DMA
        result = pl.pallas_call(
            functools.partial(kernel, n, sections),
            out_shape=jax.ShapeDtypeStruct((ticks, tokens, width), half),
            in_specs=[anywhere] * 8,
            out_specs=anywhere,
            scratch_shapes=[
                pltpu.VMEM((ticks, 1, top, tokens), routes.dtype),
                pltpu.VMEM((ticks, 1, top, tokens), single),
                pltpu.VMEM(norm_gain.shape, single),
                pltpu.VMEM((width, hidden), half),
                pltpu.VMEM((width, hidden), half),
                pltpu.VMEM((hidden, width), half),
                pltpu.VMEM((ticks, chunks, tokens, cols), half),
                pltpu.VMEM((ticks, chunks, tokens, cols), half),
                pltpu.VMEM((2 * ticks - 1, chunks, sided, cap, cols), half),
                pltpu.VMEM((ticks, chunks, mid, tokens, cols), half),
                pltpu.VMEM((ticks, chunks, mid, sided, cap, cols), half),
                pltpu.VMEM((ticks, chunks, n, cap, cols), half),
                pltpu.VMEM((ticks, chunks, n, cap, cols), half),
                pltpu.VMEM((ticks, chunks, n, cap, cols), half),
                pltpu.VMEM((moves, chunks, mid, mid, cap, cols), half),
                pltpu.VMEM((moves, chunks, mid, tokens, cols), half),
                pltpu.VMEM((moves, chunks, tokens, cols), half),
                pltpu.VMEM((ticks, 2, sided * cap, tokens), half),
                pltpu.VMEM((moves, sided * cap, tokens), half),
                pltpu.VMEM((ticks, mid, sided * cap, tokens), half),
                pltpu.VMEM((ticks, 2, top * tokens, mid * cap), half),
                pltpu.VMEM((ticks, mid, top * tokens, mid * cap), half),
                pltpu.VMEM((ticks, 8, 128), single),
                pltpu.VMEM((ticks, mid, 8, 128), single),
                dma((3,)),
                dma((3, chunks)),
                dma((1,)),
                dma((chunks + moves,)),
                dma((3, ticks)),
                dma((3, ticks)),
                dma((moves,)),
                dma((moves,)),
                dma((moves,)),
                dma((moves,)),
                dma((2 * ticks,)),
                dma((ticks, chunks)),
                dma((2 * ticks,)),
                dma((ticks, chunks)),
                dma((ticks, mid)),
                dma((ticks,)),
                dma((ticks, chunks)),
                dma((moves,)),
                dma((moves, chunks)),
                dma((moves,)),
                dma((moves, chunks)),
                pltpu.SemaphoreType.REGULAR,
            ],
            compiler_params=pltpu.CompilerParams(
                collective_id=0, has_side_effects=True, vmem_limit_bytes=34 << 20
            ),
        )(
            *(
                pltpu.with_memory_space_constraint(value, pltpu.HBM)
                for value in (
                    acts[0],
                    incoming,
                    jnp.swapaxes(routes, 2, 3),
                    jnp.swapaxes(route_weight, 2, 3),
                    norm_gain,
                    w_gate[0],
                    w_up[0],
                    w_down[0],
                )
            )
        )
        return result[:, None]

    return jax.shard_map(
        shards,
        mesh=mesh,
        in_specs=(
            P("section", "expert", None),
            P(None, "expert", None),
            P(None, "section", "expert", None),
            P(None, "section", "expert", None),
            P("section", None),
            P("section", None, "expert"),
            P("section", None, "expert"),
            P("section", "expert", None),
        ),
        out_specs=P(None, "section", "expert", None),
        check_vma=False,
    )
```

```python
import functools

import jax
import jax.numpy as jnp
from jax import lax
from jax.experimental import pallas as pl
from jax.experimental.pallas import tpu as pltpu
from jax.sharding import PartitionSpec as P

MESH = pl.DeviceIdType.MESH
EXPERTS = 4
CAP = 24


def kernel(
    n,
    sections,
    acts,
    incoming,
    routes_hbm,
    route_weight_hbm,
    gain_hbm,
    w_gate_hbm,
    w_up_hbm,
    w_down_hbm,
    out,
    routes,
    route_weight,
    gain,
    w_gate,
    w_up,
    w_down,
    xown,
    made,
    xsend,
    xraw,
    xrelay,
    xrecv,
    psend,
    precv,
    pgate,
    fsend,
    frecv,
    sel,
    sel_in,
    sel_far,
    pick,
    pick_far,
    rate,
    rate_far,
    small_sem,
    w_sem,
    out_sem,
    own_sem,
    table_send,
    table_recv,
    sel_send,
    sel_recv,
    raw_send,
    raw_recv,
    far_send,
    far_recv,
    x_send,
    x_recv,
    relay_send,
    p_send,
    p_recv,
    gate_send,
    gate_recv,
    f_send,
    f_recv,
    turn,
):
    s = lax.axis_index("section")
    e = lax.axis_index("expert")
    ticks, chunks, tokens, cols = xown.shape
    top = routes.shape[2]
    cap = xrecv.shape[3]
    group = n // EXPERTS
    mid = n // 2
    sided = EXPERTS // 2
    gated = [t < ticks - 1 for t in range(ticks)]
    early = max(chunks - 2, 1)
    width = chunks * cols
    rows = n * cap
    side = e // mid
    base, far_base = side * mid, (1 - side) * mid
    own = e - base
    near_gate = jnp.where(side == 0, mid - 1, mid)
    far_gate = jnp.where(side == 0, mid, mid - 1)
    is_gate = e == near_gate
    not_gate = e != near_gate
    has_next = s < sections - 1
    has_prev = s > 0
    following = jnp.minimum(s + 1, sections - 1)
    previous = jnp.maximum(s - 1, 0)
    half = jnp.bfloat16
    single = jnp.float32

    def remote(source, target, send, recv, section, device):
        return pltpu.make_async_remote_copy(
            source, target, send, recv, device_id=(section, device), device_id_type=MESH
        )

    def near(body, own_too=False):
        def step(i, _):
            body(base + lax.rem(own + i, mid))
            return 0

        lax.fori_loop(0 if own_too else 1, mid, step, 0)

    def far(body):
        def step(i, _):
            body(far_base + i)
            return 0

        lax.fori_loop(0, mid, step, 0)

    def sent(source, send):
        remote(source, source, send, send, s, far_gate).wait_send()

    def landed(target, recv):
        remote(target, target, recv, recv, s, far_gate).wait_recv()

    def own_copy(t, c):
        source = acts if t == 0 else incoming.at[t - 1]
        return pltpu.make_async_copy(
            source.at[:, pl.ds(c * cols, cols)],
            xown.at[t, c],
            own_sem.at[c if t == 0 else chunks + t - 1],
        )

    def gate_copy(c):
        span = pl.ds(c * cols, cols)
        return (
            pltpu.make_async_copy(w_gate_hbm.at[span], w_gate.at[span], w_sem.at[0, c]),
            pltpu.make_async_copy(w_up_hbm.at[span], w_up.at[span], w_sem.at[1, c]),
        )

    down_copy = pltpu.make_async_copy(w_down_hbm, w_down, w_sem.at[2, 0])

    def table_copies(t):
        pairs = ((sel.at[t, 1 - side], sel_far), (pick.at[t, 1 - side], pick_far), (rate.at[t], rate_far))
        return [
            remote(
                source, target.at[t, own], table_send.at[i, t], table_recv.at[i, t], s, far_gate
            )
            for i, (source, target) in enumerate(pairs)
        ][: 3 if gated[t] else 1]

    def table_arrival(i, t):
        landed((sel_far, pick_far, rate_far)[i].at[t], table_recv.at[i, t])

    def sel_copy(t):
        return remote(
            sel.at[t + 1, side], sel_in.at[t], sel_send.at[t], sel_recv.at[t], previous, e
        )

    def raw_copy(t, c):
        return remote(
            made.at[t, c], xown.at[t + 1, c], raw_send.at[t], raw_recv.at[t], following, e
        )

    def bank(slot, c):
        return slot if slot > 0 or c < early else 2 * ticks - 1

    def far_copy(slot, t, c, section, source):
        return remote(
            source, xraw.at[t, c, own], far_send.at[bank(slot, c)], far_recv.at[t, c], section, far_gate
        )

    def x_copy(slot, t, c, section, d):
        return remote(
            xsend.at[slot, c, d // group - side * sided],
            xrecv.at[t, c, e],
            x_send.at[bank(slot, c)],
            x_recv.at[t, c],
            section,
            d,
        )

    def dispatched(slot, first, last, peers):
        span = pl.ds(first, last - first)
        sent(xown.at[0, span], far_send.at[bank(slot, first)])
        if peers:
            sent(xrecv.at[0, span, pl.ds(0, peers)], x_send.at[bank(slot, first)])

    def relay_copy(t, c, j, d):
        return remote(
            xrelay.at[t, c, j, d // group - side * sided],
            xrecv.at[t, c, far_base + j],
            relay_send.at[t, j],
            x_recv.at[t, c],
            s,
            d,
        )

    def p_copy(t, c, d):
        return remote(
            psend.at[t, c, d], precv.at[t, c, e], p_send.at[t], p_recv.at[t, c], s, d
        )

    def gate_send_copy(t, c):
        return remote(
            psend.at[t, c, pl.ds(far_base, mid)],
            pgate.at[t, c, own],
            gate_send.at[t],
            gate_recv.at[t, c],
            s,
            near_gate,
        )

    def f_copy(t, c, j):
        return remote(
            fsend.at[t, c, j], frecv.at[t, c], f_send.at[t], f_recv.at[t, c], s, far_base + j
        )

    def out_copy(t, c):
        return pltpu.make_async_copy(
            made.at[t, c], out.at[t, :, pl.ds(c * cols, cols)], out_sem.at[0]
        )

    small = [
        pltpu.make_async_copy(source, target, small_sem.at[i])
        for i, (source, target) in enumerate(
            ((routes_hbm, routes), (route_weight_hbm, route_weight), (gain_hbm, gain))
        )
    ]
    for copy in small:
        copy.start()
    for c in range(chunks):
        own_copy(0, c).start()

    barrier = pltpu.get_barrier_semaphore()

    def greet(d, _):
        @pl.when(d != e)
        def _():
            pl.semaphore_signal(barrier, inc=1, device_id=(s, d), device_id_type=MESH)

        return 0

    lax.fori_loop(0, n, greet, 0)
    for there, section in ((has_next, following), (has_prev, previous)):

        @pl.when(there)
        def _():
            pl.semaphore_signal(barrier, inc=1, device_id=(section, e), device_id_type=MESH)

    for c in range(chunks):
        for copy in gate_copy(c):
            copy.start()
    down_copy.start()

    @pl.when(jnp.logical_not(has_prev))
    def _():
        for t in range(1, ticks):
            for c in range(chunks):
                own_copy(t, c).start()

    for copy in small:
        copy.wait()

    def iota(shape, axis):
        return lax.broadcasted_iota(jnp.int32, shape, axis)

    before = (iota((tokens, tokens), 0) < iota((tokens, tokens), 1)).astype(half)
    diagonal = iota((tokens, tokens), 0) == iota((tokens, tokens), 1)
    place = iota((cap, tokens), 0).astype(single)
    for t in range(ticks):
        chosen = routes[t, 0]
        hot = sum(
            (iota((EXPERTS, tokens), 0) == chosen[k : k + 1]).astype(single) for k in range(top)
        )
        rank = jnp.dot(hot.astype(half), before, preferred_element_type=single)
        blocks = [
            [
                (place == jnp.where(chosen[k : k + 1] == x, rank[x : x + 1], -1.0)).astype(single)
                for x in range(EXPERTS)
            ]
            for k in range(top)
        ]
        for h in range(2):
            experts = range(h * sided, (h + 1) * sided)
            sel[t, h] = sum(
                jnp.concatenate([blocks[k][x] for x in experts], axis=0) for k in range(top)
            ).astype(half)
            for k in range(top):
                spread = jnp.concatenate(
                    [blocks[k][x] for x in experts for _ in range(group)], axis=0
                )
                pick[t, h, k * tokens : (k + 1) * tokens, :] = lax.dot_general(
                    diagonal.astype(half),
                    spread.astype(half),
                    (((1,), (1,)), ((), ())),
                    preferred_element_type=single,
                ).astype(half)
        rate[t] = jnp.zeros_like(rate[t])
        rate[t, 0:top, 0:tokens] = route_weight[t, 0]

    pl.semaphore_wait(
        barrier, n - 1 + jnp.where(has_next, 1, 0) + jnp.where(has_prev, 1, 0)
    )

    def pack(target, table, value):
        packed = jnp.dot(table, value, preferred_element_type=single)
        for x in range(sided):
            target[x] = packed[x * cap : (x + 1) * cap].astype(half)

    def landed_own(t):
        pltpu.make_async_copy(xown.at[t], xown.at[t], own_sem.at[chunks + t - 1]).wait()

    def dispatch(t, c):
        if t == 0:
            own_copy(t, c).wait()
        far_copy(t, t, c, s, xown.at[t, c]).start()
        pack(xsend.at[t, c], sel[t, side], xown[t, c])
        near(lambda d: x_copy(t, t, c, s, d).start())
        xrecv[t, c, e] = xsend[t, c, e // group - side * sided]

    paired = sections % 2 == 0
    leads = lax.rem(s, 2) == 0
    held = leads if paired else s < 0
    table_copies(0)[0].start()
    if paired:

        @pl.when(jnp.logical_not(leads))
        def _():
            pl.semaphore_wait(turn, 1)

    for c in range(chunks):
        dispatch(0, c)
    for t in range(ticks):
        for copy in table_copies(t)[1 if t == 0 else 0 :]:
            copy.start()

    @pl.when(has_prev)
    def _():
        for t in range(ticks - 1):
            sel_copy(t).start()

    dispatched(0, 0, early, mid - 1)
    if paired:

        @pl.when(leads)
        def _():
            pl.semaphore_signal(turn, inc=1, device_id=(following, e), device_id_type=MESH)

    def relay(t, c):
        if c == 0:
            table_arrival(0, t)
        landed(xraw.at[t, c], far_recv.at[t, c])
        for j in range(mid):
            pack(xrelay.at[t, c, j], sel_far[t, j], xraw[t, c, j])
            near(lambda d: relay_copy(t, c, j, d).start())
            xrecv[t, c, far_base + j] = xrelay[t, c, j, e // group - side * sided]

    def combine(t, c):
        if c == 0:
            table_arrival(1, t)
            table_arrival(2, t)
        if mid > 1:
            landed(pgate.at[t, c, pl.ds(0, mid - 1)], gate_recv.at[t, c])
        for j in range(mid):
            value = jnp.concatenate(
                [pgate[t, c, d, j].astype(single) for d in range(mid)], axis=0
            ).astype(half)
            back = jnp.dot(pick_far[t, j], value, preferred_element_type=single)
            total = None
            for k in range(top):
                part = back[k * tokens : (k + 1) * tokens] * column(rate_far[t, j], k)
                total = part if total is None else total + part
            fsend[t, c, j] = total.astype(half)
            f_copy(t, c, j).start()

    def forward(t, c):
        far_copy(ticks + t, t + 1, c, following, made.at[t, c]).start()
        pack(xsend.at[ticks + t, c], sel_in[t], made[t, c])
        near(lambda d: x_copy(ticks + t, t + 1, c, following, d).start(), True)
        raw_copy(t, c).start()

    def column(table, k):
        return jnp.sum(
            jnp.where(diagonal, table[k : k + 1, 0:tokens], 0.0), axis=1, keepdims=True
        )

    for t in range(ticks):
        gate_val = up_val = None
        squares = jnp.zeros((rows, 1), single)
        for c in range(chunks):

            @pl.when(is_gate if t == 0 else jnp.logical_and(is_gate, has_prev))
            def _():
                relay(t, c)

            for packed, there in ((0, is_gate), (mid, not_gate)):
                if t == 0:
                    cases = ((mid - 1, there),)
                else:
                    cases = (
                        (mid, jnp.logical_and(there, has_prev)),
                        (mid - 1, jnp.logical_and(there, jnp.logical_not(has_prev))),
                    )
                for number, case in cases:
                    if packed + number:

                        @pl.when(case)
                        def _():
                            landed(xrecv.at[t, c, pl.ds(0, packed + number)], x_recv.at[t, c])

            if t == 0:
                for copy in gate_copy(c):
                    copy.wait()
            span = pl.ds(c * cols, cols)
            value = jnp.concatenate([xrecv[t, c, d].astype(single) for d in range(n)], axis=0)
            squares = squares + jnp.sum(value * value, axis=1, keepdims=True)
            normed = (value * gain[:, span]).astype(half)
            gate_part = jnp.dot(normed, w_gate[span, :], preferred_element_type=single)
            up_part = jnp.dot(normed, w_up[span, :], preferred_element_type=single)
            gate_val = gate_part if gate_val is None else gate_val + gate_part
            up_val = up_part if up_val is None else up_val + up_part
        scale = lax.rsqrt(squares * (1.0 / width) + 1e-06)
        hidden = (jax.nn.silu(gate_val * scale) * (up_val * scale)).astype(half)
        if t == 0:
            down_copy.wait()

        for c in range(chunks):
            span = pl.ds(c * cols, cols)
            value = jnp.dot(hidden, w_down[:, span], preferred_element_type=single)
            for d in range(n):
                psend[t, c, d] = value[d * cap : (d + 1) * cap].astype(half)
            if gated[t]:

                @pl.when(not_gate)
                def _():
                    gate_send_copy(t, c).start()

                @pl.when(is_gate)
                def _():
                    pgate[t, c, own] = psend[t, c, pl.ds(far_base, mid)]

            else:
                far(lambda d: p_copy(t, c, d).start())
            near(lambda d: p_copy(t, c, d).start())
            precv[t, c, e] = psend[t, c, e]

        if t < ticks - 1:

            @pl.when(jnp.logical_not(has_prev))
            def _():
                landed_own(t + 1)
                for c in range(chunks):
                    dispatch(t + 1, c)

        if gated[t]:

            @pl.when(is_gate)
            def _():
                for c in range(chunks):
                    combine(t, c)

        if gated[t]:

            @pl.when(not_gate)
            def _():
                sent(psend.at[t, :, pl.ds(0, mid)], gate_send.at[t])

            @pl.when(is_gate)
            def _():
                sent(fsend.at[t], f_send.at[t])

            peers = mid - 1
        else:
            peers = n - 1
        if peers:
            sent(psend.at[t, :, pl.ds(0, peers)], p_send.at[t])

        if t < ticks - 1:
            if paired:

                @pl.when(jnp.logical_not(leads))
                def _():
                    pl.semaphore_signal(turn, inc=1, device_id=(previous, e), device_id_type=MESH)

            @pl.when(has_next)
            def _():
                landed(sel_in.at[t], sel_recv.at[t])

        if t > 0:

            @pl.when(has_prev)
            def _():
                landed(xown.at[t], raw_recv.at[t - 1])

        weights = [column(rate[t], k) for k in range(top)]
        for c in range(chunks):
            layer = xown[t, c].astype(single)
            if gated[t]:
                landed(frecv.at[t, c], f_recv.at[t, c])
                layer = layer + frecv[t, c].astype(single)
                sources, table = [base + j for j in range(mid)], pick[t, side]
            else:
                sources = list(range(n))
                table = jnp.concatenate([pick[t, 0], pick[t, 1]], axis=1)
            if peers:
                landed(precv.at[t, c, pl.ds(0, peers)], p_recv.at[t, c])
            value = jnp.concatenate(
                [precv[t, c, d].astype(single) for d in sources], axis=0
            ).astype(half)
            back = jnp.dot(table, value, preferred_element_type=single)
            for k in range(top):
                layer = layer + back[k * tokens : (k + 1) * tokens] * weights[k]
            layer = layer.astype(half)
            made[t, c] = layer
            out_copy(t, c).start()
            if t < ticks - 1:

                @pl.when(jnp.logical_and(has_next, jnp.logical_not(held)))
                def _():
                    forward(t, c)

        if t < ticks - 1:

            @pl.when(jnp.logical_and(is_gate, jnp.logical_not(has_prev)))
            def _():
                for c in range(chunks):
                    relay(t + 1, c)

            @pl.when(held)
            def _():
                pl.semaphore_wait(turn, 1)

            @pl.when(held)
            def _():
                for c in range(chunks):
                    forward(t, c)

    dispatched(0, early, chunks, mid - 1)
    for t in range(ticks):
        for copy in table_copies(t):
            copy.wait_send()

        @pl.when(is_gate)
        def _():
            if mid > 1:
                for j in range(mid):
                    sent(xrecv.at[t, :, pl.ds(0, mid - 1)], relay_send.at[t, j])

        if t > 0:

            @pl.when(jnp.logical_not(has_prev))
            def _():
                dispatched(t, 0, chunks, mid - 1)

        if t < ticks - 1:

            @pl.when(has_next)
            def _():
                dispatched(ticks + t, 0, chunks, mid)
                sent(made.at[t], raw_send.at[t])

    pltpu.make_async_copy(made, made, out_sem.at[0]).wait()

    @pl.when(has_prev)
    def _():
        for t in range(ticks - 1):
            sel_copy(t).wait_send()


def solution(mesh):
    n = mesh.shape["expert"]
    sections = mesh.shape["section"]

    def shards(acts, incoming, routes, route_weight, norm_gain, w_gate, w_up, w_down):
        ticks, _, tokens, top = routes.shape
        width, hidden = w_gate.shape[1:]
        chunks = 5 if width % (5 * 128) == 0 else 4
        cols = width // chunks
        cap = min(CAP, tokens)
        mid, sided, moves = n // 2, EXPERTS // 2, max(ticks - 1, 1)
        half, single = jnp.bfloat16, jnp.float32
        anywhere = pl.BlockSpec(memory_space=pl.ANY)
        dma = pltpu.SemaphoreType.DMA
        result = pl.pallas_call(
            functools.partial(kernel, n, sections),
            out_shape=jax.ShapeDtypeStruct((ticks, tokens, width), half),
            in_specs=[anywhere] * 8,
            out_specs=anywhere,
            scratch_shapes=[
                pltpu.VMEM((ticks, 1, top, tokens), routes.dtype),
                pltpu.VMEM((ticks, 1, top, tokens), single),
                pltpu.VMEM(norm_gain.shape, single),
                pltpu.VMEM((width, hidden), half),
                pltpu.VMEM((width, hidden), half),
                pltpu.VMEM((hidden, width), half),
                pltpu.VMEM((ticks, chunks, tokens, cols), half),
                pltpu.VMEM((ticks, chunks, tokens, cols), half),
                pltpu.VMEM((2 * ticks - 1, chunks, sided, cap, cols), half),
                pltpu.VMEM((ticks, chunks, mid, tokens, cols), half),
                pltpu.VMEM((ticks, chunks, mid, sided, cap, cols), half),
                pltpu.VMEM((ticks, chunks, n, cap, cols), half),
                pltpu.VMEM((ticks, chunks, n, cap, cols), half),
                pltpu.VMEM((ticks, chunks, n, cap, cols), half),
                pltpu.VMEM((moves, chunks, mid, mid, cap, cols), half),
                pltpu.VMEM((moves, chunks, mid, tokens, cols), half),
                pltpu.VMEM((moves, chunks, tokens, cols), half),
                pltpu.VMEM((ticks, 2, sided * cap, tokens), half),
                pltpu.VMEM((moves, sided * cap, tokens), half),
                pltpu.VMEM((ticks, mid, sided * cap, tokens), half),
                pltpu.VMEM((ticks, 2, top * tokens, mid * cap), half),
                pltpu.VMEM((ticks, mid, top * tokens, mid * cap), half),
                pltpu.VMEM((ticks, 8, 128), single),
                pltpu.VMEM((ticks, mid, 8, 128), single),
                dma((3,)),
                dma((3, chunks)),
                dma((1,)),
                dma((chunks + moves,)),
                dma((3, ticks)),
                dma((3, ticks)),
                dma((moves,)),
                dma((moves,)),
                dma((moves,)),
                dma((moves,)),
                dma((2 * ticks,)),
                dma((ticks, chunks)),
                dma((2 * ticks,)),
                dma((ticks, chunks)),
                dma((ticks, mid)),
                dma((ticks,)),
                dma((ticks, chunks)),
                dma((moves,)),
                dma((moves, chunks)),
                dma((moves,)),
                dma((moves, chunks)),
                pltpu.SemaphoreType.REGULAR,
            ],
            compiler_params=pltpu.CompilerParams(
                collective_id=0, has_side_effects=True, vmem_limit_bytes=34 << 20
            ),
        )(
            *(
                pltpu.with_memory_space_constraint(value, pltpu.HBM)
                for value in (
                    acts[0],
                    incoming,
                    jnp.swapaxes(routes, 2, 3),
                    jnp.swapaxes(route_weight, 2, 3),
                    norm_gain,
                    w_gate[0],
                    w_up[0],
                    w_down[0],
                )
            )
        )
        return result[:, None]

    return jax.shard_map(
        shards,
        mesh=mesh,
        in_specs=(
            P("section", "expert", None),
            P(None, "expert", None),
            P(None, "section", "expert", None),
            P(None, "section", "expert", None),
            P("section", None),
            P("section", None, "expert"),
            P("section", None, "expert"),
            P("section", "expert", None),
        ),
        out_specs=P(None, "section", "expert", None),
        check_vma=False,
    )
```

```python
import functools

import jax
import jax.numpy as jnp
from jax import lax
from jax.experimental import pallas as pl
from jax.experimental.pallas import tpu as pltpu
from jax.sharding import PartitionSpec as P

MESH = pl.DeviceIdType.MESH
EXPERTS = 4
CAP = 24


def kernel(
    n,
    sections,
    acts,
    incoming,
    routes_hbm,
    route_weight_hbm,
    gain_hbm,
    w_gate_hbm,
    w_up_hbm,
    w_down_hbm,
    out,
    routes,
    route_weight,
    gain,
    w_gate,
    w_up,
    w_down,
    xown,
    made,
    xsend,
    xraw,
    xrelay,
    xrecv,
    psend,
    precv,
    pgate,
    fsend,
    frecv,
    sel,
    sel_in,
    sel_far,
    pick,
    pick_far,
    rate,
    rate_far,
    small_sem,
    w_sem,
    out_sem,
    own_sem,
    table_send,
    table_recv,
    sel_send,
    sel_recv,
    raw_send,
    raw_recv,
    far_send,
    far_recv,
    x_send,
    x_recv,
    relay_send,
    p_send,
    p_recv,
    gate_send,
    gate_recv,
    f_send,
    f_recv,
    turn,
):
    s = lax.axis_index("section")
    e = lax.axis_index("expert")
    ticks, chunks, tokens, cols = xown.shape
    top = routes.shape[2]
    cap = xrecv.shape[3]
    group = n // EXPERTS
    mid = n // 2
    sided = EXPERTS // 2
    gated = [t < ticks - 1 for t in range(ticks)]
    early = max(chunks - 1, 1)
    width = chunks * cols
    rows = n * cap
    side = e // mid
    base, far_base = side * mid, (1 - side) * mid
    own = e - base
    near_gate = jnp.where(side == 0, mid - 1, mid)
    far_gate = jnp.where(side == 0, mid, mid - 1)
    is_gate = e == near_gate
    not_gate = e != near_gate
    has_next = s < sections - 1
    has_prev = s > 0
    following = jnp.minimum(s + 1, sections - 1)
    previous = jnp.maximum(s - 1, 0)
    half = jnp.bfloat16
    single = jnp.float32

    def remote(source, target, send, recv, section, device):
        return pltpu.make_async_remote_copy(
            source, target, send, recv, device_id=(section, device), device_id_type=MESH
        )

    def near(body, own_too=False):
        def step(i, _):
            body(base + lax.rem(own + i, mid))
            return 0

        lax.fori_loop(0 if own_too else 1, mid, step, 0)

    def far(body):
        def step(i, _):
            body(far_base + i)
            return 0

        lax.fori_loop(0, mid, step, 0)

    def sent(source, send):
        remote(source, source, send, send, s, far_gate).wait_send()

    def landed(target, recv):
        remote(target, target, recv, recv, s, far_gate).wait_recv()

    def own_copy(t, c):
        source = acts if t == 0 else incoming.at[t - 1]
        return pltpu.make_async_copy(
            source.at[:, pl.ds(c * cols, cols)],
            xown.at[t, c],
            own_sem.at[c if t == 0 else chunks + t - 1],
        )

    def gate_copy(c):
        span = pl.ds(c * cols, cols)
        return (
            pltpu.make_async_copy(w_gate_hbm.at[span], w_gate.at[span], w_sem.at[0, c]),
            pltpu.make_async_copy(w_up_hbm.at[span], w_up.at[span], w_sem.at[1, c]),
        )

    down_copy = pltpu.make_async_copy(w_down_hbm, w_down, w_sem.at[2, 0])

    def table_copies(t):
        pairs = ((sel.at[t, 1 - side], sel_far), (pick.at[t, 1 - side], pick_far), (rate.at[t], rate_far))
        return [
            remote(
                source, target.at[t, own], table_send.at[i, t], table_recv.at[i, t], s, far_gate
            )
            for i, (source, target) in enumerate(pairs)
        ][: 3 if gated[t] else 1]

    def table_arrival(i, t):
        landed((sel_far, pick_far, rate_far)[i].at[t], table_recv.at[i, t])

    def sel_copy(t):
        return remote(
            sel.at[t + 1, side], sel_in.at[t], sel_send.at[t], sel_recv.at[t], previous, e
        )

    def raw_copy(t, c):
        return remote(
            made.at[t, c], xown.at[t + 1, c], raw_send.at[t], raw_recv.at[t], following, e
        )

    def bank(slot, c):
        return slot if slot > 0 or c < early else 2 * ticks - 1

    def far_copy(slot, t, c, section, source):
        return remote(
            source, xraw.at[t, c, own], far_send.at[bank(slot, c)], far_recv.at[t, c], section, far_gate
        )

    def x_copy(slot, t, c, section, d):
        return remote(
            xsend.at[slot, c, d // group - side * sided],
            xrecv.at[t, c, e],
            x_send.at[bank(slot, c)],
            x_recv.at[t, c],
            section,
            d,
        )

    def dispatched(slot, first, last, peers):
        span = pl.ds(first, last - first)
        sent(xown.at[0, span], far_send.at[bank(slot, first)])
        if peers:
            sent(xrecv.at[0, span, pl.ds(0, peers)], x_send.at[bank(slot, first)])

    def relay_copy(t, c, j, d):
        return remote(
            xrelay.at[t, c, j, d // group - side * sided],
            xrecv.at[t, c, far_base + j],
            relay_send.at[t, j],
            x_recv.at[t, c],
            s,
            d,
        )

    def p_copy(t, c, d):
        return remote(
            psend.at[t, c, d], precv.at[t, c, e], p_send.at[t], p_recv.at[t, c], s, d
        )

    def gate_send_copy(t, c):
        return remote(
            psend.at[t, c, pl.ds(far_base, mid)],
            pgate.at[t, c, own],
            gate_send.at[t],
            gate_recv.at[t, c],
            s,
            near_gate,
        )

    def f_copy(t, c, j):
        return remote(
            fsend.at[t, c, j], frecv.at[t, c], f_send.at[t], f_recv.at[t, c], s, far_base + j
        )

    def out_copy(t, c):
        return pltpu.make_async_copy(
            made.at[t, c], out.at[t, :, pl.ds(c * cols, cols)], out_sem.at[0]
        )

    small = [
        pltpu.make_async_copy(source, target, small_sem.at[i])
        for i, (source, target) in enumerate(
            ((routes_hbm, routes), (route_weight_hbm, route_weight), (gain_hbm, gain))
        )
    ]
    for copy in small:
        copy.start()
    for c in range(chunks):
        own_copy(0, c).start()

    barrier = pltpu.get_barrier_semaphore()

    def greet(d, _):
        @pl.when(d != e)
        def _():
            pl.semaphore_signal(barrier, inc=1, device_id=(s, d), device_id_type=MESH)

        return 0

    lax.fori_loop(0, n, greet, 0)
    for there, section in ((has_next, following), (has_prev, previous)):

        @pl.when(there)
        def _():
            pl.semaphore_signal(barrier, inc=1, device_id=(section, e), device_id_type=MESH)

    for c in range(chunks):
        for copy in gate_copy(c):
            copy.start()
    down_copy.start()

    @pl.when(jnp.logical_not(has_prev))
    def _():
        for t in range(1, ticks):
            for c in range(chunks):
                own_copy(t, c).start()

    for copy in small:
        copy.wait()

    def iota(shape, axis):
        return lax.broadcasted_iota(jnp.int32, shape, axis)

    before = (iota((tokens, tokens), 0) < iota((tokens, tokens), 1)).astype(half)
    diagonal = iota((tokens, tokens), 0) == iota((tokens, tokens), 1)
    place = iota((cap, tokens), 0).astype(single)
    for t in range(ticks):
        chosen = routes[t, 0]
        hot = sum(
            (iota((EXPERTS, tokens), 0) == chosen[k : k + 1]).astype(single) for k in range(top)
        )
        rank = jnp.dot(hot.astype(half), before, preferred_element_type=single)
        blocks = [
            [
                (place == jnp.where(chosen[k : k + 1] == x, rank[x : x + 1], -1.0)).astype(single)
                for x in range(EXPERTS)
            ]
            for k in range(top)
        ]
        for h in range(2):
            experts = range(h * sided, (h + 1) * sided)
            sel[t, h] = sum(
                jnp.concatenate([blocks[k][x] for x in experts], axis=0) for k in range(top)
            ).astype(half)
            for k in range(top):
                spread = jnp.concatenate(
                    [blocks[k][x] for x in experts for _ in range(group)], axis=0
                )
                pick[t, h, k * tokens : (k + 1) * tokens, :] = lax.dot_general(
                    diagonal.astype(half),
                    spread.astype(half),
                    (((1,), (1,)), ((), ())),
                    preferred_element_type=single,
                ).astype(half)
        rate[t] = jnp.zeros_like(rate[t])
        rate[t, 0:top, 0:tokens] = route_weight[t, 0]

    pl.semaphore_wait(
        barrier, n - 1 + jnp.where(has_next, 1, 0) + jnp.where(has_prev, 1, 0)
    )

    def pack(target, table, value):
        packed = jnp.dot(table, value, preferred_element_type=single)
        for x in range(sided):
            target[x] = packed[x * cap : (x + 1) * cap].astype(half)

    def landed_own(t):
        pltpu.make_async_copy(xown.at[t], xown.at[t], own_sem.at[chunks + t - 1]).wait()

    def dispatch_far(t, c):
        far_copy(t, t, c, s, xown.at[t, c]).start()

    def dispatch_near(t, c):
        pack(xsend.at[t, c], sel[t, side], xown[t, c])
        near(lambda d: x_copy(t, t, c, s, d).start())
        xrecv[t, c, e] = xsend[t, c, e // group - side * sided]

    def dispatch(t, c):
        own_copy(t, c).wait()
        dispatch_far(t, c)
        dispatch_near(t, c)

    paired = sections % 2 == 0
    leads = lax.rem(s, 2) == 0
    held = leads if paired else s < 0
    table_copies(0)[0].start()
    if paired:

        @pl.when(jnp.logical_not(leads))
        def _():
            pl.semaphore_wait(turn, 1)

    for c in range(chunks):
        dispatch(0, c)
    for t in range(ticks):
        for copy in table_copies(t)[1 if t == 0 else 0 :]:
            copy.start()

    @pl.when(has_prev)
    def _():
        for t in range(ticks - 1):
            sel_copy(t).start()

    dispatched(0, 0, early, mid - 1)
    if paired:

        @pl.when(leads)
        def _():
            pl.semaphore_signal(turn, inc=1, device_id=(following, e), device_id_type=MESH)

    def relay(t, c):
        if c == 0:
            table_arrival(0, t)
        landed(xraw.at[t, c], far_recv.at[t, c])
        for j in range(mid):
            pack(xrelay.at[t, c, j], sel_far[t, j], xraw[t, c, j])
            near(lambda d: relay_copy(t, c, j, d).start())
            xrecv[t, c, far_base + j] = xrelay[t, c, j, e // group - side * sided]

    def combine(t, c):
        if c == 0:
            table_arrival(1, t)
            table_arrival(2, t)
        if mid > 1:
            landed(pgate.at[t, c, pl.ds(0, mid - 1)], gate_recv.at[t, c])
        for j in range(mid):
            value = jnp.concatenate(
                [pgate[t, c, d, j].astype(single) for d in range(mid)], axis=0
            ).astype(half)
            back = jnp.dot(pick_far[t, j], value, preferred_element_type=single)
            total = None
            for k in range(top):
                part = back[k * tokens : (k + 1) * tokens] * column(rate_far[t, j], k)
                total = part if total is None else total + part
            fsend[t, c, j] = total.astype(half)
            f_copy(t, c, j).start()

    def forward(t, c):
        far_copy(ticks + t, t + 1, c, following, made.at[t, c]).start()
        pack(xsend.at[ticks + t, c], sel_in[t], made[t, c])
        near(lambda d: x_copy(ticks + t, t + 1, c, following, d).start(), True)
        raw_copy(t, c).start()

    def column(table, k):
        return jnp.sum(
            jnp.where(diagonal, table[k : k + 1, 0:tokens], 0.0), axis=1, keepdims=True
        )

    for t in range(ticks):
        gate_val = up_val = None
        squares = jnp.zeros((rows, 1), single)
        for c in range(chunks):

            @pl.when(is_gate if t == 0 else jnp.logical_and(is_gate, has_prev))
            def _():
                relay(t, c)

            for packed, there in ((0, is_gate), (mid, not_gate)):
                if t == 0:
                    cases = ((mid - 1, there),)
                else:
                    cases = (
                        (mid, jnp.logical_and(there, has_prev)),
                        (mid - 1, jnp.logical_and(there, jnp.logical_not(has_prev))),
                    )
                for number, case in cases:
                    if packed + number:

                        @pl.when(case)
                        def _():
                            landed(xrecv.at[t, c, pl.ds(0, packed + number)], x_recv.at[t, c])

            if t == 0:
                for copy in gate_copy(c):
                    copy.wait()
            span = pl.ds(c * cols, cols)
            value = jnp.concatenate([xrecv[t, c, d].astype(single) for d in range(n)], axis=0)
            squares = squares + jnp.sum(value * value, axis=1, keepdims=True)
            normed = (value * gain[:, span]).astype(half)
            gate_part = jnp.dot(normed, w_gate[span, :], preferred_element_type=single)
            up_part = jnp.dot(normed, w_up[span, :], preferred_element_type=single)
            gate_val = gate_part if gate_val is None else gate_val + gate_part
            up_val = up_part if up_val is None else up_val + up_part
        scale = lax.rsqrt(squares * (1.0 / width) + 1e-06)
        hidden = (jax.nn.silu(gate_val * scale) * (up_val * scale)).astype(half)
        if t == 0:
            down_copy.wait()

        for c in range(chunks):
            span = pl.ds(c * cols, cols)
            value = jnp.dot(hidden, w_down[:, span], preferred_element_type=single)
            for d in range(n):
                psend[t, c, d] = value[d * cap : (d + 1) * cap].astype(half)
            if gated[t]:

                @pl.when(not_gate)
                def _():
                    gate_send_copy(t, c).start()

                @pl.when(is_gate)
                def _():
                    pgate[t, c, own] = psend[t, c, pl.ds(far_base, mid)]

            else:
                far(lambda d: p_copy(t, c, d).start())
            near(lambda d: p_copy(t, c, d).start())
            precv[t, c, e] = psend[t, c, e]

        if t < ticks - 1:

            @pl.when(jnp.logical_not(has_prev))
            def _():
                landed_own(t + 1)
                for c in range(chunks):
                    dispatch_far(t + 1, c)

        if gated[t]:

            @pl.when(is_gate)
            def _():
                for c in range(chunks):
                    combine(t, c)

        if gated[t]:

            @pl.when(not_gate)
            def _():
                sent(psend.at[t, :, pl.ds(0, mid)], gate_send.at[t])

            @pl.when(is_gate)
            def _():
                sent(fsend.at[t], f_send.at[t])

            peers = mid - 1
        else:
            peers = n - 1
        if peers:
            sent(psend.at[t, :, pl.ds(0, peers)], p_send.at[t])

        if t < ticks - 1:
            if paired:

                @pl.when(jnp.logical_not(leads))
                def _():
                    pl.semaphore_signal(turn, inc=1, device_id=(previous, e), device_id_type=MESH)

            @pl.when(has_next)
            def _():
                landed(sel_in.at[t], sel_recv.at[t])

        if t > 0:

            @pl.when(has_prev)
            def _():
                landed(xown.at[t], raw_recv.at[t - 1])

        weights = [column(rate[t], k) for k in range(top)]
        for c in range(chunks):
            layer = xown[t, c].astype(single)
            if gated[t]:
                landed(frecv.at[t, c], f_recv.at[t, c])
                layer = layer + frecv[t, c].astype(single)
                sources, table = [base + j for j in range(mid)], pick[t, side]
            else:
                sources = list(range(n))
                table = jnp.concatenate([pick[t, 0], pick[t, 1]], axis=1)
            if peers:
                landed(precv.at[t, c, pl.ds(0, peers)], p_recv.at[t, c])
            value = jnp.concatenate(
                [precv[t, c, d].astype(single) for d in sources], axis=0
            ).astype(half)
            back = jnp.dot(table, value, preferred_element_type=single)
            for k in range(top):
                layer = layer + back[k * tokens : (k + 1) * tokens] * weights[k]
            layer = layer.astype(half)
            made[t, c] = layer
            out_copy(t, c).start()
            if t < ticks - 1:

                @pl.when(jnp.logical_and(has_next, jnp.logical_not(held)))
                def _():
                    forward(t, c)

        if t < ticks - 1:

            @pl.when(jnp.logical_and(is_gate, jnp.logical_not(has_prev)))
            def _():
                for c in range(chunks):
                    relay(t + 1, c)

            @pl.when(jnp.logical_not(has_prev))
            def _():
                for c in range(chunks):
                    dispatch_near(t + 1, c)

            @pl.when(held)
            def _():
                pl.semaphore_wait(turn, 1)

            @pl.when(held)
            def _():
                for c in range(chunks):
                    forward(t, c)

    dispatched(0, early, chunks, mid - 1)
    for t in range(ticks):
        for copy in table_copies(t):
            copy.wait_send()

        @pl.when(is_gate)
        def _():
            if mid > 1:
                for j in range(mid):
                    sent(xrecv.at[t, :, pl.ds(0, mid - 1)], relay_send.at[t, j])

        if t > 0:

            @pl.when(jnp.logical_not(has_prev))
            def _():
                dispatched(t, 0, chunks, mid - 1)

        if t < ticks - 1:

            @pl.when(has_next)
            def _():
                dispatched(ticks + t, 0, chunks, mid)
                sent(made.at[t], raw_send.at[t])

    pltpu.make_async_copy(made, made, out_sem.at[0]).wait()

    @pl.when(has_prev)
    def _():
        for t in range(ticks - 1):
            sel_copy(t).wait_send()


def solution(mesh):
    n = mesh.shape["expert"]
    sections = mesh.shape["section"]

    def shards(acts, incoming, routes, route_weight, norm_gain, w_gate, w_up, w_down):
        ticks, _, tokens, top = routes.shape
        width, hidden = w_gate.shape[1:]
        chunks = 5 if width % (5 * 128) == 0 else 4
        cols = width // chunks
        cap = min(CAP, tokens)
        mid, sided, moves = n // 2, EXPERTS // 2, max(ticks - 1, 1)
        half, single = jnp.bfloat16, jnp.float32
        anywhere = pl.BlockSpec(memory_space=pl.ANY)
        dma = pltpu.SemaphoreType.DMA
        result = pl.pallas_call(
            functools.partial(kernel, n, sections),
            out_shape=jax.ShapeDtypeStruct((ticks, tokens, width), half),
            in_specs=[anywhere] * 8,
            out_specs=anywhere,
            scratch_shapes=[
                pltpu.VMEM((ticks, 1, top, tokens), routes.dtype),
                pltpu.VMEM((ticks, 1, top, tokens), single),
                pltpu.VMEM(norm_gain.shape, single),
                pltpu.VMEM((width, hidden), half),
                pltpu.VMEM((width, hidden), half),
                pltpu.VMEM((hidden, width), half),
                pltpu.VMEM((ticks, chunks, tokens, cols), half),
                pltpu.VMEM((ticks, chunks, tokens, cols), half),
                pltpu.VMEM((2 * ticks - 1, chunks, sided, cap, cols), half),
                pltpu.VMEM((ticks, chunks, mid, tokens, cols), half),
                pltpu.VMEM((ticks, chunks, mid, sided, cap, cols), half),
                pltpu.VMEM((ticks, chunks, n, cap, cols), half),
                pltpu.VMEM((ticks, chunks, n, cap, cols), half),
                pltpu.VMEM((ticks, chunks, n, cap, cols), half),
                pltpu.VMEM((moves, chunks, mid, mid, cap, cols), half),
                pltpu.VMEM((moves, chunks, mid, tokens, cols), half),
                pltpu.VMEM((moves, chunks, tokens, cols), half),
                pltpu.VMEM((ticks, 2, sided * cap, tokens), half),
                pltpu.VMEM((moves, sided * cap, tokens), half),
                pltpu.VMEM((ticks, mid, sided * cap, tokens), half),
                pltpu.VMEM((ticks, 2, top * tokens, mid * cap), half),
                pltpu.VMEM((ticks, mid, top * tokens, mid * cap), half),
                pltpu.VMEM((ticks, 8, 128), single),
                pltpu.VMEM((ticks, mid, 8, 128), single),
                dma((3,)),
                dma((3, chunks)),
                dma((1,)),
                dma((chunks + moves,)),
                dma((3, ticks)),
                dma((3, ticks)),
                dma((moves,)),
                dma((moves,)),
                dma((moves,)),
                dma((moves,)),
                dma((2 * ticks,)),
                dma((ticks, chunks)),
                dma((2 * ticks,)),
                dma((ticks, chunks)),
                dma((ticks, mid)),
                dma((ticks,)),
                dma((ticks, chunks)),
                dma((moves,)),
                dma((moves, chunks)),
                dma((moves,)),
                dma((moves, chunks)),
                pltpu.SemaphoreType.REGULAR,
            ],
            compiler_params=pltpu.CompilerParams(
                collective_id=0, has_side_effects=True, vmem_limit_bytes=34 << 20
            ),
        )(
            *(
                pltpu.with_memory_space_constraint(value, pltpu.HBM)
                for value in (
                    acts[0],
                    incoming,
                    jnp.swapaxes(routes, 2, 3),
                    jnp.swapaxes(route_weight, 2, 3),
                    norm_gain,
                    w_gate[0],
                    w_up[0],
                    w_down[0],
                )
            )
        )
        return result[:, None]

    return jax.shard_map(
        shards,
        mesh=mesh,
        in_specs=(
            P("section", "expert", None),
            P(None, "expert", None),
            P(None, "section", "expert", None),
            P(None, "section", "expert", None),
            P("section", None),
            P("section", None, "expert"),
            P("section", None, "expert"),
            P("section", "expert", None),
        ),
        out_specs=P(None, "section", "expert", None),
        check_vma=False,
    )
```

```python
import functools

import jax
import jax.numpy as jnp
from jax import lax
from jax.experimental import pallas as pl
from jax.experimental.pallas import tpu as pltpu
from jax.sharding import PartitionSpec as P

MESH = pl.DeviceIdType.MESH
EXPERTS = 4
CAP = 24


def kernel(
    n,
    sections,
    acts,
    incoming,
    routes_hbm,
    route_weight_hbm,
    gain_hbm,
    w_gate_hbm,
    w_up_hbm,
    w_down_hbm,
    out,
    routes,
    route_weight,
    gain,
    w_gate,
    w_up,
    w_down,
    xown,
    made,
    xsend,
    xraw,
    xrelay,
    xrecv,
    psend,
    precv,
    pgate,
    fsend,
    frecv,
    sel,
    sel_in,
    sel_far,
    pick,
    pick_far,
    rate,
    rate_far,
    small_sem,
    w_sem,
    out_sem,
    own_sem,
    table_send,
    table_recv,
    sel_send,
    sel_recv,
    raw_send,
    raw_recv,
    far_send,
    far_recv,
    x_send,
    x_recv,
    relay_send,
    p_send,
    p_recv,
    gate_send,
    gate_recv,
    f_send,
    f_recv,
    turn,
):
    s = lax.axis_index("section")
    e = lax.axis_index("expert")
    ticks, chunks, tokens, cols = xown.shape
    top = routes.shape[2]
    cap = xrecv.shape[3]
    group = n // EXPERTS
    mid = n // 2
    sided = EXPERTS // 2
    gated = [t < ticks - 1 for t in range(ticks)]
    early = max(chunks - 1, 1)
    width = chunks * cols
    rows = n * cap
    side = e // mid
    base, far_base = side * mid, (1 - side) * mid
    own = e - base
    near_gate = jnp.where(side == 0, mid - 1, mid)
    far_gate = jnp.where(side == 0, mid, mid - 1)
    is_gate = e == near_gate
    not_gate = e != near_gate
    has_next = s < sections - 1
    has_prev = s > 0
    following = jnp.minimum(s + 1, sections - 1)
    previous = jnp.maximum(s - 1, 0)
    half = jnp.bfloat16
    single = jnp.float32

    def remote(source, target, send, recv, section, device):
        return pltpu.make_async_remote_copy(
            source, target, send, recv, device_id=(section, device), device_id_type=MESH
        )

    def near(body, own_too=False):
        def step(i, _):
            body(base + lax.rem(own + i, mid))
            return 0

        lax.fori_loop(0 if own_too else 1, mid, step, 0)

    def far(body):
        def step(i, _):
            body(far_base + i)
            return 0

        lax.fori_loop(0, mid, step, 0)

    def sent(source, send):
        remote(source, source, send, send, s, far_gate).wait_send()

    def landed(target, recv):
        remote(target, target, recv, recv, s, far_gate).wait_recv()

    def own_copy(t, c):
        source = acts if t == 0 else incoming.at[t - 1]
        return pltpu.make_async_copy(
            source.at[:, pl.ds(c * cols, cols)],
            xown.at[t, c],
            own_sem.at[c if t == 0 else chunks + t - 1],
        )

    def gate_copy(c):
        span = pl.ds(c * cols, cols)
        return (
            pltpu.make_async_copy(w_gate_hbm.at[span], w_gate.at[span], w_sem.at[0, c]),
            pltpu.make_async_copy(w_up_hbm.at[span], w_up.at[span], w_sem.at[1, c]),
        )

    down_copy = pltpu.make_async_copy(w_down_hbm, w_down, w_sem.at[2, 0])

    def table_copies(t):
        pairs = ((sel.at[t, 1 - side], sel_far), (pick.at[t, 1 - side], pick_far), (rate.at[t], rate_far))
        return [
            remote(
                source, target.at[t, own], table_send.at[i, t], table_recv.at[i, t], s, far_gate
            )
            for i, (source, target) in enumerate(pairs)
        ][: 3 if gated[t] else 1]

    def table_arrival(i, t):
        landed((sel_far, pick_far, rate_far)[i].at[t], table_recv.at[i, t])

    def sel_copy(t):
        return remote(
            sel.at[t + 1, side], sel_in.at[t], sel_send.at[t], sel_recv.at[t], previous, e
        )

    def raw_copy(t, c):
        return remote(
            made.at[t, c], xown.at[t + 1, c], raw_send.at[t], raw_recv.at[t], following, e
        )

    def bank(slot, c):
        return slot if slot > 0 or c < early else 2 * ticks - 1

    def far_copy(slot, t, c, section, source):
        return remote(
            source, xraw.at[t, c, own], far_send.at[bank(slot, c)], far_recv.at[t, c], section, far_gate
        )

    def x_copy(slot, t, c, section, d):
        return remote(
            xsend.at[slot, c, d // group - side * sided],
            xrecv.at[t, c, e],
            x_send.at[bank(slot, c)],
            x_recv.at[t, c],
            section,
            d,
        )

    def dispatched(slot, first, last, peers):
        span = pl.ds(first, last - first)
        sent(xown.at[0, span], far_send.at[bank(slot, first)])
        if peers:
            sent(xrecv.at[0, span, pl.ds(0, peers)], x_send.at[bank(slot, first)])

    def relay_copy(t, c, j, d):
        return remote(
            xrelay.at[t, c, j, d // group - side * sided],
            xrecv.at[t, c, far_base + j],
            relay_send.at[t, j],
            x_recv.at[t, c],
            s,
            d,
        )

    def p_copy(t, c, d):
        return remote(
            psend.at[t, c, d], precv.at[t, c, e], p_send.at[t], p_recv.at[t, c], s, d
        )

    def gate_send_copy(t, c):
        return remote(
            psend.at[t, c, pl.ds(far_base, mid)],
            pgate.at[t, c, own],
            gate_send.at[t],
            gate_recv.at[t, c],
            s,
            near_gate,
        )

    def f_copy(t, c, j):
        return remote(
            fsend.at[t, c, j], frecv.at[t, c], f_send.at[t], f_recv.at[t, c], s, far_base + j
        )

    def out_copy(t, c):
        return pltpu.make_async_copy(
            made.at[t, c], out.at[t, :, pl.ds(c * cols, cols)], out_sem.at[0]
        )

    small = [
        pltpu.make_async_copy(source, target, small_sem.at[i])
        for i, (source, target) in enumerate(
            ((routes_hbm, routes), (route_weight_hbm, route_weight), (gain_hbm, gain))
        )
    ]
    for copy in small:
        copy.start()
    for c in range(chunks):
        own_copy(0, c).start()

    barrier = pltpu.get_barrier_semaphore()

    def greet(d, _):
        @pl.when(d != e)
        def _():
            pl.semaphore_signal(barrier, inc=1, device_id=(s, d), device_id_type=MESH)

        return 0

    lax.fori_loop(0, n, greet, 0)
    for there, section in ((has_next, following), (has_prev, previous)):

        @pl.when(there)
        def _():
            pl.semaphore_signal(barrier, inc=1, device_id=(section, e), device_id_type=MESH)

    for c in range(chunks):
        for copy in gate_copy(c):
            copy.start()
    down_copy.start()

    @pl.when(jnp.logical_not(has_prev))
    def _():
        for t in range(1, ticks):
            for c in range(chunks):
                own_copy(t, c).start()

    for copy in small:
        copy.wait()

    def iota(shape, axis):
        return lax.broadcasted_iota(jnp.int32, shape, axis)

    before = (iota((tokens, tokens), 0) < iota((tokens, tokens), 1)).astype(half)
    diagonal = iota((tokens, tokens), 0) == iota((tokens, tokens), 1)
    place = iota((cap, tokens), 0).astype(single)
    for t in range(ticks):
        chosen = routes[t, 0]
        hot = sum(
            (iota((EXPERTS, tokens), 0) == chosen[k : k + 1]).astype(single) for k in range(top)
        )
        rank = jnp.dot(hot.astype(half), before, preferred_element_type=single)
        blocks = [
            [
                (place == jnp.where(chosen[k : k + 1] == x, rank[x : x + 1], -1.0)).astype(single)
                for x in range(EXPERTS)
            ]
            for k in range(top)
        ]
        for h in range(2):
            experts = range(h * sided, (h + 1) * sided)
            sel[t, h] = sum(
                jnp.concatenate([blocks[k][x] for x in experts], axis=0) for k in range(top)
            ).astype(half)
            for k in range(top):
                spread = jnp.concatenate(
                    [blocks[k][x] for x in experts for _ in range(group)], axis=0
                )
                pick[t, h, k * tokens : (k + 1) * tokens, :] = lax.dot_general(
                    diagonal.astype(half),
                    spread.astype(half),
                    (((1,), (1,)), ((), ())),
                    preferred_element_type=single,
                ).astype(half)
        rate[t] = jnp.zeros_like(rate[t])
        rate[t, 0:top, 0:tokens] = route_weight[t, 0]

    pl.semaphore_wait(
        barrier, n - 1 + jnp.where(has_next, 1, 0) + jnp.where(has_prev, 1, 0)
    )

    def pack(target, table, value):
        packed = jnp.dot(table, value, preferred_element_type=single)
        for x in range(sided):
            target[x] = packed[x * cap : (x + 1) * cap].astype(half)

    def landed_own(t):
        pltpu.make_async_copy(xown.at[t], xown.at[t], own_sem.at[chunks + t - 1]).wait()

    def dispatch_far(t, c):
        far_copy(t, t, c, s, xown.at[t, c]).start()

    def dispatch_near(t, c):
        pack(xsend.at[t, c], sel[t, side], xown[t, c])
        near(lambda d: x_copy(t, t, c, s, d).start())
        xrecv[t, c, e] = xsend[t, c, e // group - side * sided]

    def dispatch(t, c):
        own_copy(t, c).wait()
        dispatch_far(t, c)
        dispatch_near(t, c)

    paired = sections % 2 == 0
    leads = lax.rem(s, 2) == 0
    held = leads if paired else s < 0
    table_copies(0)[0].start()
    if paired:

        @pl.when(jnp.logical_not(leads))
        def _():
            pl.semaphore_wait(turn, 1)

    for c in range(chunks):
        dispatch(0, c)
    for t in range(ticks):
        for copy in table_copies(t)[1 if t == 0 else 0 :]:
            copy.start()

    @pl.when(has_prev)
    def _():
        for t in range(ticks - 1):
            sel_copy(t).start()

    dispatched(0, 0, early, mid - 1)
    if paired:

        @pl.when(leads)
        def _():
            pl.semaphore_signal(turn, inc=1, device_id=(following, e), device_id_type=MESH)

    def relay(t, c):
        if c == 0:
            table_arrival(0, t)
        landed(xraw.at[t, c], far_recv.at[t, c])
        for j in range(mid):
            pack(xrelay.at[t, c, j], sel_far[t, j], xraw[t, c, j])
            near(lambda d: relay_copy(t, c, j, d).start())
            xrecv[t, c, far_base + j] = xrelay[t, c, j, e // group - side * sided]

    def combine(t, c):
        if c == 0:
            table_arrival(1, t)
            table_arrival(2, t)
        if mid > 1:
            landed(pgate.at[t, c, pl.ds(0, mid - 1)], gate_recv.at[t, c])
        for j in range(mid):
            value = jnp.concatenate(
                [pgate[t, c, d, j].astype(single) for d in range(mid)], axis=0
            ).astype(half)
            back = jnp.dot(pick_far[t, j], value, preferred_element_type=single)
            total = None
            for k in range(top):
                part = back[k * tokens : (k + 1) * tokens] * column(rate_far[t, j], k)
                total = part if total is None else total + part
            fsend[t, c, j] = total.astype(half)
            f_copy(t, c, j).start()

    def forward(t, c):
        far_copy(ticks + t, t + 1, c, following, made.at[t, c]).start()
        pack(xsend.at[ticks + t, c], sel_in[t], made[t, c])
        near(lambda d: x_copy(ticks + t, t + 1, c, following, d).start(), True)
        raw_copy(t, c).start()

    def column(table, k):
        return jnp.sum(
            jnp.where(diagonal, table[k : k + 1, 0:tokens], 0.0), axis=1, keepdims=True
        )

    for t in range(ticks):
        gate_val = up_val = None
        squares = jnp.zeros((rows, 1), single)
        for c in range(chunks):

            @pl.when(is_gate if t == 0 else jnp.logical_and(is_gate, has_prev))
            def _():
                relay(t, c)

            for packed, there in ((0, is_gate), (mid, not_gate)):
                if t == 0:
                    cases = ((mid - 1, there),)
                else:
                    cases = (
                        (mid, jnp.logical_and(there, has_prev)),
                        (mid - 1, jnp.logical_and(there, jnp.logical_not(has_prev))),
                    )
                for number, case in cases:
                    if packed + number:

                        @pl.when(case)
                        def _():
                            landed(xrecv.at[t, c, pl.ds(0, packed + number)], x_recv.at[t, c])

            if t == 0:
                for copy in gate_copy(c):
                    copy.wait()
            span = pl.ds(c * cols, cols)
            value = jnp.concatenate([xrecv[t, c, d].astype(single) for d in range(n)], axis=0)
            squares = squares + jnp.sum(value * value, axis=1, keepdims=True)
            normed = (value * gain[:, span]).astype(half)
            gate_part = jnp.dot(normed, w_gate[span, :], preferred_element_type=single)
            up_part = jnp.dot(normed, w_up[span, :], preferred_element_type=single)
            gate_val = gate_part if gate_val is None else gate_val + gate_part
            up_val = up_part if up_val is None else up_val + up_part
        scale = lax.rsqrt(squares * (1.0 / width) + 1e-06)
        hidden = (jax.nn.silu(gate_val * scale) * (up_val * scale)).astype(half)
        if t == 0:
            down_copy.wait()

        for c in range(chunks):
            span = pl.ds(c * cols, cols)
            value = jnp.dot(hidden, w_down[:, span], preferred_element_type=single)
            for d in range(n):
                psend[t, c, d] = value[d * cap : (d + 1) * cap].astype(half)
            if gated[t]:

                @pl.when(not_gate)
                def _():
                    gate_send_copy(t, c).start()

                @pl.when(is_gate)
                def _():
                    pgate[t, c, own] = psend[t, c, pl.ds(far_base, mid)]

            else:
                far(lambda d: p_copy(t, c, d).start())
            near(lambda d: p_copy(t, c, d).start())
            precv[t, c, e] = psend[t, c, e]

        if t < ticks - 1:

            @pl.when(jnp.logical_not(has_prev))
            def _():
                landed_own(t + 1)
                for c in range(chunks):
                    dispatch_far(t + 1, c)

        if gated[t]:

            @pl.when(is_gate)
            def _():
                for c in range(chunks):
                    combine(t, c)

        if gated[t]:

            @pl.when(not_gate)
            def _():
                sent(psend.at[t, :, pl.ds(0, mid)], gate_send.at[t])

            peers = mid - 1
        else:
            peers = n - 1
        if peers:
            sent(psend.at[t, :, pl.ds(0, peers)], p_send.at[t])

        if t < ticks - 1:
            if paired:

                @pl.when(jnp.logical_not(leads))
                def _():
                    pl.semaphore_signal(turn, inc=1, device_id=(previous, e), device_id_type=MESH)

            @pl.when(has_next)
            def _():
                landed(sel_in.at[t], sel_recv.at[t])

        if t > 0:

            @pl.when(has_prev)
            def _():
                landed(xown.at[t], raw_recv.at[t - 1])

        weights = [column(rate[t], k) for k in range(top)]
        for c in range(chunks):
            layer = xown[t, c].astype(single)
            if gated[t]:
                landed(frecv.at[t, c], f_recv.at[t, c])
                layer = layer + frecv[t, c].astype(single)
                sources, table = [base + j for j in range(mid)], pick[t, side]
            else:
                sources = list(range(n))
                table = jnp.concatenate([pick[t, 0], pick[t, 1]], axis=1)
            if peers:
                landed(precv.at[t, c, pl.ds(0, peers)], p_recv.at[t, c])
            value = jnp.concatenate(
                [precv[t, c, d].astype(single) for d in sources], axis=0
            ).astype(half)
            back = jnp.dot(table, value, preferred_element_type=single)
            for k in range(top):
                layer = layer + back[k * tokens : (k + 1) * tokens] * weights[k]
            layer = layer.astype(half)
            made[t, c] = layer
            out_copy(t, c).start()
            if t < ticks - 1:

                @pl.when(jnp.logical_and(has_next, jnp.logical_not(held)))
                def _():
                    forward(t, c)

        if t < ticks - 1:

            @pl.when(jnp.logical_and(is_gate, jnp.logical_not(has_prev)))
            def _():
                for c in range(chunks):
                    relay(t + 1, c)

            @pl.when(jnp.logical_not(has_prev))
            def _():
                for c in range(chunks):
                    dispatch_near(t + 1, c)

            @pl.when(held)
            def _():
                pl.semaphore_wait(turn, 1)

            @pl.when(held)
            def _():
                for c in range(chunks):
                    forward(t, c)

    dispatched(0, early, chunks, mid - 1)
    for t in range(ticks):
        for copy in table_copies(t):
            copy.wait_send()

        @pl.when(is_gate)
        def _():
            if mid > 1:
                for j in range(mid):
                    sent(xrecv.at[t, :, pl.ds(0, mid - 1)], relay_send.at[t, j])
            if gated[t]:
                sent(fsend.at[t], f_send.at[t])

        if t > 0:

            @pl.when(jnp.logical_not(has_prev))
            def _():
                dispatched(t, 0, chunks, mid - 1)

        if t < ticks - 1:

            @pl.when(has_next)
            def _():
                dispatched(ticks + t, 0, chunks, mid)
                sent(made.at[t], raw_send.at[t])

    pltpu.make_async_copy(made, made, out_sem.at[0]).wait()

    @pl.when(has_prev)
    def _():
        for t in range(ticks - 1):
            sel_copy(t).wait_send()


def solution(mesh):
    n = mesh.shape["expert"]
    sections = mesh.shape["section"]

    def shards(acts, incoming, routes, route_weight, norm_gain, w_gate, w_up, w_down):
        ticks, _, tokens, top = routes.shape
        width, hidden = w_gate.shape[1:]
        chunks = 5 if width % (5 * 128) == 0 else 4
        cols = width // chunks
        cap = min(CAP, tokens)
        mid, sided, moves = n // 2, EXPERTS // 2, max(ticks - 1, 1)
        half, single = jnp.bfloat16, jnp.float32
        anywhere = pl.BlockSpec(memory_space=pl.ANY)
        dma = pltpu.SemaphoreType.DMA
        result = pl.pallas_call(
            functools.partial(kernel, n, sections),
            out_shape=jax.ShapeDtypeStruct((ticks, tokens, width), half),
            in_specs=[anywhere] * 8,
            out_specs=anywhere,
            scratch_shapes=[
                pltpu.VMEM((ticks, 1, top, tokens), routes.dtype),
                pltpu.VMEM((ticks, 1, top, tokens), single),
                pltpu.VMEM(norm_gain.shape, single),
                pltpu.VMEM((width, hidden), half),
                pltpu.VMEM((width, hidden), half),
                pltpu.VMEM((hidden, width), half),
                pltpu.VMEM((ticks, chunks, tokens, cols), half),
                pltpu.VMEM((ticks, chunks, tokens, cols), half),
                pltpu.VMEM((2 * ticks - 1, chunks, sided, cap, cols), half),
                pltpu.VMEM((ticks, chunks, mid, tokens, cols), half),
                pltpu.VMEM((ticks, chunks, mid, sided, cap, cols), half),
                pltpu.VMEM((ticks, chunks, n, cap, cols), half),
                pltpu.VMEM((ticks, chunks, n, cap, cols), half),
                pltpu.VMEM((ticks, chunks, n, cap, cols), half),
                pltpu.VMEM((moves, chunks, mid, mid, cap, cols), half),
                pltpu.VMEM((moves, chunks, mid, tokens, cols), half),
                pltpu.VMEM((moves, chunks, tokens, cols), half),
                pltpu.VMEM((ticks, 2, sided * cap, tokens), half),
                pltpu.VMEM((moves, sided * cap, tokens), half),
                pltpu.VMEM((ticks, mid, sided * cap, tokens), half),
                pltpu.VMEM((ticks, 2, top * tokens, mid * cap), half),
                pltpu.VMEM((ticks, mid, top * tokens, mid * cap), half),
                pltpu.VMEM((ticks, 8, 128), single),
                pltpu.VMEM((ticks, mid, 8, 128), single),
                dma((3,)),
                dma((3, chunks)),
                dma((1,)),
                dma((chunks + moves,)),
                dma((3, ticks)),
                dma((3, ticks)),
                dma((moves,)),
                dma((moves,)),
                dma((moves,)),
                dma((moves,)),
                dma((2 * ticks,)),
                dma((ticks, chunks)),
                dma((2 * ticks,)),
                dma((ticks, chunks)),
                dma((ticks, mid)),
                dma((ticks,)),
                dma((ticks, chunks)),
                dma((moves,)),
                dma((moves, chunks)),
                dma((moves,)),
                dma((moves, chunks)),
                pltpu.SemaphoreType.REGULAR,
            ],
            compiler_params=pltpu.CompilerParams(
                collective_id=0, has_side_effects=True, vmem_limit_bytes=34 << 20
            ),
        )(
            *(
                pltpu.with_memory_space_constraint(value, pltpu.HBM)
                for value in (
                    acts[0],
                    incoming,
                    jnp.swapaxes(routes, 2, 3),
                    jnp.swapaxes(route_weight, 2, 3),
                    norm_gain,
                    w_gate[0],
                    w_up[0],
                    w_down[0],
                )
            )
        )
        return result[:, None]

    return jax.shard_map(
        shards,
        mesh=mesh,
        in_specs=(
            P("section", "expert", None),
            P(None, "expert", None),
            P(None, "section", "expert", None),
            P(None, "section", "expert", None),
            P("section", None),
            P("section", None, "expert"),
            P("section", None, "expert"),
            P("section", "expert", None),
        ),
        out_specs=P(None, "section", "expert", None),
        check_vma=False,
    )
```
